32 devices in a mesh: dp: 8 (over z, y), tensor: 4 (over x, core).
Axes of the slice: x: 2, y: 2, z: 4, core: 2. Of those that a mesh axis runs over, the one named last changes fastest.
Arguments:
- hidden_in: bfloat16 [24576, 768], P('dp'), may hold values from -6 to 6
- box_coords: int32 [4, 24576], P(None, 'dp'), may hold values from 0 to 1000
- page_lengths: int32 [48], P('dp'), may hold values from 40 to 512, as said below
- query_weight: bfloat16 [768, 768], P(None, 'tensor'), may hold values from -0.21875 to 0.21875
- query_bias: float32 [768], P('tensor'), may hold values from -3 to 3
- key_weight: bfloat16 [768, 768], P(None, 'tensor'), may hold values from -0.21875 to 0.21875
- value_weight: bfloat16 [768, 768], P(None, 'tensor'), may hold values from -0.21875 to 0.21875
- value_bias: float32 [768], P('tensor'), may hold values from -3 to 3
- box_weight: bfloat16 [768, 1536], P(None, 'tensor'), may hold values from -0.21875 to 0.21875
- box_bias: float32 [1536], P('tensor'), may hold values from -3 to 3
- output_weight: bfloat16 [768, 768], P('tensor'), may hold values from -0.875 to 0.875
- output_bias: float32 [768], replicated, may hold values from -3 to 3
- first_gain: float32 [768], replicated, may hold values from 0.25 to 1.75
- first_shift: float32 [768], replicated, may hold values from -3 to 3
- up_weight: bfloat16 [768, 3072], P(None, 'tensor'), may hold values from -0.21875 to 0.21875
- up_bias: float32 [3072], P('tensor'), may hold values from -3 to 3
- down_weight: bfloat16 [3072, 768], P('tensor'), may hold values from -0.109375 to 0.109375
- down_bias: float32 [768], replicated, may hold values from -3 to 3
- second_gain: float32 [768], replicated, may hold values from 0.25 to 1.75
- second_shift: float32 [768], replicated, may hold values from -3 to 3
- output_grad: bfloat16 [24576, 768], P(('dp', 'tensor')), may hold values from -6 to 6
Outputs:
- layer_out: bfloat16 [24576, 768], P(('dp', 'tensor'))
- input_grad: float32 [24576, 768], P(('dp', 'tensor'))
- query_weight_grad: float32 [768, 768], P(None, 'tensor')
- query_bias_grad: float32 [768], P('tensor')
- key_weight_grad: float32 [768, 768], P(None, 'tensor')
- value_weight_grad: float32 [768, 768], P(None, 'tensor')
- value_bias_grad: float32 [768], P('tensor')
- box_weight_grad: float32 [768, 1536], P(None, 'tensor')
- box_bias_grad: float32 [1536], P('tensor')
- output_weight_grad: float32 [768, 768], P('tensor')
- output_bias_grad: float32 [768], P('tensor')
- first_gain_grad: float32 [768], P('tensor')
- first_shift_grad: float32 [768], P('tensor')
- up_weight_grad: float32 [768, 3072], P(None, 'tensor')
- up_bias_grad: float32 [3072], P('tensor')
- down_weight_grad: float32 [3072, 768], P('tensor')
- down_bias_grad: float32 [768], P('tensor')
- second_gain_grad: float32 [768], P('tensor')
- second_shift_grad: float32 [768], P('tensor')
The draws below stay inside these ranges and needn't reach their ends.
Inputs may be any that keep to these rules, and one draw needn't show every extreme that they name: Page p holds real tokens in its first page_lengths[p] slots; every draw has a page of 512 real tokens.
All inputs are finite; a program needn't handle non-finite values.
Results may differ from the reference program's by a relative error of at most 0.02.
Values may be sent and summed in bfloat16 or wider, within the bound.
A program may use at most 192 MiB of HBM per device.

```python
import math
import jax
import jax.numpy as jnp
from jax import lax

D = 768
HEADS = 12
HEAD = 64
FF = 3072
FREQ = 16
POS = 128
PAGE = 512
PAGES_DEV = 6
SHORT = 40
TOK_DEV = 3072
PAGES = 48
TOKENS = 24576
N_DP = 8
N_TENSOR = 4


def draw_page_lengths(key, part):
    first_key, second_key = jax.random.split(jax.random.fold_in(key, 7))
    drawn = jax.random.randint(first_key, (PAGES,), SHORT, PAGE + 1)
    chosen = jax.random.randint(second_key, (), 0, PAGES)
    return jnp.where(jnp.arange(PAGES, dtype=jnp.int32) == chosen, PAGE, drawn).astype(jnp.int32)


def place_ends(entries, rng, least, top_value):
    extent = entries.shape
    index_at = [jax.random.randint(jax.random.fold_in(rng, axis), (), 0, extent[axis]) for axis in range(len(extent))]
    entries = entries.at[tuple(index_at)].set(least)
    longest = extent.index(max(extent))
    index_at[longest] = (index_at[longest] + 1) % extent[longest]
    return entries.at[tuple(index_at)].set(top_value)


def block_scale(stream_key, dims, cuts, least, high):
    def one(dim, blocks):
        steps = jax.random.uniform(jax.random.fold_in(jax.random.fold_in(stream_key, 6), dim), (blocks,), jnp.float32, least / len(cuts), high / len(cuts))
        return jnp.repeat(jnp.exp(steps), dims[dim] // blocks).reshape((-1,) + (1,) * (len(dims) - dim - 1))

    loudness = one(*cuts[0])
    for cut in cuts[1:]:
        loudness = loudness * one(*cut)
    return loudness


def scatter_about(key, extent, spread, limit, cuts=(), held_as=jnp.bfloat16):
    values = jax.random.normal(key, extent, jnp.float32) * spread
    if len(cuts) > 0:
        values = block_scale(key, extent, cuts, -0.22, 0.18) * values
    return jnp.clip(values, min=-limit, max=limit).astype(held_as)


def setup_inputs(seed: int = 0) -> dict:
    keys = jax.random.split(jax.random.key(seed), 22)
    hidden_in = scatter_about(keys[0], (TOKENS, D), 1.0, 6.0, ((0, 8),))
    box_coords = place_ends(jax.random.randint(keys[1], (4, TOKENS), 0, 1001), jax.random.fold_in(keys[1], 1), 0, 1000).astype(jnp.int32)
    page_lengths = draw_page_lengths(jax.random.fold_in(keys[21], 71), 0)
    query_weight = scatter_about(keys[3], (D, D), D ** -0.5, 0.21875, ((1, 4),))
    query_bias = scatter_about(keys[4], (D,), 0.5, 3.0, ((0, 4),), jnp.float32)
    key_weight = scatter_about(keys[5], (D, D), D ** -0.5, 0.21875, ((1, 4),))
    value_weight = scatter_about(keys[6], (D, D), D ** -0.5, 0.21875, ((1, 4),))
    value_bias = scatter_about(keys[7], (D,), 0.5, 3.0, ((0, 4),), jnp.float32)
    box_weight = scatter_about(keys[8], (D, HEADS * POS), D ** -0.5, 0.21875, ((1, 4),))
    box_bias = scatter_about(keys[9], (HEADS * POS,), 0.5, 3.0, ((0, 4),), jnp.float32)
    output_weight = scatter_about(keys[10], (D, D), (D // 16) ** -0.5, 0.875, ((0, 4),))
    output_bias = scatter_about(keys[11], (D,), 0.5, 3.0, (), jnp.float32)
    first_gain = jnp.clip(1.0 + 0.15 * jax.random.normal(keys[12], (D,), jnp.float32), 0.25, 1.75)
    first_shift = scatter_about(keys[13], (D,), 0.5, 3.0, (), jnp.float32)
    up_weight = scatter_about(keys[14], (D, FF), D ** -0.5, 0.21875, ((1, 4),))
    up_bias = scatter_about(keys[15], (FF,), 0.5, 3.0, ((0, 4),), jnp.float32)
    down_weight = scatter_about(keys[16], (FF, D), FF ** -0.5, 0.109375, ((0, 4),))
    down_bias = scatter_about(keys[17], (D,), 0.5, 3.0, (), jnp.float32)
    second_gain = jnp.clip(1.0 + 0.15 * jax.random.normal(keys[18], (D,), jnp.float32), 0.25, 1.75)
    second_shift = scatter_about(keys[19], (D,), 0.5, 3.0, (), jnp.float32)
    output_grad = scatter_about(keys[20], (TOKENS, D), 1.0, 6.0, ((0, 32),))
    return {"hidden_in": hidden_in, "box_coords": box_coords, "page_lengths": page_lengths, "query_weight": query_weight, "query_bias": query_bias, "key_weight": key_weight, "value_weight": value_weight, "value_bias": value_bias, "box_weight": box_weight, "box_bias": box_bias, "output_weight": output_weight, "output_bias": output_bias, "first_gain": first_gain, "first_shift": first_shift, "up_weight": up_weight, "up_bias": up_bias, "down_weight": down_weight, "down_bias": down_bias, "second_gain": second_gain, "second_shift": second_shift, "output_grad": output_grad}


@jax.custom_vjp
def low(v):
    return lax.optimization_barrier(v.astype(jnp.bfloat16)).astype(jnp.float32)

@jax.custom_vjp
def low_back(v):
    return v

def low_keep(v):
    return (low(v), None)

def low_pass(kept, grad):
    return (grad,)

def back_keep(v):
    return (v, None)

def back_low(kept, grad):
    return (low(grad),)
low.defvjp(low_keep, low_pass)
low_back.defvjp(back_keep, back_low)
EPS = 1e-05
HIGHEST = lax.Precision.HIGHEST

def features(box_coords):
    rates = jnp.power(1000.0, -jnp.arange(FREQ, dtype=jnp.float32) / FREQ)
    angles = box_coords.astype(jnp.float32)[:, :, None] * rates[None, None, :]
    angles = jnp.transpose(angles, (1, 0, 2)).reshape(box_coords.shape[1], 4 * FREQ)
    return jnp.concatenate([jnp.cos(angles), jnp.sin(angles)], axis=1)

def mix_position(box_coeff, geometry):
    middle = POS // 2
    first_half = box_coeff[..., :middle]
    second_half = box_coeff[..., middle:]
    cosine = geometry[:, None, :middle]
    sine_part = geometry[:, None, middle:]
    return jnp.concatenate([first_half * cosine + second_half * sine_part, first_half * sine_part - second_half * cosine], axis=-1)

def page_attend(page_block):
    query_states, key_states, value_states, box_coeff, geometry, page_length = page_block
    box_query = low(mix_position(box_coeff, geometry))
    raw_scores = jnp.einsum('qhd,khd->hqk', query_states, key_states, precision=HIGHEST) + jnp.einsum('qhp,kp->hqk', box_query, geometry, precision=HIGHEST)
    scores = low_back(raw_scores * (1.0 / math.sqrt(HEAD)))
    is_valid = jnp.arange(PAGE, dtype=jnp.int32) < page_length
    scores = jnp.where(is_valid[None, None, :], scores, -1000000000.0)
    maxima = lax.optimization_barrier(jnp.max(scores, axis=-1, keepdims=True))
    exponent = jnp.exp(scores - maxima)
    weights = low(exponent / lax.optimization_barrier(jnp.sum(exponent, axis=-1, keepdims=True)))
    context = jnp.einsum('hqk,khd->qhd', weights, value_states, precision=HIGHEST)
    return context.reshape(PAGE, HEADS * HEAD)

def normalize(total, gain, shift):
    row_mean = lax.optimization_barrier(jnp.mean(total, axis=-1, keepdims=True))
    centred = total - row_mean
    return centred * lax.rsqrt(lax.optimization_barrier(jnp.mean(centred * centred, axis=-1, keepdims=True)) + EPS) * gain + shift

def group_sum(left, right):
    tokens_here = left.shape[0]
    inner_width = left.shape[1] // N_TENSOR
    pieces = jnp.einsum('ngk,gkd->gnd', left.reshape(tokens_here, N_TENSOR, inner_width), right.reshape(N_TENSOR, inner_width, right.shape[1]), precision=HIGHEST)
    return low_back(lax.optimization_barrier(jnp.sum(low(pieces), axis=0)))

def layer(hidden, query_weight, query_bias, key_weight, value_weight, value_bias, box_weight, box_bias, output_weight, output_bias, first_gain, first_shift, up_weight, up_bias, down_weight, down_bias, second_gain, second_shift, geometry, page_lengths):
    tokens_here = hidden.shape[0]
    page_count = tokens_here // PAGE
    query_states = low_back(low(jnp.dot(hidden, query_weight, precision=HIGHEST) + query_bias))
    key_states = low_back(low(jnp.dot(hidden, key_weight, precision=HIGHEST)))
    value_states = low_back(low(jnp.dot(hidden, value_weight, precision=HIGHEST) + value_bias))
    box_coeff = low_back(jnp.dot(hidden, box_weight, precision=HIGHEST) + box_bias)
    page_blocks = (query_states.reshape(page_count, PAGE, HEADS, HEAD), key_states.reshape(page_count, PAGE, HEADS, HEAD), value_states.reshape(page_count, PAGE, HEADS, HEAD), box_coeff.reshape(page_count, PAGE, HEADS, POS), geometry.reshape(page_count, PAGE, POS), page_lengths)
    context = lax.map(jax.checkpoint(page_attend), page_blocks).reshape(tokens_here, D)
    context = low_back(low(context))
    first = normalize(group_sum(context, output_weight) + output_bias + hidden, first_gain, first_shift)
    pre_active = low_back(jnp.dot(low(first), up_weight, precision=HIGHEST) + up_bias)
    activated = low(jax.nn.gelu(pre_active, approximate=False))
    return normalize(group_sum(activated, down_weight) + down_bias + first, second_gain, second_shift)

def reference(hidden_in, box_coords, page_lengths, query_weight, query_bias, key_weight, value_weight, value_bias, box_weight, box_bias, output_weight, output_bias, first_gain, first_shift, up_weight, up_bias, down_weight, down_bias, second_gain, second_shift, output_grad):
    weights_in = tuple((tensor_in.astype(jnp.float32) for tensor_in in (query_weight, query_bias, key_weight, value_weight, value_bias, box_weight, box_bias, output_weight, output_bias, first_gain, first_shift, up_weight, up_bias, down_weight, down_bias, second_gain, second_shift)))
    geometry = low(features(box_coords))
    blocks = (hidden_in.astype(jnp.float32).reshape(N_DP, TOK_DEV, D), geometry.reshape(N_DP, TOK_DEV, POS), page_lengths.reshape(N_DP, PAGES_DEV), output_grad.astype(jnp.float32).reshape(N_DP, TOK_DEV, D))

    def group_step(running, group_block):
        hidden, geo_part, length_part, cotangent = group_block

        def forward(*arguments):
            return layer(*arguments, geo_part, length_part)
        layer_value, pullback = jax.vjp(forward, hidden, *weights_in)
        gradients = pullback(cotangent)
        running = tuple((total + fresh for total, fresh in zip(running, gradients[1:])))
        return (running, (layer_value, gradients[0]))
    running, (layer_value, input_grad) = lax.scan(group_step, tuple((jnp.zeros_like(tensor_in) for tensor_in in weights_in)), blocks)
    return (layer_value.reshape(TOKENS, D).astype(jnp.bfloat16), input_grad.reshape(TOKENS, D), running[0], running[1], running[2], running[3], running[4], running[5], running[6], running[7], running[8], running[9], running[10], running[11], running[12], running[13], running[14], running[15], running[16])
```

```python
import math
from functools import partial
import jax, jax.numpy as jnp
from jax import lax
from jax.experimental import pallas as pl
from jax.experimental.pallas import tpu as pltpu
HEAD=64; POS=128; PAGE=512
F32=jnp.float32; BF=jnp.bfloat16
LOG2E=1.4426950408889634

def mm(a,b): return jnp.dot(a,b,preferred_element_type=F32)
def mm_nt(a,b): return lax.dot_general(a,b,(((1,),(1,)),((),())),preferred_element_type=F32)
def mm_tn(a,b): return lax.dot_general(a,b,(((0,),(0,)),((),())),preferred_element_type=F32)

def mixing(geo):
    half=POS//2
    c=geo[:,:half]; s=geo[:,half:]
    return jnp.concatenate([c,-c],axis=1), jnp.concatenate([s,s],axis=1)

def mix(coeff, cos_sign, sin_twice):
    return coeff*cos_sign + pltpu.roll(coeff, POS//2, 1)*sin_twice

def attend_forward(base_ref, len_ref, h_ref, geo_ref, wq_ref, wk_ref, wv_ref, wb_ref, qb_ref, vb_ref, bb_ref, ctx_ref, q_ref, k_ref, v_ref, p_ref, cat_q, cat_k, *, rows):
    heads=q_ref.shape[1]//HEAD
    length=len_ref[base_ref[0]+pl.program_id(0)]
    h=h_ref[...]
    geo=geo_ref[...]
    q_ref[...]=(mm(h,wq_ref[...])+qb_ref[...]).astype(BF)
    k_ref[...]=mm(h,wk_ref[...]).astype(BF)
    v_ref[...]=(mm(h,wv_ref[...])+vb_ref[...]).astype(BF)
    cs,ss=mixing(geo.astype(F32))
    for head in range(heads):
        coeff=mm(h,wb_ref[:,head*POS:(head+1)*POS])+bb_ref[:,head*POS:(head+1)*POS]
        cat_q[head,:,:POS]=mix(coeff,cs,ss).astype(BF)
        cat_q[head,:,POS:]=q_ref[:,head*HEAD:(head+1)*HEAD]
        cat_k[head,:,:POS]=geo
        cat_k[head,:,POS:]=k_ref[:,head*HEAD:(head+1)*HEAD]
    valid=lax.broadcasted_iota(jnp.int32,(1,PAGE),1)<length
    scale=LOG2E/math.sqrt(HEAD)
    for head in range(heads):
        keys=cat_k[head]
        values=v_ref[:,head*HEAD:(head+1)*HEAD]
        for r in range(0,PAGE,rows):
            s=mm_nt(cat_q[head,r:r+rows,:],keys)
            s=jnp.where(valid,s,-1e30)
            top=jnp.max(s,axis=1,keepdims=True)
            e=jnp.exp2((s-top)*scale)
            total=jnp.sum(e,axis=1,keepdims=True)
            p=(e*(1.0/total)).astype(BF)
            p_ref[head,r:r+rows,:]=p
            ctx_ref[r:r+rows,head*HEAD:(head+1)*HEAD]=mm(p,values).astype(BF)

def run_forward(base, lengths, hidden, geo, wq, wk, wv, wb, qb, vb, bb, pages, rows=256):
    cols=wq.shape[1]; heads=cols//HEAD; d=hidden.shape[1]
    page_in=lambda w: pl.BlockSpec((PAGE,w),lambda i,b,l:(b[0]+i,0))
    page_out=lambda w: pl.BlockSpec((PAGE,w),lambda i,b,l:(i,0))
    whole=lambda a: pl.BlockSpec(a.shape,lambda i,b,l:(0,0),pipeline_mode=pl.Buffered(1))
    rows_out=pages*PAGE
    return pl.pallas_call(partial(attend_forward,rows=rows),
        out_shape=[jax.ShapeDtypeStruct((rows_out,cols),BF)]*4+[jax.ShapeDtypeStruct((pages,heads,PAGE,PAGE),BF)],
        grid_spec=pltpu.PrefetchScalarGridSpec(num_scalar_prefetch=2,grid=(pages,),
            in_specs=[page_in(d),page_in(POS)]+[whole(a) for a in (wq,wk,wv,wb,qb,vb,bb)],
            out_specs=[page_out(cols)]*4+[pl.BlockSpec((pl.Squeezed(),heads,PAGE,PAGE),lambda i,b,l:(i,0,0,0))],
            scratch_shapes=[pltpu.VMEM((heads,PAGE,POS+HEAD),BF)]*2),
        compiler_params=pltpu.CompilerParams(vmem_limit_bytes=60<<20),
        name="attend_forward",
    )(base,lengths,hidden,geo,wq,wk,wv,wb,qb,vb,bb)
EPS=1e-05

def normal(z):
    mean=jnp.mean(z,axis=1,keepdims=True)
    centred=z-mean
    inverse=lax.rsqrt(jnp.mean(centred*centred,axis=1,keepdims=True)+EPS)
    return centred*inverse, inverse

def normal_back(inner, scaled, inverse):
    return inverse*(inner-jnp.mean(inner,axis=1,keepdims=True)-scaled*jnp.mean(inner*scaled,axis=1,keepdims=True))

def columns(x): return jnp.sum(x,axis=0,keepdims=True)

def middle(t_ref, hid_any, og_any, ctx_any, w0, w1, w2, w3, w4, w5, w6, w7, w8, w9, w10, w11, ub_ref, vec_ref,
           out_any, ag_any, dctx_any, act_any, ug_any, fl_any, sl_any, al_any, vg_ref, ubg_ref,
           hid, og, ctx, wo, wu, wd, act, ug, fl, sl, al, lo, ag, first, scaled1, inv1, ffn, dctx, sem_in, sem_w, sem_out, *, tile):
    rows,d=hid.shape
    groups=wu.shape[0]
    weights=(w0,w1,w2,w3,w4,w5,w6,w7,w8,w9,w10,w11)
    head_loads=[pltpu.make_async_copy(hid_any.at[pl.ds(t_ref[0]*rows,rows)],hid,sem_in.at[0]),
           pltpu.make_async_copy(og_any,og,sem_in.at[1]),
           pltpu.make_async_copy(ctx_any,ctx,sem_in.at[2])]
    loads=[[pltpu.make_async_copy(weights[3*g+k],(wo,wu,wd)[k].at[g],sem_w.at[k,g]) for g in range(groups)] for k in range(3)]
    for c in head_loads: c.start()
    for k in range(3):
        for c in loads[k]: c.start()
    for c in head_loads: c.wait()
    for c in loads[0]: c.wait()
    ob,g1,s1,db,g2,s2=(vec_ref[i:i+1,:] for i in range(6))
    vg_ref[...]=jnp.zeros_like(vg_ref)
    ubg_ref[...]=jnp.zeros_like(ubg_ref)
    for c in loads[1]: c.wait()
    for c in loads[2]: c.wait()
    def step(i,_):
        r=pl.ds(pl.multiple_of(i*tile,tile),tile)
        attn=mm(ctx[0,r],wo[0])
        for g in range(1,groups): attn=attn+mm(ctx[g,r],wo[g])
        scaled,inverse=normal(attn+ob+hid[r].astype(F32))
        f=scaled*g1+s1
        first[...]=f
        scaled1[...]=scaled
        inv1[...]=inverse
        fl[r]=f.astype(BF)
        ffn[...]=jnp.zeros_like(ffn)
        def up(g,_):
            x=mm(fl[r],wu[g])+ub_ref[g]
            half=0.5+0.5*lax.erf(x*0.7071067811865476)
            a=(x*half).astype(BF)
            act[g,r]=a
            ug[g,r]=(half+x*jnp.exp(-0.5*x*x)*0.3989422804014327).astype(BF)
            ffn[...]+=mm(a,wd[g])
            return 0
        lax.fori_loop(0,groups,up,0)
        scaled,inverse=normal(ffn[...]+db+first[...])
        lo[r]=(scaled*g2+s2).astype(BF)
        o=og[r].astype(F32)
        second=normal_back(o*g2,scaled,inverse)
        vg_ref[3:4,:]+=columns(second)
        vg_ref[4:5,:]+=columns(o*scaled)
        vg_ref[5:6,:]+=columns(o)
        sl[r]=second.astype(BF)
        ffn[...]=second
        def down(g,_):
            u=(mm_nt(sl[r],wd[g])*ug[g,r].astype(F32)).astype(BF)
            ug[g,r]=u
            ubg_ref[g]+=columns(u.astype(F32))
            ffn[...]+=mm_nt(u,wu[g])
            return 0
        lax.fori_loop(0,groups,down,0)
        fg=ffn[...]
        scaled=scaled1[...]
        a=normal_back(fg*g1,scaled,inv1[...])
        vg_ref[0:1,:]+=columns(a)
        vg_ref[1:2,:]+=columns(fg*scaled)
        vg_ref[2:3,:]+=columns(fg)
        ag[r]=a
        alow=a.astype(BF)
        al[r]=alow
        for g in range(groups): dctx[g,r]=mm_nt(alow,wo[g]).astype(BF)
        return 0
    lax.fori_loop(0,rows//tile,step,0)
    stores=[pltpu.make_async_copy(a,b,sem_out.at[i]) for i,(a,b) in enumerate(((dctx,dctx_any),(act,act_any),(ug,ug_any),(fl,fl_any),(sl,sl_any),(al,al_any),(lo,out_any),(ag,ag_any)))]
    for c in stores: c.start()
    for c in stores: c.wait()

def run_middle(t, hidden, og, ctx, weights, ub, vec, tile=256):
    rows,d=og.shape; groups=4; q=weights[0].shape[0]; f=weights[1].shape[1]
    anyspec=pl.BlockSpec(memory_space=pl.ANY)
    vm=pl.BlockSpec(memory_space=pltpu.VMEM)
    S=jax.ShapeDtypeStruct
    return pl.pallas_call(partial(middle,tile=tile),
        out_shape=[S((rows,d),BF),S((rows,d),F32),S((groups,rows,q),BF),S((groups,rows,f),BF),S((groups,rows,f),BF),S((rows,d),BF),S((rows,d),BF),S((rows,d),BF),S((8,d),F32),S((groups,1,f),F32)],
        in_specs=[pl.BlockSpec(memory_space=pltpu.SMEM)]+[anyspec]*15+[vm,vm],
        out_specs=[anyspec]*8+[vm,vm],
        scratch_shapes=[pltpu.VMEM((rows,d),BF),pltpu.VMEM((rows,d),BF),pltpu.VMEM((groups,rows,q),BF),
            pltpu.VMEM((groups,q,d),BF),pltpu.VMEM((groups,d,f),BF),pltpu.VMEM((groups,f,d),BF),
            pltpu.VMEM((groups,rows,f),BF),pltpu.VMEM((groups,rows,f),BF),
            pltpu.VMEM((rows,d),BF),pltpu.VMEM((rows,d),BF),pltpu.VMEM((rows,d),BF),pltpu.VMEM((rows,d),BF),pltpu.VMEM((rows,d),F32),
            pltpu.VMEM((tile,d),F32),pltpu.VMEM((tile,d),F32),pltpu.VMEM((tile,1),F32),pltpu.VMEM((tile,d),F32),
            pltpu.VMEM((groups,rows,q),BF),
            pltpu.SemaphoreType.DMA((3,)),pltpu.SemaphoreType.DMA((3,groups)),pltpu.SemaphoreType.DMA((8,))],
        compiler_params=pltpu.CompilerParams(vmem_limit_bytes=62<<20),
        name="middle",
    )(t,hidden,og,ctx,*weights,ub,vec)

def weight_grads(ctx_ref,al_ref,fl_ref,ug_ref,act_ref,sl_ref,extra_ref,g_ref,*,step):
    q=ctx_ref.shape[1]; d=fl_ref.shape[1]; f=ug_ref.shape[1]
    g_ref[0:q]=mm_tn(ctx_ref[...],al_ref[...]).astype(BF)
    g_ref[q:q+d]=mm_tn(fl_ref[...],ug_ref[...]).astype(BF)
    g_ref[q+d:q+d+f]=mm_tn(act_ref[...],sl_ref[...]).astype(BF)
    g_ref[q+d+f:q+d+f+8]=extra_ref[...].astype(BF)
    g_ref[q+d+f+8:]=jnp.zeros((g_ref.shape[0]-(q+d+f+8),d),BF)

def run_weight_grads(ctx,al,fl,ug,act,sl,extra,padded):
    groups,rows,q=ctx.shape; d=fl.shape[1]; f=ug.shape[2]
    order=lambda i:(i%2)*2+i//2
    per=lambda w: pl.BlockSpec((pl.Squeezed(),rows,w),lambda i:(order(i),0,0))
    whole=pl.BlockSpec((rows,d),lambda i:(0,0),pipeline_mode=pl.Buffered(1))
    return pl.pallas_call(partial(weight_grads,step=256),
        out_shape=jax.ShapeDtypeStruct((groups,padded,d),BF),
        grid=(groups,),
        in_specs=[per(q),whole,whole,per(f),per(f),whole,pl.BlockSpec((pl.Squeezed(),8,d),lambda i:(order(i),0,0))],
        out_specs=pl.BlockSpec((pl.Squeezed(),padded,d),lambda i:(i,0,0)),
        compiler_params=pltpu.CompilerParams(vmem_limit_bytes=60<<20),
        name="weight_grads")(ctx,al,fl,ug,act,sl,extra)
def attend_backward(base_ref, h_ref, geo_ref, w_ref, q_ref, k_ref, v_ref, p_ref, dc_ref, *rest, has_start, last):
    if has_start: start_ref,bstart_ref,*rest=rest
    dx_ref,dw_ref,db_ref,total,btotal,mixed=rest
    i=pl.program_id(0)
    cols=q_ref.shape[1]; heads=cols//HEAD
    @pl.when(i==0)
    def _():
        if has_start:
            total[...]=start_ref[...]; btotal[...]=bstart_ref[...]
        else:
            total[...]=jnp.zeros_like(total); btotal[...]=jnp.zeros_like(btotal)
    geo=geo_ref[...]
    cs,ss=mixing(geo.astype(F32))
    factor=1.0/math.sqrt(HEAD)
    for head in range(heads):
        lanes=slice(head*HEAD,(head+1)*HEAD)
        p=p_ref[head]
        dc=dc_ref[:,lanes]
        mixed[:,2*cols+head*HEAD:2*cols+(head+1)*HEAD]=mm_tn(p,dc).astype(BF)
        dp=mm_nt(dc,v_ref[:,lanes])
        pf=p.astype(F32)
        delta=jnp.sum(pf*dp,axis=1,keepdims=True)
        ds=(pf*(dp-delta)).astype(BF)
        both=mm(ds,jnp.concatenate([geo,k_ref[:,lanes]],axis=1))*factor
        mixed[:,lanes]=both[:,POS:].astype(BF)
        mixed[:,3*cols+head*POS:3*cols+(head+1)*POS]=mix(both[:,:POS],cs,ss).astype(BF)
        mixed[:,cols+head*HEAD:cols+(head+1)*HEAD]=(mm_tn(ds,q_ref[:,lanes])*factor).astype(BF)
    total[...]+=mm_tn(h_ref[...],mixed[...])
    btotal[0:1,:]+=jnp.sum(mixed[...].astype(F32),axis=0,keepdims=True)
    dx_ref[...]=mm_nt(mixed[...],w_ref[...]).astype(BF)
    @pl.when(i==pl.num_programs(0)-1)
    def _():
        dw_ref[...]=total[...].astype(dw_ref.dtype); db_ref[...]=btotal[...]

def run_backward(base,hidden,geo,w,q,k,v,p,dc,start=None,last=False):
    pages,heads=p.shape[:2]; cols=q.shape[1]; d=hidden.shape[1]; wide=w.shape[1]
    page_in=lambda n: pl.BlockSpec((PAGE,n),lambda i,b:(b[0]+i,0))
    page=lambda n: pl.BlockSpec((PAGE,n),lambda i,b:(i,0))
    whole=lambda s: pl.BlockSpec(s,lambda i,b:(0,0),pipeline_mode=pl.Buffered(1))
    extra=[] if start is None else list(start)
    S=jax.ShapeDtypeStruct
    return pl.pallas_call(partial(attend_backward,has_start=start is not None,last=last),
        out_shape=[S((pages*PAGE,d),BF),S((d,wide),BF if last else F32),S((8,wide),F32)],
        grid_spec=pltpu.PrefetchScalarGridSpec(num_scalar_prefetch=1,grid=(pages,),
            in_specs=[page_in(d),page_in(POS),whole(w.shape),page(cols),page(cols),page(cols),pl.BlockSpec((pl.Squeezed(),heads,PAGE,PAGE),lambda i,b:(i,0,0,0)),page(cols)]+[whole(a.shape) for a in extra],
            out_specs=[page(d),pl.BlockSpec((d,wide),lambda i,b:(0,0)),pl.BlockSpec((8,wide),lambda i,b:(0,0))],
            scratch_shapes=[pltpu.VMEM((d,wide),F32),pltpu.VMEM((8,wide),F32),pltpu.VMEM((PAGE,wide),BF)]),
        compiler_params=pltpu.CompilerParams(vmem_limit_bytes=60<<20),
        name="attend_backward")(base,hidden,geo,w,q,k,v,p,dc,*extra)

FREQ=16

def features(box_coords):
    rates = jnp.power(1000.0, -jnp.arange(FREQ, dtype=jnp.float32) / FREQ)
    angles = box_coords.astype(jnp.float32)[:, :, None] * rates[None, None, :]
    angles = jnp.transpose(angles, (1, 0, 2)).reshape(box_coords.shape[1], 4 * FREQ)
    return jnp.concatenate([jnp.cos(angles), jnp.sin(angles)], axis=1)

from jax.sharding import PartitionSpec as P

def body(hidden_in, box_coords, page_lengths, query_weight, query_bias, key_weight, value_weight, value_bias,
         box_weight, box_bias, output_weight, output_bias, first_gain, first_shift, up_weight, up_bias,
         down_weight, down_bias, second_gain, second_shift, output_grad):
    ways=lax.axis_size("tensor")
    place=lax.axis_index("tensor")
    core=place%2; chip=place//2
    rows=hidden_in.shape[0]//ways
    pages=page_lengths.shape[0]//2
    def swap(x,by):
        return lax.ppermute(x,"tensor",[(i,i^by) for i in range(ways)])
    def part(x,which):
        return lax.dynamic_slice_in_dim(x,which*rows,rows,0)
    own=(output_weight,up_weight,down_weight)
    far=tuple(swap(x,2) for x in own)
    near=tuple(swap(x,1) for x in own)
    cross=tuple(swap(x,1) for x in far)
    up_rel=jnp.stack([up_bias]+[swap(up_bias,b) for b in (1,2,3)])[:,None,:]
    geo=features(box_coords).astype(BF)
    far_base=((1-chip)*pages).reshape(1).astype(jnp.int32)
    own_base=(chip*pages).reshape(1).astype(jnp.int32)
    proj=(query_weight,key_weight,value_weight,box_weight,query_bias[None],value_bias[None],box_bias[None])
    ctx_f,*saved_f=run_forward(far_base,page_lengths,hidden_in,geo,*proj,pages=pages,rows=PAGE)
    ctx_o,*saved_o=run_forward(own_base,page_lengths,hidden_in,geo,*proj,pages=pages,rows=PAGE)
    ctx=jnp.stack([part(ctx_o,core),swap(part(ctx_o,1-core),1),swap(part(ctx_f,core),2),swap(part(ctx_f,1-core),3)])
    vec=jnp.stack([output_bias,first_gain,first_shift,down_bias,second_gain,second_shift,output_bias,output_bias])
    here=place.reshape(1).astype(jnp.int32)
    layer_out,attn_grad,dctx,act,ug,fl,sl,al,vg,ubg=run_middle(here,hidden_in,output_grad,ctx,own+near+far+cross,up_rel,vec,tile=384)
    d0,d1,d2,d3=(dctx[i] for i in range(4))
    d1=swap(d1,1); d2=swap(d2,2); d3=swap(d3,3)
    order=lambda a,b: jnp.where(core==0,jnp.concatenate([a,b]),jnp.concatenate([b,a]))
    dc_o=order(d0,d1); dc_f=order(d2,d3)
    width=vg.shape[1]//ways
    small=jnp.stack([jnp.concatenate([ubg[g],lax.dynamic_slice_in_dim(vg[:6],(place^g)*width,width,1).reshape(-1,width*ways//2)[:,:].reshape(1,-1)],axis=1) for g in range(ways)])
    small=jnp.pad(small,((0,0),(0,0),(0,8*vg.shape[1]-small.shape[2]))).reshape(ways,8,vg.shape[1])
    size=sum(x.shape[0] for x in own); padded=-(-(size+8)//64)*64
    grads=run_weight_grads(ctx,al,fl,ug,act,sl,small,padded)
    add=lambda a,b: (a.astype(F32)+b.astype(F32)).astype(BF)
    grads=add(grads[:2],swap(grads[2:],1))
    grads=add(grads[0],swap(grads[1],2))
    grads=lax.psum(grads,"dp").astype(F32)
    wide=jnp.concatenate([query_weight,key_weight,value_weight,box_weight],axis=1)
    dx_f,*start=run_backward(far_base,hidden_in,geo,wide,*saved_f,dc_f)
    dx_o,dw,db=run_backward(own_base,hidden_in,geo,wide,*saved_o,dc_o,start=start,last=True)
    half=add(part(dx_f,core),swap(part(dx_f,1-core),1))
    near_half=part(dx_o,core).astype(F32)+swap(part(dx_o,1-core),1).astype(F32)
    input_grad=near_half+swap(half,2).astype(F32)+attn_grad
    dw=lax.psum(dw,"dp").astype(F32)
    db=lax.psum(db[0],"dp")
    h=query_weight.shape[1]
    o=output_weight.shape[0]; f=up_weight.shape[0]
    tail=grads[size:size+8].reshape(-1)
    ubias=tail[:up_bias.shape[0]]
    norms=tail[up_bias.shape[0]:up_bias.shape[0]+6*width].reshape(6,width)
    return (layer_out,input_grad,dw[:,:h],db[:h],dw[:,h:2*h],dw[:,2*h:3*h],db[2*h:3*h],dw[:,3*h:],db[3*h:],
            grads[:o],norms[0],norms[1],norms[2],grads[o:o+f],ubias,grads[o+f:size],norms[3],norms[4],norms[5])


def solution(mesh):
    rep=P()
    in_specs=(P("dp",None),P(None,"dp"),P("dp"),P(None,"tensor"),P("tensor"),P(None,"tensor"),P(None,"tensor"),P("tensor"),
        P(None,"tensor"),P("tensor"),P("tensor",None),rep,rep,rep,P(None,"tensor"),P("tensor"),P("tensor",None),rep,rep,rep,P(("dp","tensor"),None))
    out_specs=(P(("dp","tensor"),None),P(("dp","tensor"),None),P(None,"tensor"),P("tensor"),P(None,"tensor"),P(None,"tensor"),P("tensor"),
        P(None,"tensor"),P("tensor"),P("tensor",None),P("tensor"),P("tensor"),P("tensor"),P(None,"tensor"),P("tensor"),P("tensor",None),P("tensor"),P("tensor"),P("tensor"))
    return jax.shard_map(body,mesh=mesh,in_specs=in_specs,out_specs=out_specs,check_vma=False)
```

```python
import math
from functools import partial
import jax, jax.numpy as jnp
from jax import lax
from jax.experimental import pallas as pl
from jax.experimental.pallas import tpu as pltpu
from jax.sharding import PartitionSpec as P
HEAD=64; POS=128; PAGE=512
F32=jnp.float32; BF=jnp.bfloat16
LOG2E=1.4426950408889634

def mm(a,b): return jnp.dot(a,b,preferred_element_type=F32)
def mm_nt(a,b): return lax.dot_general(a,b,(((1,),(1,)),((),())),preferred_element_type=F32)
def mm_tn(a,b): return lax.dot_general(a,b,(((0,),(0,)),((),())),preferred_element_type=F32)

def mixing(geo):
    half=POS//2
    c=geo[:,:half]; s=geo[:,half:]
    return jnp.concatenate([c,-c],axis=1), jnp.concatenate([s,s],axis=1)

def mix(coeff, cos_sign, sin_twice):
    return coeff*cos_sign + pltpu.roll(coeff, POS//2, 1)*sin_twice

EPS=1e-05

def normal(z):
    mean=jnp.mean(z,axis=1,keepdims=True)
    centred=z-mean
    inverse=lax.rsqrt(jnp.mean(centred*centred,axis=1,keepdims=True)+EPS)
    return centred*inverse, inverse

def normal_back(inner, scaled, inverse):
    return inverse*(inner-jnp.mean(inner,axis=1,keepdims=True)-scaled*jnp.mean(inner*scaled,axis=1,keepdims=True))

def columns(x): return jnp.sum(x,axis=0,keepdims=True)

def middle(t_ref, hid_any, og_any, ctx_any, w0, w1, w2, w3, w4, w5, w6, w7, w8, w9, w10, w11, ub_ref, vec_ref,
           out_any, ag_any, dctx_any, act_any, ug_any, fl_any, sl_any, al_any, small_ref,
           hid, og, ctx, wo, wu, wd, act, ug, fl, sl, al, lo, ag, first, scaled1, inv1, ffn, dctx, vg_ref, sem_in, sem_w, sem_out, *, tile):
    rows,d=hid.shape
    groups=wu.shape[0]
    weights=(w0,w1,w2,w3,w4,w5,w6,w7,w8,w9,w10,w11)
    head_loads=[pltpu.make_async_copy(hid_any.at[pl.ds(t_ref[0]*rows,rows)],hid,sem_in.at[0]),
           pltpu.make_async_copy(og_any,og,sem_in.at[1]),
           pltpu.make_async_copy(ctx_any,ctx,sem_in.at[2])]
    loads=[[pltpu.make_async_copy(weights[3*g+k],(wo,wu,wd)[k].at[g],sem_w.at[k,g]) for g in range(groups)] for k in range(3)]
    for c in head_loads: c.start()
    for k in range(3):
        for c in loads[k]: c.start()
    for c in head_loads: c.wait()
    for c in loads[0]: c.wait()
    ob,g1,s1,db,g2,s2=(vec_ref[i:i+1,:] for i in range(6))
    vg_ref[...]=jnp.zeros_like(vg_ref)
    small_ref[...]=jnp.zeros_like(small_ref)
    for c in loads[1]: c.wait()
    for c in loads[2]: c.wait()
    def step(i,_):
        r=pl.ds(pl.multiple_of(i*tile,tile),tile)
        attn=mm(ctx[0,r],wo[0])
        for g in range(1,groups): attn=attn+mm(ctx[g,r],wo[g])
        scaled,inverse=normal(attn+ob+hid[r].astype(F32))
        f=scaled*g1+s1
        first[...]=f
        scaled1[...]=scaled
        inv1[...]=inverse
        fl[r]=f.astype(BF)
        ffn[...]=jnp.zeros_like(ffn)
        def up(g,_):
            x=mm(fl[r],wu[g])+ub_ref[g]
            half=0.5+0.5*lax.erf(x*0.7071067811865476)
            a=(x*half).astype(BF)
            act[g,r]=a
            ug[g,r]=(half+x*jnp.exp(-0.5*x*x)*0.3989422804014327).astype(BF)
            ffn[...]+=mm(a,wd[g])
            return 0
        lax.fori_loop(0,groups,up,0)
        scaled,inverse=normal(ffn[...]+db+first[...])
        lo[r]=(scaled*g2+s2).astype(BF)
        o=og[r].astype(F32)
        second=normal_back(o*g2,scaled,inverse)
        vg_ref[3:4,:]+=columns(second)
        vg_ref[4:5,:]+=columns(o*scaled)
        vg_ref[5:6,:]+=columns(o)
        sl[r]=second.astype(BF)
        ffn[...]=second
        def down(g,_):
            u=(mm_nt(sl[r],wd[g])*ug[g,r].astype(F32)).astype(BF)
            ug[g,r]=u
            small_ref[g,0:1,:]+=columns(u.astype(F32))
            ffn[...]+=mm_nt(u,wu[g])
            return 0
        lax.fori_loop(0,groups,down,0)
        fg=ffn[...]
        scaled=scaled1[...]
        a=normal_back(fg*g1,scaled,inv1[...])
        vg_ref[0:1,:]+=columns(a)
        vg_ref[1:2,:]+=columns(fg*scaled)
        vg_ref[2:3,:]+=columns(fg)
        ag[r]=a
        alow=a.astype(BF)
        al[r]=alow
        for g in range(groups): dctx[g,r]=mm_nt(alow,wo[g]).astype(BF)
        return 0
    lax.fori_loop(0,rows//tile,step,0)
    width=d//groups
    for a in range(groups):
        small_ref[a^t_ref[0],1:7,:width]=vg_ref[0:6,a*width:(a+1)*width]
    stores=[pltpu.make_async_copy(a,b,sem_out.at[i]) for i,(a,b) in enumerate(((dctx,dctx_any),(act,act_any),(ug,ug_any),(fl,fl_any),(sl,sl_any),(al,al_any),(lo,out_any),(ag,ag_any)))]
    for c in stores: c.start()
    for c in stores: c.wait()

def run_middle(t, hidden, og, ctx, weights, ub, vec, tile=256):
    rows,d=og.shape; groups=4; q=weights[0].shape[0]; f=weights[1].shape[1]
    anyspec=pl.BlockSpec(memory_space=pl.ANY)
    vm=pl.BlockSpec(memory_space=pltpu.VMEM)
    S=jax.ShapeDtypeStruct
    return pl.pallas_call(partial(middle,tile=tile),
        out_shape=[S((rows,d),BF),S((rows,d),F32),S((groups,rows,q),BF),S((groups,rows,f),BF),S((groups,rows,f),BF),S((rows,d),BF),S((rows,d),BF),S((rows,d),BF),S((groups,8,d),F32)],
        in_specs=[pl.BlockSpec(memory_space=pltpu.SMEM)]+[anyspec]*15+[vm,vm],
        out_specs=[anyspec]*8+[vm],
        scratch_shapes=[pltpu.VMEM((rows,d),BF),pltpu.VMEM((rows,d),BF),pltpu.VMEM((groups,rows,q),BF),
            pltpu.VMEM((groups,q,d),BF),pltpu.VMEM((groups,d,f),BF),pltpu.VMEM((groups,f,d),BF),
            pltpu.VMEM((groups,rows,f),BF),pltpu.VMEM((groups,rows,f),BF),
            pltpu.VMEM((rows,d),BF),pltpu.VMEM((rows,d),BF),pltpu.VMEM((rows,d),BF),pltpu.VMEM((rows,d),BF),pltpu.VMEM((rows,d),F32),
            pltpu.VMEM((tile,d),F32),pltpu.VMEM((tile,d),F32),pltpu.VMEM((tile,1),F32),pltpu.VMEM((tile,d),F32),
            pltpu.VMEM((groups,rows,q),BF),pltpu.VMEM((8,d),F32),
            pltpu.SemaphoreType.DMA((3,)),pltpu.SemaphoreType.DMA((3,groups)),pltpu.SemaphoreType.DMA((8,))],
        compiler_params=pltpu.CompilerParams(vmem_limit_bytes=62<<20),
        name="middle",
    )(t,hidden,og,ctx,*weights,ub,vec)


MESH=pl.DeviceIdType.MESH

def remote(src,dst,sent,got,device):
    return pltpu.make_async_remote_copy(src_ref=src,dst_ref=dst,send_sem=sent,recv_sem=got,device_id=device,device_id_type=MESH)

def seats():
    group=lax.axis_index("dp"); place=lax.axis_index("tensor")
    core=lax.rem(place,2); chip=place//2
    near=place+1-2*core
    far=place+2-4*chip
    cross=far+1-2*core
    return group,place,core,chip,near,far,cross

def greet(devices):
    barrier=pltpu.get_barrier_semaphore()
    for device in devices:
        pl.semaphore_signal(barrier,inc=1,device_id=device,device_id_type=MESH)
    pl.semaphore_wait(barrier,len(devices))

def page_of(i,pages):
    chip=lax.axis_index("tensor")//2
    return jnp.where(i<pages,(1-chip)*pages+i,chip*pages+i-pages)

PART=192

def forward_kernel(len_ref, h_ref, geo_ref, w_ref, qb_ref, vb_ref, bb_ref, wo_any, wu_any, wd_any, ub_any,
                   q_ref, k_ref, v_ref, p_ref, ctx_any, no_any, nu_any, nd_any, fo_any, fu_any, fd_any, co_any, cu_any, cd_any, ua_any,
                   cat_q, cat_k, cpage, x_s, x_r, y_s, y_r, n_s, n_r, c_s, c_r, u_s, u_r, t_s, t_r, *, pages):
    i=pl.program_id(0)
    heads=q_ref.shape[1]//HEAD; cols=q_ref.shape[1]
    group,place,core,chip,near,far,cross=seats()
    side=lax.rem(group,2)
    beside=group+1-2*side
    own=(wo_any,wu_any,wd_any); nears=(no_any,nu_any,nd_any); fars=(fo_any,fu_any,fd_any); crosses=(co_any,cu_any,cd_any)
    chunks=[]
    for a,w in enumerate(own):
        half=w.shape[0]//2; step=min(PART,half)
        chunks+=[(a,s,step) for s in range(0,half,step)]
    def rows(c,other):
        a,s,n=chunks[c]
        half=own[a].shape[0]//2
        return a,pl.ds(pl.multiple_of(half*(1-side if other else side)+s,16),n)
    def x_copy(c):
        a,r=rows(c,False)
        return remote(own[a].at[r],fars[a].at[r],x_s.at[c],x_r.at[c],(group,far))
    def y_copy(c):
        a,r=rows(c,False)
        return remote(fars[a].at[r],fars[a].at[r],y_s.at[c],y_r.at[c],(beside,place))
    def y_got(c):
        a,r=rows(c,True)
        return remote(fars[a].at[r],fars[a].at[r],y_s.at[c],y_r.at[c],(beside,place))
    def c_copy(c,other):
        a,r=rows(c,other)
        k=1 if other else 0
        return remote(fars[a].at[r],crosses[a].at[r],c_s.at[k,c],c_r.at[k,c],(group,near))
    n_copies=[remote(own[a],nears[a],n_s.at[a],n_r.at[a],(group,near)) for a in range(3)]
    u_copies=[remote(ub_any,ua_any.at[g],u_s.at[g-1],u_r.at[g-1],(group,d)) for g,d in ((1,near),(2,far),(3,cross))]
    u_local=pltpu.make_async_copy(ub_any,ua_any.at[0],u_s.at[3])
    @pl.when(i==0)
    def _():
        greet([(group,near),(group,far),(group,cross),(beside,place)])
        for c in range(len(chunks)): x_copy(c).start()
        for n in n_copies: n.start()
        for u in u_copies: u.start()
        u_local.start()
    length=len_ref[page_of(i,pages)]
    h=h_ref[...]
    geo=geo_ref[...]
    q_ref[...]=(mm(h,w_ref[:,:cols])+qb_ref[...]).astype(BF)
    k_ref[...]=mm(h,w_ref[:,cols:2*cols]).astype(BF)
    v_ref[...]=(mm(h,w_ref[:,2*cols:3*cols])+vb_ref[...]).astype(BF)
    cs,ss=mixing(geo.astype(F32))
    for head in range(heads):
        coeff=mm(h,w_ref[:,3*cols+head*POS:3*cols+(head+1)*POS])+bb_ref[:,head*POS:(head+1)*POS]
        cat_q[head,:,:POS]=mix(coeff,cs,ss).astype(BF)
        cat_q[head,:,POS:]=q_ref[:,head*HEAD:(head+1)*HEAD]
        cat_k[head,:,:POS]=geo
        cat_k[head,:,POS:]=k_ref[:,head*HEAD:(head+1)*HEAD]
    valid=lax.broadcasted_iota(jnp.int32,(1,PAGE),1)<length
    scale=LOG2E/math.sqrt(HEAD)
    half=PAGE//2
    for head in range(heads):
        s=mm_nt(cat_q[head],cat_k[head])
        s=jnp.where(valid,s,-1e30)
        top=jnp.max(s,axis=1,keepdims=True)
        e=jnp.exp2((s-top)*scale)
        total=jnp.sum(e,axis=1,keepdims=True)
        p=(e*(1.0/total)).astype(BF)
        p_ref[head]=p
        c=mm(p,v_ref[:,head*HEAD:(head+1)*HEAD]).astype(BF)
        for k in range(2): cpage[2*i+k,:,head*HEAD:(head+1)*HEAD]=c[k*half:(k+1)*half]
    def context_copy(k):
        piece=2*lax.rem(i,pages)+k
        oc=piece//pages
        slot=lax.rem(piece,pages)
        return piece,oc,slot
    for k in range(2):
        piece,oc,slot=context_copy(k)
        mine=oc==core
        @pl.when(i<pages)
        def _():
            g=jnp.where(mine,2,3)
            remote(cpage.at[2*i+k],ctx_any.at[g,slot],t_s.at[2*i+k],t_r.at[g,slot],(group,2*(1-chip)+oc)).start()
        @pl.when((i>=pages) & jnp.logical_not(mine))
        def _():
            remote(cpage.at[2*i+k],ctx_any.at[1,slot],t_s.at[2*i+k],t_r.at[1,slot],(group,near)).start()
        @pl.when((i>=pages) & mine)
        def _():
            pltpu.make_async_copy(cpage.at[2*i+k],ctx_any.at[0,slot],t_r.at[0,slot]).start()
    count=2*pages
    plan={0:[0],1:[1],3:[2],4:[3],5:[4]}
    left=[c for c in range(len(chunks)) if not any(c in v for v in plan.values())]
    for at,todo in plan.items():
        @pl.when(i==at)
        def _():
            for c in todo:
                x_copy(c).wait_recv()
                y_copy(c).start()
                c_copy(c,False).start()
    @pl.when(i==count-1)
    def _():
        for c in left:
            x_copy(c).wait_recv()
            y_copy(c).start()
            c_copy(c,False).start()
        for c in range(len(chunks)):
            y_got(c).wait_recv()
            c_copy(c,True).start()
        for n in n_copies: n.wait()
        for u in u_copies: u.wait()
        u_local.wait()
        for slot in range(pages):
            pltpu.make_async_copy(ctx_any.at[0,slot],ctx_any.at[0,slot],t_r.at[0,slot]).wait()
            for g in (1,2,3):
                pltpu.make_async_copy(ctx_any.at[g,slot],ctx_any.at[g,slot],t_r.at[g,slot]).wait()
        for j in range(2*count):
            if j<count:
                pltpu.make_async_copy(cpage.at[j],cpage.at[j],t_s.at[j]).wait()
            else:
                @pl.when((j-count)//pages!=core)
                def _():
                    pltpu.make_async_copy(cpage.at[j],cpage.at[j],t_s.at[j]).wait()
        for c in range(len(chunks)):
            x_copy(c).wait_send()
            y_copy(c).wait_send()
            c_copy(c,False).wait()
            c_copy(c,True).wait()

def run_forward(lengths, hidden, geo, w, qb, vb, bb, wo, wu, wd, ub):
    cols=qb.shape[1]; heads=cols//HEAD; d=hidden.shape[1]
    pages=lengths.shape[0]//2
    page_in=lambda n: pl.BlockSpec((PAGE,n),lambda i:(page_of(i,pages),0))
    page_out=lambda n: pl.BlockSpec((PAGE,n),lambda i:(i,0))
    whole=lambda a: pl.BlockSpec(a.shape,lambda i:(0,0),pipeline_mode=pl.Buffered(1))
    anyspec=pl.BlockSpec(memory_space=pl.ANY)
    S=jax.ShapeDtypeStruct
    half=PAGE//2
    own=(wo,wu,wd)
    n=sum((x.shape[0]//2)//min(PART,x.shape[0]//2) for x in own)
    D=pltpu.SemaphoreType.DMA
    return pl.pallas_call(partial(forward_kernel,pages=pages),
        out_shape=[S((2*pages*PAGE,cols),BF)]*3+[S((2*pages,heads,PAGE,PAGE),BF),S((4,pages,half,cols),BF)]+[S(x.shape,BF) for x in own]*3+[S((4,)+ub.shape,F32)],
        grid=(2*pages,),
        in_specs=[pl.BlockSpec(memory_space=pltpu.SMEM),page_in(d),page_in(POS)]+[whole(a) for a in (w,qb,vb,bb)]+[anyspec]*4,
        out_specs=[page_out(cols)]*3+[pl.BlockSpec((pl.Squeezed(),heads,PAGE,PAGE),lambda i:(i,0,0,0))]+[anyspec]*11,
        scratch_shapes=[pltpu.VMEM((heads,PAGE,POS+HEAD),BF)]*2+[pltpu.VMEM((4*pages,half,cols),BF),
            D((n,)),D((n,)),D((n,)),D((n,)),D((3,)),D((3,)),D((2,n)),D((2,n)),D((4,)),D((3,)),D((4*pages,)),D((4,pages))],
        compiler_params=pltpu.CompilerParams(vmem_limit_bytes=56<<20,collective_id=0,has_side_effects=True),
        name="forward",
    )(lengths,hidden,geo,w,qb,vb,bb,wo,wu,wd,ub)

BLOCK=256

def cube(x,pr): return x.reshape(x.shape[0]//pr,pr,x.shape[1])

class Reduce:
    def __init__(self,main,yrecv,zrecv,final,out,sems,group,place,m):
        self.main,self.yrecv,self.zrecv,self.final,self.out=main,yrecv,zrecv,final,out
        self.sems=sems; self.m=m; self.place=place
        self.side=lax.rem(group,2); self.z=group//2
        self.beside=group+1-2*self.side
    def half(self,j,s): return pl.ds((2*j+s)*self.m,self.m)
    def y_copy(self,j):
        return remote(self.main.at[self.half(j,1-self.side)],self.yrecv.at[j],self.sems.at[0,j],self.sems.at[1,j],(self.beside,self.place))
    def y_add(self,j):
        self.y_copy(j).wait_recv()
        def one(k,_):
            at=(2*j+self.side)*self.m+k
            self.main[at]=(self.main[at].astype(F32)+self.yrecv[j,k].astype(F32)).astype(BF)
            return 0
        lax.fori_loop(0,self.m,one,0)
        def send(k,_):
            z=lax.rem(self.z+k,self.m)
            remote(self.main.at[(2*j+self.side)*self.m+z],self.zrecv.at[j,self.m-k-1],self.sems.at[2,j],self.sems.at[3,j],(2*z+self.side,self.place)).start()
            return 0
        lax.fori_loop(1,self.m,send,0)
    def z_add(self,j):
        pltpu.make_async_copy(self.zrecv.at[j],self.zrecv.at[j],self.sems.at[3,j]).wait()
        def one(k,acc): return acc+self.zrecv[j,k].astype(F32)
        acc=lax.fori_loop(0,self.m-1,one,self.main[(2*j+self.side)*self.m+self.z].astype(F32))
        self.final[j]=acc.astype(BF)
        at=(2*j+self.side)*self.m+self.z
        pltpu.make_async_copy(self.final.at[j],self.out.at[at],self.sems.at[8,j]).start()
        def send(k,_):
            z=lax.rem(self.z+k,self.m)
            remote(self.final.at[j],self.out.at[at],self.sems.at[4,j],self.sems.at[5,j],(2*z+self.side,self.place)).start()
            return 0
        lax.fori_loop(1,self.m,send,0)
    def g_copy(self,j):
        here=self.half(j,self.side)
        return remote(self.out.at[here],self.out.at[here],self.sems.at[6,j],self.sems.at[7,j],(self.beside,self.place))
    def g_send(self,j):
        pltpu.make_async_copy(self.zrecv.at[j],self.zrecv.at[j],self.sems.at[5,j]).wait()
        pltpu.make_async_copy(self.final.at[j],self.final.at[j],self.sems.at[8,j]).wait()
        self.g_copy(j).start()
    def finish(self,j):
        self.g_copy(j).wait()
        self.y_copy(j).wait_send()
        pltpu.make_async_copy(self.zrecv.at[j],self.zrecv.at[j],self.sems.at[2,j]).wait()
        pltpu.make_async_copy(self.zrecv.at[j],self.zrecv.at[j],self.sems.at[4,j]).wait()

def backward_kernel(h_ref, geo_ref, w_ref, q_ref, k_ref, v_ref, p_ref, small_ref, dctx_any, act_any, ug_any, fl_any, sl_any, al_any, ctx_any, ag_any,
                    fin_any, afin_any, ig_any,
                    act, ug, fl, sl, ctx, cs, crecv, gx, xrecv, main, yrecv, zrecv, final,
                    amain, ayrecv, azrecv, afinal, dc, dcp, total, btotal, mixed, keep, give, drecv, dxrecv, ag,
                    l_sem, c_s, c_r, x_s, x_r, r_sem, a_sem, e_s, e_r, d_s, d_r, f_s, f_r, o_sem, *, pages, m, blocks, per):
    i=pl.program_id(0)
    count=2*pages
    group,place,core,chip,near,far,cross=seats()
    cols=q_ref.shape[1]; heads=cols//HEAD; d=h_ref.shape[1]
    pr=main.shape[1]; pb=BLOCK//pr
    f=act.shape[2]; qc=ctx.shape[2]
    chunks=blocks//per; achunks=amain.shape[0]//(2*m)
    ffn=Reduce(main,yrecv,zrecv,final,fin_any,r_sem,group,place,m)
    att=Reduce(amain,ayrecv,azrecv,afinal,afin_any,a_sem,group,place,m)
    loads=[pltpu.make_async_copy(a,b,l_sem.at[n]) for n,(a,b) in enumerate(((sl_any,sl),(act_any,act),(fl_any,fl),(ug_any,ug),(al_any,act.at[0]),(ctx_any,ctx)))]
    e_copies=[remote(dctx_any.at[g],dc.at[g],e_s.at[g-1],e_r.at[g-1],(group,t)) for g,t in ((2,far),(3,cross),(1,near))]
    e_local=pltpu.make_async_copy(dctx_any.at[0],dc.at[0],e_s.at[3])
    ag_loads=[pltpu.make_async_copy(ag_any.at[pl.ds(k*BLOCK,BLOCK)],ag.at[k],l_sem.at[6+k]) for k in range(pages)]
    def c_copy(b,slot): return remote(cs.at[slot],crecv.at[b],c_s.at[b],c_r.at[b],(group,near))
    def x_copy(b): return remote(gx.at[b],xrecv.at[b],x_s.at[b],x_r.at[b],(group,far))
    def span(b): return pl.ds(b*pb,pb)
    def put(b,g,value):
        value=cube(value.astype(BF),pr)
        if g==0: main[span(b)]=value
        elif g==2: gx[b]=value
        else: cs[lax.rem(b,2),g//2]=value
    def c_add(b):
        c_copy(b,lax.rem(b,2)).wait_recv()
        def one(k,_):
            at=b*pb+k
            main[at]=(main[at].astype(F32)+crecv[b,0,k].astype(F32)).astype(BF)
            gx[b,k]=(gx[b,k].astype(F32)+crecv[b,1,k].astype(F32)).astype(BF)
            return 0
        lax.fori_loop(0,pb,one,0)
        x_copy(b).start()
    def x_add(b):
        x_copy(b).wait_recv()
        def one(k,_):
            at=b*pb+k
            main[at]=(main[at].astype(F32)+xrecv[b,k].astype(F32)).astype(BF)
            return 0
        lax.fori_loop(0,pb,one,0)

    @pl.when(i==0)
    def _():
        peers=[(group,near),(group,far),(group,cross),(ffn.beside,place)]
        barrier=pltpu.get_barrier_semaphore()
        for device in peers:
            pl.semaphore_signal(barrier,inc=1,device_id=device,device_id_type=MESH)
        def call(k,_):
            z=lax.rem(ffn.z+k,m)
            pl.semaphore_signal(barrier,inc=1,device_id=(2*z+ffn.side,place),device_id_type=MESH)
            return 0
        lax.fori_loop(1,m,call,0)
        for n in (0,1,2,3,5): loads[n].start()
        for c in ag_loads: c.start()
        pl.semaphore_wait(barrier,len(peers)+m-1)
        for c in e_copies: c.start()
        e_local.start()
        def block(b,kind):
            slot=lax.rem(b,2)
            @pl.when(b>=2)
            def _(): c_copy(b-2,slot).wait_send()
            if kind=="down":
                r=pl.ds(pl.multiple_of(b*BLOCK,BLOCK),BLOCK)
                for g in range(4): put(b,g,mm_tn(act[g,:,r],sl[...]))
            elif kind=="up":
                r=pl.ds(pl.multiple_of((b-f//BLOCK)*BLOCK,BLOCK),BLOCK)
                for g in range(4): put(b,g,mm_tn(fl[:,r],ug[g]))
            elif kind=="out":
                for g in range(4):
                    top=mm_tn(ctx[g],act[0])
                    pad=jnp.concatenate([top,small_ref[g],jnp.zeros((BLOCK-qc-small_ref.shape[1],d),F32)],axis=0)
                    put(b,g,pad)
            else:
                for g in range(4): put(b,g,jnp.zeros((BLOCK,d),F32))
            c_copy(b,slot).start()
            @pl.when(b>=1)
            def _(): c_add(b-1)
        loads[0].wait(); loads[1].wait()
        lax.fori_loop(0,f//BLOCK,lambda b,_: (block(b,"down"),0)[1],0)
        loads[4].start()
        loads[2].wait(); loads[3].wait()
        lax.fori_loop(f//BLOCK,(f+d)//BLOCK,lambda b,_: (block(b,"up"),0)[1],0)
        loads[4].wait(); loads[5].wait()
        block((f+d)//BLOCK,"out")
        for b in range((f+d)//BLOCK+1,blocks): block(b,"zero")
        c_add(blocks-1)
        for b in (blocks-2,blocks-1): c_copy(b,b%2).wait_send()
        total[...]=jnp.zeros_like(total); btotal[...]=jnp.zeros_like(btotal)
        for c in e_copies: c.wait_recv()
        e_local.wait()

    half=PAGE//2
    for k in range(2):
        piece=2*lax.rem(i,pages)+k
        g=jnp.where(piece//pages==core,0,1)+jnp.where(i<pages,2,0)
        dcp[k*half:(k+1)*half,:]=dc[g,lax.rem(piece,pages)]
    geo=geo_ref[...]
    co,si=mixing(geo.astype(F32))
    factor=1.0/math.sqrt(HEAD)
    for head in range(heads):
        lanes=slice(head*HEAD,(head+1)*HEAD)
        p=p_ref[head]
        dcl=dcp[:,lanes]
        mixed[:,2*cols+head*HEAD:2*cols+(head+1)*HEAD]=mm_tn(p,dcl).astype(BF)
        dp=mm_nt(dcl,v_ref[:,lanes])
        pf=p.astype(F32)
        delta=jnp.sum(pf*dp,axis=1,keepdims=True)
        ds=(pf*(dp-delta)).astype(BF)
        both=mm(ds,jnp.concatenate([geo,k_ref[:,lanes]],axis=1))*factor
        mixed[:,lanes]=both[:,POS:].astype(BF)
        mixed[:,3*cols+head*POS:3*cols+(head+1)*POS]=mix(both[:,:POS],co,si).astype(BF)
        mixed[:,cols+head*HEAD:cols+(head+1)*HEAD]=(mm_tn(ds,q_ref[:,lanes])*factor).astype(BF)
    total[...]+=mm_tn(h_ref[...],mixed[...])
    btotal[0:1,:]+=jnp.sum(mixed[...].astype(F32),axis=0,keepdims=True)
    def d_copy(kind,slot): return remote(give.at[kind,slot],drecv.at[kind,slot],d_s.at[kind,slot],d_r.at[kind,slot],(group,near))
    def f_copy(slot): return remote(keep.at[0,slot],dxrecv.at[slot],f_s.at[slot],f_r.at[slot],(group,far))
    kind=jnp.where(i<pages,0,1)
    for k in range(2):
        piece=2*lax.rem(i,pages)+k
        slot=lax.rem(piece,pages)
        value=mm_nt(mixed[k*half:(k+1)*half,:],w_ref[...]).astype(BF)
        mine=piece//pages==core
        @pl.when(mine)
        def _(): keep[kind,slot]=value
        @pl.when(jnp.logical_not(mine))
        def _():
            give[kind,slot]=value
            d_copy(kind,slot).start()
    @pl.when(i==pages)
    def _():
        for slot in range(pages):
            d_copy(0,slot).wait_recv()
            keep[0,slot]=(keep[0,slot].astype(F32)+drecv[0,slot].astype(F32)).astype(BF)
            f_copy(slot).start()

    def advance(s):
        b=s
        @pl.when((b>=0)&(b<blocks))
        def _():
            x_add(b)
            @pl.when(b==(f+d)//BLOCK)
            def _():
                at=b*pb+qc//pr
                bias=btotal[0:1,:]
                row=jnp.concatenate([bias[:,:cols],bias[:,2*cols:]],axis=1)
                sub=qc%pr
                eight=jnp.where(lax.broadcasted_iota(jnp.int32,(16,d),0)==7,row,0.0)
                main[at,sub:sub+16,:]=(main[at,sub:sub+16,:].astype(F32)+eight).astype(BF)
            @pl.when(lax.rem(b+1,per)==0)
            def _(): ffn.y_copy(b//per).start()
        c=s-per
        ready=lambda c: (c>=0)&(c<blocks)&(lax.rem(c+1,per)==0)
        @pl.when(ready(s-1))
        def _(): ffn.y_add((s-1)//per)
        @pl.when(ready(s-2))
        def _(): ffn.z_add((s-2)//per)
        @pl.when(ready(s-3))
        def _(): ffn.g_send((s-3)//per)
    @pl.when((i>=1)&(i<count-1))
    def _(): advance(i-1)

    @pl.when(i==count-1)
    def _():
        rows=amain.shape[0]*pr
        for b in range(rows//BLOCK):
            if b*BLOCK<d: amain[span(b)]=cube(total[b*BLOCK:(b+1)*BLOCK,:].astype(BF),pr)
            else: amain[span(b)]=jnp.zeros((pb,pr,total.shape[1]),BF)
        for j in range(achunks): att.y_copy(j).start()
        advance(count-2)
        for j in range(achunks): att.y_add(j)
        advance(count-1)
        for j in range(achunks): att.z_add(j)
        advance(count)
        for j in range(achunks): att.g_send(j)
        lax.fori_loop(count+1,blocks+3,lambda s,_: (advance(s),0)[1],0)
        for slot in range(pages):
            d_copy(1,slot).wait_recv()
            f_copy(slot).wait_recv()
            ag_loads[slot].wait()
            ag[slot]=ag[slot]+keep[1,slot].astype(F32)+drecv[1,slot].astype(F32)+dxrecv[slot].astype(F32)
            pltpu.make_async_copy(ag.at[slot],ig_any.at[pl.ds(slot*BLOCK,BLOCK)],o_sem.at[slot]).start()
        for slot in range(pages):
            pltpu.make_async_copy(ag.at[slot],ig_any.at[pl.ds(slot*BLOCK,BLOCK)],o_sem.at[slot]).wait()
            f_copy(slot).wait_send()
            d_copy(0,slot).wait_send()
            d_copy(1,slot).wait_send()
        for j in range(achunks): att.finish(j)
        lax.fori_loop(0,chunks,lambda j,_: (ffn.finish(j),0)[1],0)
        lax.fori_loop(0,blocks,lambda b,_: (x_copy(b).wait_send(),0)[1],0)
        for c in e_copies: c.wait_send()

def run_backward(hidden,geo,w,q,k,v,p,small,dctx,act,ug,fl,sl,al,ctx,ag):
    count,heads=p.shape[:2]; pages=count//2; cols=q.shape[1]; d=hidden.shape[1]; wide=w.shape[1]
    f=act.shape[2]; rows=fl.shape[0]
    ways=lax.axis_size("dp"); m=ways//2
    chunk=max(BLOCK,16*ways); per=chunk//BLOCK; pr=chunk//ways; pb=BLOCK//pr
    blocks=-(-((f+d)//BLOCK+1)//per)*per
    ablocks=-(-(d//BLOCK)//per)*per
    chunks=blocks//per; achunks=ablocks//per
    page_in=lambda n: pl.BlockSpec((PAGE,n),lambda i:(page_of(i,pages),0))
    page=lambda n: pl.BlockSpec((PAGE,n),lambda i:(i,0))
    whole=lambda s: pl.BlockSpec(s,lambda i:(0,)*len(s),pipeline_mode=pl.Buffered(1))
    anyspec=pl.BlockSpec(memory_space=pl.ANY)
    S=jax.ShapeDtypeStruct; V=pltpu.VMEM; D=pltpu.SemaphoreType.DMA
    half=PAGE//2
    dctx=dctx.reshape(4,pages,half,cols)
    return pl.pallas_call(partial(backward_kernel,pages=pages,m=m,blocks=blocks,per=per),
        out_shape=[S((blocks*pb,pr,d),BF),S((ablocks*pb,pr,wide),BF),S((rows,d),F32)],
        grid=(count,),
        in_specs=[page_in(d),page_in(POS),whole(w.shape),page(cols),page(cols),page(cols),pl.BlockSpec((pl.Squeezed(),heads,PAGE,PAGE),lambda i:(i,0,0,0)),whole(small.shape)]+[anyspec]*8,
        out_specs=[anyspec]*3,
        scratch_shapes=[V(act.shape,BF),V(ug.shape,BF),V(fl.shape,BF),V(sl.shape,BF),V(ctx.shape,BF),
            V((2,2,pb,pr,d),BF),V((blocks,2,pb,pr,d),BF),V((blocks,pb,pr,d),BF),V((blocks,pb,pr,d),BF),V((blocks*pb,pr,d),BF),
            V((chunks,m,pr,d),BF),V((chunks,m-1,pr,d),BF),V((chunks,pr,d),BF),
            V((ablocks*pb,pr,wide),BF),V((achunks,m,pr,wide),BF),V((achunks,m-1,pr,wide),BF),V((achunks,pr,wide),BF),
            V((4,pages,half,cols),BF),V((PAGE,cols),BF),V((d,wide),F32),V((8,wide),F32),V((PAGE,wide),BF),
            V((2,pages,half,d),BF),V((2,pages,half,d),BF),V((2,pages,half,d),BF),V((pages,half,d),BF),V((pages,half,d),F32),
            D((6+pages,)),D((blocks,)),D((blocks,)),D((blocks,)),D((blocks,)),D((9,chunks)),D((9,achunks)),D((4,)),D((3,)),
            D((2,pages)),D((2,pages)),D((pages,)),D((pages,)),D((pages,))],
        compiler_params=pltpu.CompilerParams(vmem_limit_bytes=67043328,collective_id=1,has_side_effects=True),
        name="backward")(hidden,geo,w,q,k,v,p,small,dctx,act,ug,fl,sl,al,ctx,ag)

FREQ=16

def features(box_coords):
    rates = jnp.power(1000.0, -jnp.arange(FREQ, dtype=jnp.float32) / FREQ)
    angles = box_coords.astype(jnp.float32)[:, :, None] * rates[None, None, :]
    angles = jnp.transpose(angles, (1, 0, 2)).reshape(box_coords.shape[1], 4 * FREQ)
    return jnp.concatenate([jnp.cos(angles), jnp.sin(angles)], axis=1)

def body(hidden_in, box_coords, page_lengths, query_weight, query_bias, key_weight, value_weight, value_bias,
         box_weight, box_bias, output_weight, output_bias, first_gain, first_shift, up_weight, up_bias,
         down_weight, down_bias, second_gain, second_shift, output_grad):
    place=lax.axis_index("tensor")
    geo=features(box_coords).astype(BF)
    wide=jnp.concatenate([query_weight,key_weight,value_weight,box_weight],axis=1)
    vec=jnp.stack([output_bias,first_gain,first_shift,down_bias,second_gain,second_shift,output_bias,output_bias])
    q,k,v,p,ctx,*gathered=run_forward(page_lengths,hidden_in,geo,wide,query_bias[None],value_bias[None],box_bias[None],
        output_weight,up_weight,down_weight,up_bias[None])
    ups=gathered.pop()
    rows=output_grad.shape[0]
    ctx=ctx.reshape(ctx.shape[0],rows,ctx.shape[3])
    here=place.reshape(1).astype(jnp.int32)
    layer_out,attn_grad,dctx,act,ug,fl,sl,al,small=run_middle(here,hidden_in,output_grad,ctx,(output_weight,up_weight,down_weight,*gathered),ups,vec,tile=384)
    fin,afin,input_grad=run_backward(hidden_in,geo,wide,q,k,v,p,small,dctx,act,ug,fl,sl,al,ctx,attn_grad)
    d=fin.shape[2]; h=query_weight.shape[1]; o=output_weight.shape[0]; f=up_weight.shape[1]
    fin=fin.reshape(-1,d); afin=afin.reshape(-1,afin.shape[2])[:d]
    down=fin[:f].astype(F32); up=fin[f:f+d].astype(F32); out=fin[f+d:f+d+o].astype(F32)
    tail=fin[f+d+o:f+d+o+8].astype(F32)
    width=d//4
    part=lambda a,b: afin[:,a:b].astype(F32)
    bias=tail[7]
    return (layer_out,input_grad,part(0,h),bias[:h],part(h,2*h),part(2*h,3*h),bias[h:2*h],part(3*h,afin.shape[1]),bias[2*h:],
            out,tail[1,:width],tail[2,:width],tail[3,:width],up,tail[0],down,tail[4,:width],tail[5,:width],tail[6,:width])


def solution(mesh):
    rep=P()
    in_specs=(P("dp",None),P(None,"dp"),P("dp"),P(None,"tensor"),P("tensor"),P(None,"tensor"),P(None,"tensor"),P("tensor"),
        P(None,"tensor"),P("tensor"),P("tensor",None),rep,rep,rep,P(None,"tensor"),P("tensor"),P("tensor",None),rep,rep,rep,P(("dp","tensor"),None))
    out_specs=(P(("dp","tensor"),None),P(("dp","tensor"),None),P(None,"tensor"),P("tensor"),P(None,"tensor"),P(None,"tensor"),P("tensor"),
        P(None,"tensor"),P("tensor"),P("tensor",None),P("tensor"),P("tensor"),P("tensor"),P(None,"tensor"),P("tensor"),P("tensor",None),P("tensor"),P("tensor"),P("tensor"))
    return jax.shard_map(body,mesh=mesh,in_specs=in_specs,out_specs=out_specs,check_vma=False)
```

```python
from functools import partial
import math
import jax
import jax.numpy as jnp
from jax import lax
from jax.experimental import pallas as pl
from jax.experimental.pallas import tpu as pltpu
from jax.sharding import PartitionSpec as P

HEAD = 64
POS = 128
FREQ = 16
PAGE = 512
HALF = PAGE // 2
BLOCK = 256
PART = 192
EPS = 1e-05
LOG2E = 1.4426950408889634
F32 = jnp.float32
BF = jnp.bfloat16
MESH = pl.DeviceIdType.MESH
V = pltpu.VMEM
D = pltpu.SemaphoreType.DMA
S = jax.ShapeDtypeStruct
ANY = pl.BlockSpec(memory_space=pl.ANY)
WHOLE = pl.BlockSpec(memory_space=pltpu.VMEM)


def mm(a, b):
    return jnp.dot(a, b, preferred_element_type=F32)


def mm_nt(a, b):
    return lax.dot_general(a, b, (((1,), (1,)), ((), ())), preferred_element_type=F32)


def mm_tn(a, b):
    return lax.dot_general(a, b, (((0,), (0,)), ((), ())), preferred_element_type=F32)


def columns(x):
    return jnp.sum(x, axis=0, keepdims=True)


def row(ref):
    return ref[...].reshape(1, ref.shape[0])


def normal(z):
    mean = jnp.mean(z, axis=1, keepdims=True)
    centred = z - mean
    inverse = lax.rsqrt(jnp.mean(centred * centred, axis=1, keepdims=True) + EPS)
    return centred * inverse, inverse


def normal_back(inner, scaled, inverse):
    return inverse * (
        inner
        - jnp.mean(inner, axis=1, keepdims=True)
        - scaled * jnp.mean(inner * scaled, axis=1, keepdims=True)
    )


def geometry_of(coords, rates):
    n = coords.shape[1]
    split = jnp.concatenate([coords // 256, coords % 256], axis=0).astype(F32)
    split = jnp.concatenate([split, jnp.zeros_like(split)], axis=0).astype(BF)
    lane = lax.broadcasted_iota(jnp.int32, (16, POS), 1)
    which = lax.broadcasted_iota(jnp.int32, (16, POS), 0)
    spread = jnp.where((lane % (POS // 2)) // FREQ == which % 4, 1.0, 0.0)
    spread = jnp.where(which < 4, 256.0 * spread, spread).astype(BF)
    angle = mm_tn(split, spread) * rates
    turns = jnp.round(angle * 0.6366197723675814)
    r = ((angle - turns * 1.5703125) - turns * 4.837512969970703125e-4) - turns * 7.54978995489188216e-8
    z = r * r
    sine = r + r * z * (-1.6666654611e-1 + z * (8.3321608736e-3 - z * 1.9515295891e-4))
    cosine = 1.0 - 0.5 * z + z * z * (4.166664568298827e-2 + z * (-1.388731625493765e-3 + z * 2.443315711809948e-5))
    quarter = turns.astype(jnp.int32) + jnp.where(lax.broadcasted_iota(jnp.int32, (n, POS), 1) < POS // 2, 1, 0)
    value = jnp.where((quarter & 1) == 1, cosine, sine)
    return jnp.where((quarter & 2) == 2, -value, value).astype(BF)


def mixing(geo):
    half = POS // 2
    c = geo[:, :half]
    s = geo[:, half:]
    return jnp.concatenate([c, -c], axis=1), jnp.concatenate([s, s], axis=1)


def mix(coeff, cos_sign, sin_twice):
    return coeff * cos_sign + pltpu.roll(coeff, POS // 2, 1) * sin_twice


def remote(src, dst, sent, got, device):
    return pltpu.make_async_remote_copy(
        src_ref=src, dst_ref=dst, send_sem=sent, recv_sem=got, device_id=device, device_id_type=MESH
    )


def arrived(ref, sem):
    pltpu.make_async_copy(ref, ref, sem).wait()


def seats():
    group = lax.axis_index("dp")
    place = lax.axis_index("tensor")
    core = lax.rem(place, 2)
    chip = place // 2
    near = place + 1 - 2 * core
    far = place + 2 - 4 * chip
    cross = far + 1 - 2 * core
    return group, place, core, chip, near, far, cross


def page_of(i, pages):
    chip = lax.axis_index("tensor") // 2
    return jnp.where(i < pages, (1 - chip) * pages + i, chip * pages + i - pages)


def forward_kernel(len_ref, rates_ref, h_ref, coords_ref, wb_ref, qb_ref, vb_ref, bb_ref, ub_ref, wq_any, wk_any, wv_any, wo_any, wu_any, wd_any,
                   q_ref, k_ref, v_ref, geo_ref, p_ref, ctx_any, wt_any, ua_any, no_any, nu_any, nd_any, fo_any, fu_any, fd_any, co_any, cu_any, cd_any,
                   wt, cat_q, cat_k, cpage, ubs, l_s, x_s, x_r, y_s, y_r, n_s, n_r, c_s, c_r, u_s, u_r, t_s, t_r, *, pages):
    i = pl.program_id(0)
    cols = q_ref.shape[1]
    heads = cols // HEAD
    box = heads * POS
    group, place, core, chip, near, far, cross = seats()
    side = lax.rem(group, 2)
    beside = group + 1 - 2 * side
    own = (wo_any, wu_any, wd_any)
    nears = (no_any, nu_any, nd_any)
    fars = (fo_any, fu_any, fd_any)
    crosses = (co_any, cu_any, cd_any)
    chunks = []
    for a, w in enumerate(own):
        half = w.shape[0] // 2
        step = min(PART, half)
        chunks += [(a, s, step) for s in range(0, half, step)]

    def rows(c, other):
        a, s, n = chunks[c]
        half = own[a].shape[0] // 2
        return a, pl.ds(pl.multiple_of(half * (1 - side if other else side) + s, 16), n)

    def x_copy(c):
        a, r = rows(c, False)
        return remote(own[a].at[r], fars[a].at[r], x_s.at[c], x_r.at[c], (group, far))

    def y_copy(c, other=False):
        a, r = rows(c, other)
        return remote(fars[a].at[r], fars[a].at[r], y_s.at[c], y_r.at[c], (beside, place))

    def c_copy(c, other):
        a, r = rows(c, other)
        k = 1 if other else 0
        return remote(fars[a].at[r], crosses[a].at[r], c_s.at[k, c], c_r.at[k, c], (group, near))

    n_copies = [remote(own[a], nears[a], n_s.at[a], n_r.at[a], (group, near)) for a in range(3)]
    u_copies = [remote(ubs.at[0], ubs.at[g], u_s.at[g - 1], u_r.at[g - 1], (group, d)) for g, d in ((1, near), (2, far), (3, cross))]
    loads = [pltpu.make_async_copy(w, wt.at[pl.ds(box + n * cols, cols)], l_s.at[n]) for n, w in enumerate((wq_any, wk_any, wv_any))]
    keep_wt = pltpu.make_async_copy(wt, wt_any, l_s.at[3])

    @pl.when(i == 0)
    def _():
        for c in loads:
            c.start()
        ubs[0] = row(ub_ref)
        barrier = pltpu.get_barrier_semaphore()
        peers = [(group, near), (group, far), (group, cross), (beside, place)]
        for device in peers:
            pl.semaphore_signal(barrier, inc=1, device_id=device, device_id_type=MESH)
        pl.semaphore_wait(barrier, len(peers))
        for c in range(len(chunks)):
            x_copy(c).start()
        for n in n_copies:
            n.start()
        for u in u_copies:
            u.start()
        wt[:box, :] = wb_ref[...].T
        for c in loads:
            c.wait()
        keep_wt.start()

    length = len_ref[page_of(i, pages)]
    geo = geometry_of(coords_ref[...], rates_ref[...])
    geo_ref[...] = geo
    proj = mm_nt(h_ref[...], wt[...])
    q_ref[...] = (proj[:, box : box + cols] + row(qb_ref)).astype(BF)
    k_ref[...] = proj[:, box + cols : box + 2 * cols].astype(BF)
    v_ref[...] = (proj[:, box + 2 * cols :] + row(vb_ref)).astype(BF)
    co, si = mixing(geo.astype(F32))
    bias = row(bb_ref)
    for head in range(heads):
        wide = slice(head * POS, (head + 1) * POS)
        lanes = slice(head * HEAD, (head + 1) * HEAD)
        cat_q[head, :, :POS] = mix(proj[:, wide] + bias[:, wide], co, si).astype(BF)
        cat_q[head, :, POS:] = q_ref[:, lanes]
        cat_k[head, :, :POS] = geo
        cat_k[head, :, POS:] = k_ref[:, lanes]
    valid = lax.broadcasted_iota(jnp.int32, (1, PAGE), 1) < length
    scale = LOG2E / math.sqrt(HEAD)
    for head in range(heads):
        lanes = slice(head * HEAD, (head + 1) * HEAD)
        s = mm_nt(cat_q[head], cat_k[head])
        s = jnp.where(valid, s, -1e30)
        top = jnp.max(s, axis=1, keepdims=True)
        e = jnp.exp2((s - top) * scale)
        total = jnp.sum(e, axis=1, keepdims=True)
        p = (e * (1.0 / total)).astype(BF)
        p_ref[head] = p
        c = mm(p, v_ref[:, lanes]).astype(BF)
        for k in range(2):
            cpage[2 * i + k, :, lanes] = c[k * HALF : (k + 1) * HALF]
    for k in range(2):
        piece = 2 * lax.rem(i, pages) + k
        oc = piece // pages
        slot = lax.rem(piece, pages)
        mine = oc == core

        @pl.when(i < pages)
        def _():
            g = jnp.where(mine, 2, 3)
            remote(cpage.at[2 * i + k], ctx_any.at[g, slot], t_s.at[2 * i + k], t_r.at[g, slot], (group, 2 * (1 - chip) + oc)).start()

        @pl.when((i >= pages) & jnp.logical_not(mine))
        def _():
            remote(cpage.at[2 * i + k], ctx_any.at[1, slot], t_s.at[2 * i + k], t_r.at[1, slot], (group, near)).start()

        @pl.when((i >= pages) & mine)
        def _():
            pltpu.make_async_copy(cpage.at[2 * i + k], ctx_any.at[0, slot], t_r.at[0, slot]).start()

    count = 2 * pages

    def forward_on(c):
        x_copy(c).wait_recv()
        y_copy(c).start()
        c_copy(c, False).start()

    plan = {0: [0], 1: [1], 3: [2], 4: [3], 5: [4]}
    for at, todo in plan.items():

        @pl.when(i == at)
        def _():
            for c in todo:
                forward_on(c)

    @pl.when(i == count - 1)
    def _():
        keep_wt.wait()
        for u in u_copies:
            u.wait()
        keep_ub = pltpu.make_async_copy(ubs, ua_any, u_s.at[3])
        keep_ub.start()
        for c in range(len(chunks)):
            y_copy(c, True).wait_recv()
            c_copy(c, True).start()
        for n in n_copies:
            n.wait()
        keep_ub.wait()
        for slot in range(pages):
            for g in range(4):
                arrived(ctx_any.at[g, slot], t_r.at[g, slot])
        for j in range(2 * count):
            if j < count:
                arrived(cpage.at[j], t_s.at[j])
            else:

                @pl.when((j - count) // pages != core)
                def _():
                    arrived(cpage.at[j], t_s.at[j])

        for c in range(len(chunks)):
            x_copy(c).wait_send()
            y_copy(c).wait_send()
            c_copy(c, False).wait()
            c_copy(c, True).wait()


def run_forward(lengths, rates, hidden, coords, wb, qb, vb, bb, ub, wq, wk, wv, wo, wu, wd):
    cols, d = wq.shape
    heads = cols // HEAD
    pages = lengths.shape[0] // 2
    wide = wb.shape[1] + 3 * cols
    own = (wo, wu, wd)
    n = sum((x.shape[0] // 2) // min(PART, x.shape[0] // 2) for x in own)
    page_out = lambda w: pl.BlockSpec((PAGE, w), lambda i: (i, 0))
    rows = 2 * pages * PAGE
    return pl.pallas_call(
        partial(forward_kernel, pages=pages),
        out_shape=[S((rows, cols), BF)] * 3
        + [S((rows, POS), BF), S((2 * pages, heads, PAGE, PAGE), BF), S((4, pages, HALF, cols), BF), S((wide, d), BF), S((4, 1, ub.shape[0]), F32)]
        + [S(x.shape, BF) for x in own] * 3,
        grid=(2 * pages,),
        in_specs=[
            pl.BlockSpec(memory_space=pltpu.SMEM),
            WHOLE,
            pl.BlockSpec((PAGE, d), lambda i: (page_of(i, pages), 0)),
            pl.BlockSpec((4, PAGE), lambda i: (0, page_of(i, pages))),
        ]
        + [WHOLE] * 5
        + [ANY] * 6,
        out_specs=[page_out(cols)] * 3
        + [page_out(POS), pl.BlockSpec((pl.Squeezed(), heads, PAGE, PAGE), lambda i: (i, 0, 0, 0))]
        + [ANY] * 12,
        scratch_shapes=[V((wide, d), BF), V((heads, PAGE, POS + HEAD), BF), V((heads, PAGE, POS + HEAD), BF), V((4 * pages, HALF, cols), BF), V((4, 1, ub.shape[0]), F32)]
        + [D((4,)), D((n,)), D((n,)), D((n,)), D((n,)), D((3,)), D((3,)), D((2, n)), D((2, n)), D((4,)), D((3,)), D((4 * pages,)), D((4, pages))],
        compiler_params=pltpu.CompilerParams(vmem_limit_bytes=56 << 20, collective_id=0, has_side_effects=True),
        name="forward",
    )(lengths, rates, hidden, coords, wb, qb, vb, bb, ub, wq, wk, wv, wo, wu, wd)


def middle_kernel(hid_any, og_any, ctx_any, w0, w1, w2, w3, w4, w5, w6, w7, w8, w9, w10, w11, ub_ref, ob_ref, g1_ref, s1_ref, db_ref, g2_ref, s2_ref,
                  out_any, act_any, ug_any, fl_any, sl_any, scaled_any, second_any, inv_ref, vg_ref,
                  hid, og, ctx, wo, wu, wd, act, ug, fl, sl, lo, first, scaled1, second2, ffn, sem_in, sem_w, sem_out, *, tile):
    rows, d = og.shape
    groups = wu.shape[0]
    weights = (w0, w1, w2, w3, w4, w5, w6, w7, w8, w9, w10, w11)
    place = lax.axis_index("tensor")
    head_loads = [
        pltpu.make_async_copy(ctx_any, ctx, sem_in.at[0]),
        pltpu.make_async_copy(hid_any.at[pl.ds(place * rows, rows)], hid, sem_in.at[1]),
        pltpu.make_async_copy(og_any, og, sem_in.at[2]),
    ]
    loads = [[pltpu.make_async_copy(weights[3 * g + k], (wo, wu, wd)[k].at[g], sem_w.at[k, g]) for g in range(groups)] for k in range(3)]
    head_loads[0].start()
    for c in loads[0]:
        c.start()
    head_loads[1].start()
    for g in range(groups):
        loads[1][g].start()
        loads[2][g].start()
    head_loads[2].start()
    head_loads[0].wait()
    for c in loads[0]:
        c.wait()
    head_loads[1].wait()
    vg_ref[...] = jnp.zeros_like(vg_ref)
    steps = rows // tile

    def stores(i):
        r = pl.ds(pl.multiple_of(i * tile, tile), tile)
        pairs = ((act.at[:, r], act_any.at[:, r]), (ug.at[:, r], ug_any.at[:, r]), (fl.at[r], fl_any.at[r]), (sl.at[r], sl_any.at[r]),
                 (lo.at[r], out_any.at[r]), (scaled1.at[r], scaled_any.at[r]), (second2.at[r], second_any.at[r]))
        return [pltpu.make_async_copy(a, b, sem_out.at[n, i]) for n, (a, b) in enumerate(pairs)]

    def step(i, _):
        r = pl.ds(pl.multiple_of(i * tile, tile), tile)
        attn = mm(ctx[0, r], wo[0])
        for g in range(1, groups):
            attn = attn + mm(ctx[g, r], wo[g])
        scaled, inverse = normal(attn + row(ob_ref) + hid[r].astype(F32))
        f = scaled * row(g1_ref) + row(s1_ref)
        first[...] = f
        scaled1[r] = scaled
        inv_ref[r] = inverse
        fl[r] = f.astype(BF)
        for g in range(groups):

            @pl.when(i == 0)
            def _():
                loads[1][g].wait()

            x = mm(fl[r], wu[g]) + ub_ref[g]
            half = 0.5 + 0.5 * lax.erf(x * 0.7071067811865476)
            a = (x * half).astype(BF)
            act[g, r] = a
            ug[g, r] = (half + x * jnp.exp(-0.5 * x * x) * 0.3989422804014327).astype(BF)

            @pl.when(i == 0)
            def _():
                loads[2][g].wait()

            part = mm(a, wd[g])
            if g == 0:
                ffn[...] = part
            else:
                ffn[...] += part

        scaled, inverse = normal(ffn[...] + row(db_ref) + first[...])
        lo[r] = (scaled * row(g2_ref) + row(s2_ref)).astype(BF)

        @pl.when(i == 0)
        def _():
            head_loads[2].wait()

        o = og[r].astype(F32)
        second = normal_back(o * row(g2_ref), scaled, inverse)
        vg_ref[3:4, :] += columns(second)
        vg_ref[4:5, :] += columns(o * scaled)
        vg_ref[5:6, :] += columns(o)
        sl[r] = second.astype(BF)
        second2[r] = second
        for c in stores(i):
            c.start()
        return 0

    lax.fori_loop(0, steps, step, 0)
    for i in range(steps):
        for c in stores(i):
            c.wait()


def run_middle(hidden, og, ctx, weights, ub, vectors, tile):
    rows, d = og.shape
    groups = 4
    q = weights[0].shape[0]
    f = weights[1].shape[1]
    return pl.pallas_call(
        partial(middle_kernel, tile=tile),
        out_shape=[S((rows, d), BF), S((groups, rows, f), BF), S((groups, rows, f), BF), S((rows, d), BF), S((rows, d), BF), S((rows, d), F32), S((rows, d), F32), S((rows, 1), F32), S((8, d), F32)],
        in_specs=[ANY] * 15 + [WHOLE] * 7,
        out_specs=[ANY] * 7 + [WHOLE] * 2,
        scratch_shapes=[
            V((rows, d), BF), V((rows, d), BF), V((groups, rows, q), BF), V((groups, q, d), BF), V((groups, d, f), BF), V((groups, f, d), BF),
            V((groups, rows, f), BF), V((groups, rows, f), BF), V((rows, d), BF), V((rows, d), BF), V((rows, d), BF),
            V((tile, d), F32), V((rows, d), F32), V((rows, d), F32), V((tile, d), F32),
            D((3,)), D((3, groups)), D((7, rows // tile)),
        ],
        compiler_params=pltpu.CompilerParams(vmem_limit_bytes=62 << 20),
        name="middle",
    )(hidden, og, ctx, *weights, ub, *vectors)


class Cube:
    def __init__(self, main, recv, out, sems, group, place, rows, levels):
        self.main, self.recv, self.out, self.sems = main, recv, out, sems
        self.group, self.place, self.rows, self.levels = group, place, rows, levels
        self.steps = 2 * levels - 1

    def bit(self, j, s):
        if s > 1:
            return 2**s
        return jnp.where(lax.rem(j, 4) == 3, 2 - s, 1 + s)

    def side(self, j, s):
        return lax.rem(self.group // self.bit(j, s), 2)

    def partner(self, j, s):
        return (self.group + self.bit(j, s) * (1 - 2 * self.side(j, s)), self.place)

    def low(self, j, s):
        at = j * self.rows
        for t in range(s):
            at = at + self.side(j, t) * (self.rows >> (t + 1))
        return at

    def span(self, start, n):
        return pl.ds(pl.multiple_of(start, 16), n)

    def r_copy(self, j, s):
        n = self.rows >> (s + 1)
        src = self.main.at[self.span(self.low(j, s) + (1 - self.side(j, s)) * n, n)]
        dst = self.recv.at[self.span(j * self.rows + self.rows - (self.rows >> s), n)]
        return remote(src, dst, self.sems.at[0, j, s], self.sems.at[1, j, s], self.partner(j, s))

    def g_copy(self, j, s):
        here = self.span(self.low(j, s + 1), self.rows >> (s + 1))
        src = self.main if s == self.levels - 1 else self.out
        return remote(src.at[here], self.out.at[here], self.sems.at[2, j, s], self.sems.at[3, j, s], self.partner(j, s))

    def keep(self, j):
        here = self.span(self.low(j, self.levels), self.rows >> self.levels)
        return pltpu.make_async_copy(self.main.at[here], self.out.at[here], self.sems.at[0, j, self.levels])

    def start(self, j):
        self.r_copy(j, 0).start()

    def step(self, k, j):
        last = self.levels - 1
        if k <= last:
            self.r_copy(j, k).wait_recv()
            n = self.rows >> (k + 1)
            mine = self.span(self.low(j, k + 1), n)
            got = self.span(j * self.rows + self.rows - (self.rows >> k), n)
            self.main[mine] = self.main[mine] + self.recv[got]
            if k < last:
                self.r_copy(j, k + 1).start()
            else:
                self.keep(j).start()
                self.g_copy(j, last).start()
        else:
            s = 2 * self.levels - 2 - k
            self.g_copy(j, s + 1).wait_recv()
            if s + 1 == last:
                self.keep(j).wait()
            self.g_copy(j, s).start()

    def finish(self, j):
        self.g_copy(j, 0).wait_recv()
        for s in range(self.levels):
            self.r_copy(j, s).wait_send()
            self.g_copy(j, s).wait_send()


SLOTS = 3


def backward_kernel(h_ref, wt_ref, q_ref, k_ref, v_ref, geo_ref, p_ref, inv_ref, vgin_ref, g1_ref,
                    act_any, ug_any, fl_any, sl_any, scaled_any, second_any, ctx_any,
                    o0, u0, n0, o1, u1, n1, o2, u2, n2, o3, u3, n3,
                    fin_any, afin_any, ig_any,
                    act, ug, wd, wo, fl, sl, al, ctx, cs, crecv, gx, xrecv, main, mrecv, amain, arecv, dsrc, dc, dcp, total, btotal, mixed, drecv, dxrecv, ag, acc, vg, ubg,
                    l_sem, w_sem, c_s, c_r, free, x_s, x_r, r_sem, a_sem, e_s, e_r, d_s, d_r, f_s, f_r, o_sem, *, pages, ways, blocks, per, arows):
    i = pl.program_id(0)
    count = 2 * pages
    group, place, core, chip, near, far, cross = seats()
    cols = q_ref.shape[1]
    heads = cols // HEAD
    box = heads * POS
    d = h_ref.shape[1]
    levels = ways.bit_length() - 1
    f = act.shape[2]
    qc = ctx.shape[2]
    downs = f // BLOCK
    ups = downs + d // BLOCK
    chunks = blocks // per
    achunks = amain.shape[0] // arows
    ffn = Cube(main, mrecv, fin_any, r_sem, group, place, per * BLOCK, levels)
    att = Cube(amain, arecv, afin_any, a_sem, group, place, arows, levels)
    second = total.at[pl.ds(0, pages * BLOCK), :]
    loads = [pltpu.make_async_copy(a, b, l_sem.at[n]) for n, (a, b) in enumerate(((sl_any, sl), (fl_any, fl), (ug_any, ug), (scaled_any, ag), (second_any, second), (ctx_any, ctx)))]
    act_loads = [pltpu.make_async_copy(act_any.at[g], act.at[g], w_sem.at[3, g]) for g in range(4)]
    wo_loads = [pltpu.make_async_copy(a, wo.at[g], w_sem.at[0, g]) for g, a in enumerate((o0, o1, o2, o3))]
    wu_loads = [pltpu.make_async_copy(a, act.at[g], w_sem.at[1, g]) for g, a in enumerate((u0, u1, u2, u3))]
    wd_loads = [pltpu.make_async_copy(a, wd.at[g], w_sem.at[2, g]) for g, a in enumerate((n0, n1, n2, n3))]
    spare = lambda which, slot: wd.at[which, pl.ds(slot * HALF, HALF)]

    def e_copy(g, slot):
        return remote(dsrc.at[g - 1, slot], dc.at[g, slot], e_s.at[g - 1, slot], e_r.at[g - 1, slot], (group, (near, far, cross)[g - 1]))

    def c_copy(b):
        return remote(cs.at[lax.rem(b, 2)], crecv.at[lax.rem(b, SLOTS)], c_s.at[b], c_r.at[b], (group, near))

    def x_copy(b):
        return remote(gx.at[b], xrecv.at[b], x_s.at[b], x_r.at[b], (group, far))

    def span(b):
        return pl.ds(pl.multiple_of(b * BLOCK, BLOCK), BLOCK)

    def plus(a, b):
        return a + b

    def put(b, g, value):
        value = value.astype(BF)
        if g == 0:
            main[span(b)] = value
        elif g == 2:
            gx[b] = value
        else:
            cs[lax.rem(b, 2), g // 2] = value

    def c_add(b):
        c_copy(b).wait_recv()
        slot = lax.rem(b, SLOTS)

        main[span(b)] = plus(main[span(b)], crecv[slot, 0])
        gx[b] = plus(gx[b], crecv[slot, 1])
        x_copy(b).start()

        @pl.when(b + SLOTS < blocks)
        def _():
            pl.semaphore_signal(free, inc=1, device_id=(group, near), device_id_type=MESH)

    def block(b, kind):
        @pl.when(b >= 2)
        def _():
            c_copy(b - 2).wait_send()

        if kind == "down":
            r = pl.ds(pl.multiple_of(b * BLOCK, BLOCK), BLOCK)
            for g in range(4):

                @pl.when(b == 0)
                def _():
                    act_loads[g].wait()

                put(b, g, mm_tn(act[g, :, r], sl[...]))
        elif kind == "up":
            r = pl.ds(pl.multiple_of((b - downs) * BLOCK, BLOCK), BLOCK)
            for g in range(4):
                put(b, g, mm_tn(fl[:, r], ug[g]))
        elif kind == "out":
            width = d // 4
            for g, place_g in enumerate((place, near, far, cross)):
                norms = vg[0:6, :width]
                for a in range(1, 4):
                    norms = jnp.where(place_g == a, vg[0:6, a * width : (a + 1) * width], norms)
                norms = jnp.concatenate([norms, jnp.zeros((6, d - width), F32)], axis=1)
                extra = jnp.concatenate([ubg[g, 0:1, :], norms, jnp.zeros((BLOCK - qc - 7, d), F32)], axis=0)
                put(b, g, jnp.concatenate([mm_tn(ctx[g], al[...]), extra], axis=0))
        else:
            for g in range(4):
                put(b, g, jnp.zeros((BLOCK, d), F32))

        @pl.when(b >= SLOTS)
        def _():
            pl.semaphore_wait(free, 1)

        c_copy(b).start()

    def x_add(b):
        x_copy(b).wait_recv()

        main[span(b)] = plus(main[span(b)], xrecv[b])

        @pl.when(lax.rem(b + 1, per) == 0)
        def _():
            ffn.start(b // per)

    def tick(u, low, high=blocks):
        half = u // 2
        odd = lax.rem(u, 2)
        if high == blocks:

            @pl.when((odd == 0) & (half >= low) & (half < high))
            def _():
                x_add(half)

        for k in range(ffn.steps):
            b = (u - k - 1) // 2

            @pl.when((lax.rem(u + k, 2) == 1) & (u > k) & (b >= low) & (b < high) & (lax.rem(b + 1, per) == 0))
            def _():
                ffn.step(k, b // per)

    @pl.when(i == 0)
    def _():
        loads[0].start()
        for c in act_loads:
            c.start()
        peers = [(group, near), (group, far), (group, cross)]
        peers += [(group + 2**n * (1 - 2 * lax.rem(group // 2**n, 2)), place) for n in range(levels)]
        barrier = pltpu.get_barrier_semaphore()
        for device in peers:
            pl.semaphore_signal(barrier, inc=1, device_id=device, device_id_type=MESH)

        for c in wd_loads:
            c.start()
        loads[2].start()
        loads[4].start()
        loads[3].start()
        for c in wo_loads:
            c.start()
        loads[1].start()
        loads[5].start()
        pl.semaphore_wait(barrier, len(peers))
        loads[0].wait()

        def down_block(b, _):
            block(b, "down")

            @pl.when(b >= 1)
            def _():
                c_add(b - 1)

            return 0

        lax.fori_loop(0, downs, down_block, 0)
        for c in wu_loads:
            c.start()
        for c in wd_loads:
            c.wait()
        for n in (2, 3, 4):
            loads[n].wait()
        c_add(downs - 1)
        for c in wo_loads:
            c.wait()
        for n in (1, 5):
            loads[n].wait()
        vg[...] = vgin_ref[...]
        ubg[...] = jnp.zeros_like(ubg)

        def tile(t, _):
            r = pl.ds(pl.multiple_of(t * BLOCK, BLOCK), BLOCK)
            acc[...] = total[r, :]
            for g in range(4):
                u = (mm_nt(sl[r], wd[g]) * ug[g, r].astype(F32)).astype(BF)
                ug[g, r] = u
                ubg[g, 0:1, :] += columns(u.astype(F32))

                @pl.when(t == 0)
                def _():
                    wu_loads[g].wait()

                acc[...] += mm_nt(u, act[g])

            @pl.when(t == 1)
            def _():
                tick(0, 0)

            fg = acc[...]
            scaled = ag[r]
            a = normal_back(fg * row(g1_ref), scaled, inv_ref[r])
            vg[0:1, :] += columns(a)
            vg[1:2, :] += columns(fg * scaled)
            vg[2:3, :] += columns(fg)
            ag[r] = a
            low = a.astype(BF)
            al[r] = low
            for g in (2, 3, 1, 0):
                value = mm_nt(low, wo[g]).astype(BF)
                if g == 0:
                    dc[0, t] = value
                else:
                    dsrc[g - 1, t] = value
                    e_copy(g, t).start()

            @pl.when(t == 2)
            def _():
                tick(1, 0)

            return 0

        lax.fori_loop(0, pages, tile, 0)

        def up_block(b, _):
            block(b, "up")

            @pl.when(b > downs)
            def _():
                c_add(b - 1)

            @pl.when(b == downs + 1)
            def _():
                tick(2, 0)

            return 0

        lax.fori_loop(downs, ups, up_block, 0)
        block(ups, "out")
        c_add(ups - 1)
        for b in range(ups + 1, blocks):
            block(b, "zero")
            c_add(b - 1)
        c_add(blocks - 1)
        for b in (blocks - 2, blocks - 1):
            c_copy(b).wait_send()
        total[...] = jnp.zeros_like(total)
        btotal[...] = jnp.zeros_like(btotal)
        tick(3, 0)
        for slot in range(pages):
            e_copy(1, slot).wait_recv()

    @pl.when(i == pages)
    def _():
        for g in (2, 3):
            for slot in range(pages):
                e_copy(g, slot).wait_recv()

    for k in range(2):
        piece = 2 * lax.rem(i, pages) + k
        g = jnp.where(piece // pages == core, 0, 1) + jnp.where(i < pages, 0, 2)
        dcp[k * HALF : (k + 1) * HALF, :] = dc[g, lax.rem(piece, pages)]
    geo = geo_ref[...]
    co, si = mixing(geo.astype(F32))
    factor = 1.0 / math.sqrt(HEAD)
    for head in range(heads):
        lanes = slice(head * HEAD, (head + 1) * HEAD)
        p = p_ref[head]
        dcl = dcp[:, lanes]
        mixed[:, box + 2 * cols + head * HEAD : box + 2 * cols + (head + 1) * HEAD] = mm_tn(p, dcl).astype(BF)
        dp = mm_nt(dcl, v_ref[:, lanes])
        pf = p.astype(F32)
        delta = jnp.sum(pf * dp, axis=1, keepdims=True)
        ds = (pf * (dp - delta)).astype(BF)
        both = mm(ds, jnp.concatenate([geo, k_ref[:, lanes]], axis=1)) * factor
        mixed[:, box + head * HEAD : box + (head + 1) * HEAD] = both[:, POS:].astype(BF)
        mixed[:, head * POS : (head + 1) * POS] = mix(both[:, :POS], co, si).astype(BF)
        mixed[:, box + cols + head * HEAD : box + cols + (head + 1) * HEAD] = (mm_tn(ds, q_ref[:, lanes]) * factor).astype(BF)
        if head == heads // 2:

            @pl.when(i < 2)
            def _():
                tick(4 + i, 0)

    total[...] += mm_tn(mixed[...], h_ref[...])
    btotal[0:1, :] += columns(mixed[...].astype(F32))

    def d_copy(kind, slot):
        return remote(spare(2 + kind, slot), drecv.at[kind, slot], d_s.at[kind, slot], d_r.at[kind, slot], (group, near))

    def f_copy(slot):
        return remote(spare(0, slot), dxrecv.at[slot], f_s.at[slot], f_r.at[slot], (group, far))

    kind = jnp.where(i < pages, 1, 0)
    for k in range(2):
        piece = 2 * lax.rem(i, pages) + k
        slot = lax.rem(piece, pages)
        value = mm(mixed[k * HALF : (k + 1) * HALF, :], wt_ref[...]).astype(BF)
        mine = piece // pages == core
        r = pl.ds(pl.multiple_of(slot * HALF, HALF), HALF)

        @pl.when(mine)
        def _():
            wd[kind, r] = value

        @pl.when(jnp.logical_not(mine))
        def _():
            wd[2 + kind, r] = value
            remote(wd.at[2 + kind, r], drecv.at[kind, slot], d_s.at[kind, slot], d_r.at[kind, slot], (group, near)).start()

    @pl.when(i >= 1)
    def _():
        tick(5 + i, 0)

    @pl.when(i == count - 1)
    def _():
        bias = btotal[0:1, :]
        bias = jnp.concatenate([bias[:, : box + cols], bias[:, box + 2 * cols :]], axis=1)
        wide = total.shape[0]
        for b in range(0, wide, 64):
            amain[b : b + 64, :] = total[b : b + 64, :].astype(BF)
        ending = jnp.where(lax.broadcasted_iota(jnp.int32, (amain.shape[0] - wide, d), 0) == 0, bias, 0.0)
        amain[wide:, :] = ending.astype(BF)
        for j in range(achunks):
            att.start(j)
        for slot in range(pages):
            d_copy(0, slot).wait_recv()
            here = spare(0, slot)
            here[...] = plus(here[...], drecv[0, slot])
            f_copy(slot).start()
        first = 5 + count
        when = [0, 4, 7, 9, 11, 13]
        ticks = 2 * (blocks - 1) + ffn.steps - first + 1
        when += list(range(14, 14 + ticks - len(when)))
        waves = max(achunks + 2 * (att.steps - 1), when[-1] + 1)

        def wave(w, _):
            u = -100
            for n in range(ticks):
                u = jnp.where(w == when[n], first + n, u)
            tick(u, 0)
            for k in range(att.steps):

                @pl.when((w >= 2 * k) & (w - 2 * k < achunks))
                def _():
                    att.step(k, w - 2 * k)

            return 0

        lax.fori_loop(0, waves, wave, 0)
        outs = [pltpu.make_async_copy(ag.at[pl.ds(slot * HALF, HALF)], ig_any.at[pl.ds(slot * HALF, HALF)], o_sem.at[slot]) for slot in range(pages)]
        for slot in range(pages):
            r = pl.ds(slot * HALF, HALF)
            d_copy(1, slot).wait_recv()
            f_copy(slot).wait_recv()
            ag[r] = ag[r] + wd[1, r].astype(F32) + drecv[1, slot].astype(F32) + dxrecv[slot].astype(F32)
            outs[slot].start()
        for slot in range(pages):
            outs[slot].wait()
            f_copy(slot).wait_send()
            d_copy(0, slot).wait_send()
            d_copy(1, slot).wait_send()
            for g in (1, 2, 3):
                e_copy(g, slot).wait_send()
        lax.fori_loop(0, achunks, lambda j, _: (att.finish(j), 0)[1], 0)
        lax.fori_loop(0, chunks, lambda j, _: (ffn.finish(j), 0)[1], 0)
        lax.fori_loop(0, blocks, lambda b, _: (x_copy(b).wait_send(), 0)[1], 0)


def run_backward(hidden, wt, q, k, v, geo, p, inv, vg, g1, act, ug, fl, sl, scaled, second, ctx, weights):
    count, heads = p.shape[:2]
    pages = count // 2
    cols = q.shape[1]
    wide, d = wt.shape
    f = act.shape[2]
    rows = fl.shape[0]
    ways = lax.axis_size("dp")
    levels = ways.bit_length() - 1
    chunk = max(BLOCK, 16 * ways)
    per = chunk // BLOCK
    blocks = -(-((f + d) // BLOCK + 1) // per) * per
    chunks = blocks // per
    arows = 16 * ways
    achunks = -(-(wide + 1) // arows)
    turn = lambda i: lax.rem(i + pages, count)
    page = lambda n: pl.BlockSpec((PAGE, n), lambda i: (turn(i), 0))
    once = lambda a: pl.BlockSpec(a.shape, lambda i: (0,) * len(a.shape), pipeline_mode=pl.Buffered(1))
    return pl.pallas_call(
        partial(backward_kernel, pages=pages, ways=ways, blocks=blocks, per=per, arows=arows),
        out_shape=[S((blocks * BLOCK, d), BF), S((achunks * arows, d), BF), S((rows, d), F32)],
        grid=(count,),
        in_specs=[
            pl.BlockSpec((PAGE, d), lambda i: (page_of(turn(i), pages), 0)),
            once(wt), page(cols), page(cols), page(cols), page(POS),
            pl.BlockSpec((pl.Squeezed(), heads, PAGE, PAGE), lambda i: (turn(i), 0, 0, 0)),
            once(inv), once(vg), WHOLE,
        ]
        + [ANY] * 19,
        out_specs=[ANY] * 3,
        scratch_shapes=[
            V(act.shape, BF), V(ug.shape, BF), V((4, f, d), BF), V((4, cols, d), BF), V(fl.shape, BF), V(sl.shape, BF), V(fl.shape, BF), V(ctx.shape, BF),
            V((2, 2, BLOCK, d), BF), V((SLOTS, 2, BLOCK, d), BF), V((blocks, BLOCK, d), BF), V((blocks, BLOCK, d), BF),
            V((blocks * BLOCK, d), BF), V((blocks * BLOCK, d), BF), V((achunks * arows, d), BF), V((achunks * arows, d), BF),
            V((3, pages, HALF, cols), BF), V((4, pages, HALF, cols), BF), V((PAGE, cols), BF), V((wide, d), F32), V((8, wide), F32), V((PAGE, wide), BF),
            V((2, pages, HALF, d), BF), V((pages, HALF, d), BF), V((rows, d), F32), V((BLOCK, d), F32), V((8, d), F32), V((4, 8, f), F32),
            D((6,)), D((4, 4)), D((blocks,)), D((blocks,)), pltpu.SemaphoreType.REGULAR, D((blocks,)), D((blocks,)), D((4, chunks, levels + 1)), D((4, achunks, levels + 1)),
            D((3, pages)), D((3, pages)), D((2, pages)), D((2, pages)), D((pages,)), D((pages,)), D((pages,)),
        ],
        compiler_params=pltpu.CompilerParams(vmem_limit_bytes=67043328, collective_id=1, has_side_effects=True),
        name="backward",
    )(hidden, wt, q, k, v, geo, p, inv, vg, g1, act, ug, fl, sl, scaled, second, ctx, *weights)


def body(
    hidden_in, box_coords, page_lengths, query_weight, query_bias, key_weight, value_weight, value_bias, box_weight, box_bias, output_weight, output_bias,
    first_gain, first_shift, up_weight, up_bias, down_weight, down_bias, second_gain, second_shift, output_grad,
):
    rates = jnp.power(1000.0, -jnp.arange(FREQ, dtype=F32) / FREQ)
    rates = jnp.tile(rates, POS // FREQ).reshape(1, POS)
    q, k, v, geo, p, ctx, wt, ups, *gathered = run_forward(
        page_lengths, rates, hidden_in, box_coords, box_weight, query_bias, value_bias, box_bias, up_bias,
        query_weight.T, key_weight.T, value_weight.T, output_weight, up_weight, down_weight,
    )
    rows, d = output_grad.shape
    ctx = ctx.reshape(ctx.shape[0], rows, ctx.shape[3])
    weights = (output_weight, up_weight, down_weight, *gathered)
    layer_out, act, ug, fl, sl, scaled, second, inv, vg = run_middle(
        hidden_in, output_grad, ctx, weights, ups, (output_bias, first_gain, first_shift, down_bias, second_gain, second_shift), tile=384 if rows % 384 == 0 else BLOCK
    )
    fin, afin, input_grad = run_backward(hidden_in, wt, q, k, v, geo, p, inv, vg, first_gain, act, ug, fl, sl, scaled, second, ctx, weights)
    h = query_weight.shape[1]
    box = box_weight.shape[1]
    o = output_weight.shape[0]
    f = up_weight.shape[1]
    fin = fin.reshape(-1, d)
    afin = afin.reshape(-1, d)
    take = lambda a, n: afin[a : a + n].astype(F32).T
    tail = fin[f + d + o : f + d + o + 8].astype(F32)
    width = d // 4
    bias = afin[box + 3 * h].astype(F32)
    return (
        layer_out, input_grad,
        take(box, h), bias[box : box + h], take(box + h, h), take(box + 2 * h, h), bias[box + h : box + 2 * h], take(0, box), bias[:box],
        fin[f + d : f + d + o].astype(F32), tail[1, :width], tail[2, :width], tail[3, :width],
        fin[f : f + d].astype(F32), tail[0], fin[:f].astype(F32), tail[4, :width], tail[5, :width], tail[6, :width],
    )


def solution(mesh):
    shared = P()
    by_column = P(None, "tensor")
    by_row = P("tensor", None)
    vector = P("tensor")
    tokens = P(("dp", "tensor"), None)
    in_specs = (
        P("dp", None), P(None, "dp"), P("dp"), by_column, vector, by_column, by_column, vector, by_column, vector, by_row, shared,
        shared, shared, by_column, vector, by_row, shared, shared, shared, tokens,
    )
    out_specs = (
        tokens, tokens, by_column, vector, by_column, by_column, vector, by_column, vector, by_row, vector, vector, vector,
        by_column, vector, by_row, vector, vector, vector,
    )
    return jax.shard_map(body, mesh=mesh, in_specs=in_specs, out_specs=out_specs, check_vma=False)
```

```python
from functools import partial
import math
import jax
import jax.numpy as jnp
from jax import lax
from jax.experimental import pallas as pl
from jax.experimental.pallas import tpu as pltpu
from jax.sharding import PartitionSpec as P

HEAD = 64
POS = 128
FREQ = 16
PAGE = 512
HALF = PAGE // 2
BLOCK = 256
PART = 192
EPS = 1e-05
LOG2E = 1.4426950408889634
F32 = jnp.float32
BF = jnp.bfloat16
MESH = pl.DeviceIdType.MESH
V = pltpu.VMEM
D = pltpu.SemaphoreType.DMA
S = jax.ShapeDtypeStruct
ANY = pl.BlockSpec(memory_space=pl.ANY)
WHOLE = pl.BlockSpec(memory_space=pltpu.VMEM)


def mm(a, b):
    return jnp.dot(a, b, preferred_element_type=F32)


def mm_nt(a, b):
    return lax.dot_general(a, b, (((1,), (1,)), ((), ())), preferred_element_type=F32)


def mm_tn(a, b):
    return lax.dot_general(a, b, (((0,), (0,)), ((), ())), preferred_element_type=F32)


def columns(x):
    return jnp.sum(x, axis=0, keepdims=True)


def row(ref):
    return ref[...].reshape(1, ref.shape[0])


def normal(z):
    mean = jnp.mean(z, axis=1, keepdims=True)
    centred = z - mean
    inverse = lax.rsqrt(jnp.mean(centred * centred, axis=1, keepdims=True) + EPS)
    return centred * inverse, inverse


def normal_back(inner, scaled, inverse):
    return inverse * (
        inner
        - jnp.mean(inner, axis=1, keepdims=True)
        - scaled * jnp.mean(inner * scaled, axis=1, keepdims=True)
    )


def geometry_of(coords, rates):
    n = coords.shape[1]
    split = jnp.concatenate([coords // 256, coords % 256], axis=0).astype(F32)
    split = jnp.concatenate([split, jnp.zeros_like(split)], axis=0).astype(BF)
    lane = lax.broadcasted_iota(jnp.int32, (16, POS), 1)
    which = lax.broadcasted_iota(jnp.int32, (16, POS), 0)
    spread = jnp.where((lane % (POS // 2)) // FREQ == which % 4, 1.0, 0.0)
    spread = jnp.where(which < 4, 256.0 * spread, spread).astype(BF)
    angle = mm_tn(split, spread) * rates
    turns = jnp.round(angle * 0.6366197723675814)
    r = ((angle - turns * 1.5703125) - turns * 4.837512969970703125e-4) - turns * 7.54978995489188216e-8
    z = r * r
    sine = r + r * z * (-1.6666654611e-1 + z * (8.3321608736e-3 - z * 1.9515295891e-4))
    cosine = 1.0 - 0.5 * z + z * z * (4.166664568298827e-2 + z * (-1.388731625493765e-3 + z * 2.443315711809948e-5))
    quarter = turns.astype(jnp.int32) + jnp.where(lax.broadcasted_iota(jnp.int32, (n, POS), 1) < POS // 2, 1, 0)
    value = jnp.where((quarter & 1) == 1, cosine, sine)
    return jnp.where((quarter & 2) == 2, -value, value).astype(BF)


def mixing(geo):
    half = POS // 2
    c = geo[:, :half]
    s = geo[:, half:]
    return jnp.concatenate([c, -c], axis=1), jnp.concatenate([s, s], axis=1)


def mix(coeff, cos_sign, sin_twice):
    return coeff * cos_sign + pltpu.roll(coeff, POS // 2, 1) * sin_twice


def remote(src, dst, sent, got, device):
    return pltpu.make_async_remote_copy(
        src_ref=src, dst_ref=dst, send_sem=sent, recv_sem=got, device_id=device, device_id_type=MESH
    )


def arrived(ref, sem):
    pltpu.make_async_copy(ref, ref, sem).wait()


def seats():
    group = lax.axis_index("dp")
    place = lax.axis_index("tensor")
    core = lax.rem(place, 2)
    chip = place // 2
    near = place + 1 - 2 * core
    far = place + 2 - 4 * chip
    cross = far + 1 - 2 * core
    return group, place, core, chip, near, far, cross


def page_of(i, pages):
    chip = lax.axis_index("tensor") // 2
    return jnp.where(i < pages, (1 - chip) * pages + i, chip * pages + i - pages)


def weight_chunks(arrays):
    chunks = []
    for a, w in enumerate(arrays):
        n = w.shape[0] // 4
        step = n // 2 if n > PART // 2 else n
        chunks += [(a, s, step) for s in range(0, n, step)]
    return chunks


def splits(chunk):
    return chunk[2] % 32 == 0


def forward_kernel(len_ref, rates_ref, h_ref, coords_ref, wb_ref, qb_ref, vb_ref, bb_ref, ub_ref, wq_any, wk_any, wv_any, wo_any, wu_any, wd_any,
                   q_ref, k_ref, v_ref, geo_ref, p_ref, ctx_any, wt_any, ua_any, no_any, nu_any, nd_any, fo_any, fu_any, fd_any, co_any, cu_any, cd_any,
                   wt, cat_q, cat_k, cpage, ubs, l_s, x_s, x_r, y_s, y_r, z_s, z_r, n_s, n_r, c_s, c_r, u_s, u_r, t_s, t_r, *, pages):
    i = pl.program_id(0)
    cols = q_ref.shape[1]
    heads = cols // HEAD
    box = heads * POS
    group, place, core, chip, near, far, cross = seats()
    y = lax.rem(group, 2)
    z = lax.rem(group // 2, 2)
    beside = group + 1 - 2 * y
    above = group + 2 - 4 * z
    q = y + 2 * z
    quarter = (q, q + 1 - 2 * y, q + 2 - 4 * z, q + 3 - 2 * y - 4 * z)
    own = (wo_any, wu_any, wd_any)
    nears = (no_any, nu_any, nd_any)
    fars = (fo_any, fu_any, fd_any)
    crosses = (co_any, cu_any, cd_any)
    chunks = weight_chunks(own)

    def rows(c, k, part=None):
        a, s, n = chunks[c]
        start = quarter[k] * (own[a].shape[0] // 4) + s
        if part is not None and splits(chunks[c]):
            n //= 2
            start += part * n
        return pl.ds(pl.multiple_of(start, 16), n)

    def hop(c, k, sems, to, part=None, source=fars):
        a = chunks[c][0]
        r = rows(c, k, part)
        return remote(source[a].at[r], fars[a].at[r], sems[0], sems[1], to)

    def x_copy(c):
        return hop(c, 0, (x_s.at[c], x_r.at[c]), (group, far), source=own)

    def y_copy(c, step, k):
        return hop(c, k, (y_s.at[step, c], y_r.at[step, c]), (beside, place), None if step == 0 else 0)

    def z_copy(c, step, k):
        return hop(c, k, (z_s.at[step, c], z_r.at[step, c]), (above, place), None if step == 0 else 1)

    def c_copy(c, k):
        a = chunks[c][0]
        r = rows(c, k)
        return remote(fars[a].at[r], crosses[a].at[r], c_s.at[k, c], c_r.at[k, c], (group, near))

    def stage(n, c):
        if n == 0:
            x_copy(c).wait_recv()
            y_copy(c, 0, 0).start()
            z_copy(c, 0, 0).start()
            c_copy(c, 0).start()
        elif n == 1:
            y_copy(c, 0, 1).wait_recv()
            if splits(chunks[c]):
                z_copy(c, 1, 1).start()
            z_copy(c, 0, 2).wait_recv()
            y_copy(c, 1, 2).start()
            c_copy(c, 1).start()
            c_copy(c, 2).start()
        else:
            y_copy(c, 1, 3).wait_recv()
            if splits(chunks[c]):
                z_copy(c, 1, 3).wait_recv()
            c_copy(c, 3).start()

    n_copies = [remote(own[a], nears[a], n_s.at[a], n_r.at[a], (group, near)) for a in range(3)]
    u_copies = [remote(ubs.at[0], ubs.at[g], u_s.at[g - 1], u_r.at[g - 1], (group, d)) for g, d in ((1, near), (2, far), (3, cross))]
    loads = [pltpu.make_async_copy(w, wt.at[pl.ds(box + n * cols, cols)], l_s.at[n]) for n, w in enumerate((wq_any, wk_any, wv_any))]
    keep_wt = pltpu.make_async_copy(wt, wt_any, l_s.at[3])

    @pl.when(i == 0)
    def _():
        for c in loads:
            c.start()
        ubs[0] = row(ub_ref)
        barrier = pltpu.get_barrier_semaphore()
        peers = [(group, near), (group, far), (group, cross), (beside, place), (above, place)]
        for device in peers:
            pl.semaphore_signal(barrier, inc=1, device_id=device, device_id_type=MESH)
        pl.semaphore_wait(barrier, len(peers))
        for c in range(len(chunks)):
            x_copy(c).start()
        for n in n_copies:
            n.start()
        for u in u_copies:
            u.start()
        wt[:box, :] = wb_ref[...].T
        for c in loads:
            c.wait()
        keep_wt.start()

    length = len_ref[page_of(i, pages)]
    geo = geometry_of(coords_ref[...], rates_ref[...])
    geo_ref[...] = geo
    proj = mm_nt(h_ref[...], wt[...])
    q_ref[...] = (proj[:, box : box + cols] + row(qb_ref)).astype(BF)
    k_ref[...] = proj[:, box + cols : box + 2 * cols].astype(BF)
    v_ref[...] = (proj[:, box + 2 * cols :] + row(vb_ref)).astype(BF)
    co, si = mixing(geo.astype(F32))
    bias = row(bb_ref)
    for head in range(heads):
        wide = slice(head * POS, (head + 1) * POS)
        lanes = slice(head * HEAD, (head + 1) * HEAD)
        cat_q[head, :, :POS] = mix(proj[:, wide] + bias[:, wide], co, si).astype(BF)
        cat_q[head, :, POS:] = q_ref[:, lanes]
        cat_k[head, :, :POS] = geo
        cat_k[head, :, POS:] = k_ref[:, lanes]
    count = 2 * pages
    plan = {0: [(0, 0)], 1: [(0, 1)], 2: [(1, 0)], 3: [(0, 2)], 4: [(1, 1)], 5: [(0, 3), (0, 4)], 7: [(1, 2), (2, 1)], 8: [(1, 3), (1, 4)], 10: [(2, 0), (2, 2)], 11: [(2, 3), (2, 4)]}

    def tick(odd):
        for at, todo in plan.items():
            if at % 2 == odd:

                @pl.when(i == at // 2)
                def _():
                    for n, c in todo:
                        stage(n, c)

    valid = lax.broadcasted_iota(jnp.int32, (1, PAGE), 1) < length
    scale = LOG2E / math.sqrt(HEAD)
    s = mm_nt(cat_q[0], cat_k[0])
    for head in range(heads):
        lanes = slice(head * HEAD, (head + 1) * HEAD)
        now = s
        if head + 1 < heads:
            s = mm_nt(cat_q[head + 1], cat_k[head + 1])
        now = jnp.where(valid, now, -1e30)
        top = jnp.max(now, axis=1, keepdims=True)
        e = jnp.exp2((now - top) * scale)
        total = jnp.sum(e, axis=1, keepdims=True)
        p = (e * (1.0 / total)).astype(BF)
        p_ref[head] = p
        c = mm(p, v_ref[:, lanes]).astype(BF)
        for k in range(2):
            cpage[2 * i + k, :, lanes] = c[k * HALF : (k + 1) * HALF]
        if head == heads // 2:
            tick(0)
    for k in range(2):
        piece = 2 * lax.rem(i, pages) + k
        oc = piece // pages
        slot = lax.rem(piece, pages)
        mine = oc == core

        @pl.when(i < pages)
        def _():
            g = jnp.where(mine, 2, 3)
            remote(cpage.at[2 * i + k], ctx_any.at[g, slot], t_s.at[2 * i + k], t_r.at[g, slot], (group, 2 * (1 - chip) + oc)).start()

        @pl.when((i >= pages) & jnp.logical_not(mine))
        def _():
            remote(cpage.at[2 * i + k], ctx_any.at[1, slot], t_s.at[2 * i + k], t_r.at[1, slot], (group, near)).start()

        @pl.when((i >= pages) & mine)
        def _():
            pltpu.make_async_copy(cpage.at[2 * i + k], ctx_any.at[0, slot], t_r.at[0, slot]).start()

    tick(1)

    @pl.when(i == count - 1)
    def _():
        keep_wt.wait()
        for u in u_copies:
            u.wait()
        keep_ub = pltpu.make_async_copy(ubs, ua_any, u_s.at[3])
        keep_ub.start()
        for n in n_copies:
            n.wait()
        keep_ub.wait()
        for slot in range(pages):
            for g in range(4):
                arrived(ctx_any.at[g, slot], t_r.at[g, slot])
        for j in range(2 * count):
            if j < count:
                arrived(cpage.at[j], t_s.at[j])
            else:

                @pl.when((j - count) // pages != core)
                def _():
                    arrived(cpage.at[j], t_s.at[j])

        for c in range(len(chunks)):
            x_copy(c).wait_send()
            for step in range(2):
                y_copy(c, step, 2 * step).wait_send()
                if step == 0 or splits(chunks[c]):
                    z_copy(c, step, step).wait_send()
            for k in range(4):
                c_copy(c, k).wait()


def run_forward(lengths, rates, hidden, coords, wb, qb, vb, bb, ub, wq, wk, wv, wo, wu, wd):
    cols, d = wq.shape
    heads = cols // HEAD
    pages = lengths.shape[0] // 2
    wide = wb.shape[1] + 3 * cols
    own = (wo, wu, wd)
    n = len(weight_chunks(own))
    page_out = lambda w: pl.BlockSpec((PAGE, w), lambda i: (i, 0))
    rows = 2 * pages * PAGE
    return pl.pallas_call(
        partial(forward_kernel, pages=pages),
        out_shape=[S((rows, cols), BF)] * 3
        + [S((rows, POS), BF), S((2 * pages, heads, PAGE, PAGE), BF), S((4, pages, HALF, cols), BF), S((wide, d), BF), S((4, 1, ub.shape[0]), F32)]
        + [S(x.shape, BF) for x in own] * 3,
        grid=(2 * pages,),
        in_specs=[
            pl.BlockSpec(memory_space=pltpu.SMEM),
            WHOLE,
            pl.BlockSpec((PAGE, d), lambda i: (page_of(i, pages), 0)),
            pl.BlockSpec((4, PAGE), lambda i: (0, page_of(i, pages))),
        ]
        + [WHOLE] * 5
        + [ANY] * 6,
        out_specs=[page_out(cols)] * 3
        + [page_out(POS), pl.BlockSpec((pl.Squeezed(), heads, PAGE, PAGE), lambda i: (i, 0, 0, 0))]
        + [ANY] * 12,
        scratch_shapes=[V((wide, d), BF), V((heads, PAGE, POS + HEAD), BF), V((heads, PAGE, POS + HEAD), BF), V((4 * pages, HALF, cols), BF), V((4, 1, ub.shape[0]), F32)]
        + [D((4,)), D((n,)), D((n,)), D((2, n)), D((2, n)), D((2, n)), D((2, n)), D((3,)), D((3,)), D((4, n)), D((4, n)), D((4,)), D((3,)), D((4 * pages,)), D((4, pages))],
        compiler_params=pltpu.CompilerParams(vmem_limit_bytes=56 << 20, collective_id=0, has_side_effects=True),
        name="forward",
    )(lengths, rates, hidden, coords, wb, qb, vb, bb, ub, wq, wk, wv, wo, wu, wd)


def middle_kernel(hid_any, og_any, ctx_any, w0, w1, w2, w3, w4, w5, w6, w7, w8, w9, w10, w11, ub_ref, ob_ref, g1_ref, s1_ref, db_ref, g2_ref, s2_ref,
                  out_any, act_any, ug_any, fl_any, sl_any, scaled_any, second_any, inv_ref, vg_ref,
                  hid, og, ctx, wo, wu, wd, act, ug, fl, sl, lo, first, scaled1, second2, ffn, sem_in, sem_w, sem_out, *, tile):
    rows, d = og.shape
    groups = wu.shape[0]
    weights = (w0, w1, w2, w3, w4, w5, w6, w7, w8, w9, w10, w11)
    place = lax.axis_index("tensor")
    head_loads = [
        pltpu.make_async_copy(ctx_any, ctx, sem_in.at[0]),
        pltpu.make_async_copy(hid_any.at[pl.ds(place * rows, rows)], hid, sem_in.at[1]),
        pltpu.make_async_copy(og_any, og, sem_in.at[2]),
    ]
    loads = [[pltpu.make_async_copy(weights[3 * g + k], (wo, wu, wd)[k].at[g], sem_w.at[k, g]) for g in range(groups)] for k in range(3)]
    head_loads[0].start()
    for c in loads[0]:
        c.start()
    head_loads[1].start()
    for g in range(groups):
        loads[1][g].start()
        loads[2][g].start()
    head_loads[2].start()
    head_loads[0].wait()
    for c in loads[0]:
        c.wait()
    head_loads[1].wait()
    vg_ref[...] = jnp.zeros_like(vg_ref)
    for g in range(groups):
        loads[1][g].wait()
        loads[2][g].wait()
    head_loads[2].wait()
    steps = rows // tile

    def stores(i):
        r = pl.ds(pl.multiple_of(i * tile, tile), tile)
        pairs = ((act.at[:, r], act_any.at[:, r]), (ug.at[:, r], ug_any.at[:, r]), (fl.at[r], fl_any.at[r]), (sl.at[r], sl_any.at[r]),
                 (lo.at[r], out_any.at[r]), (scaled1.at[r], scaled_any.at[r]), (second2.at[r], second_any.at[r]))
        return [pltpu.make_async_copy(a, b, sem_out.at[n, i]) for n, (a, b) in enumerate(pairs)]

    def step(i, _):
        r = pl.ds(pl.multiple_of(i * tile, tile), tile)
        attn = mm(ctx[0, r], wo[0])
        for g in range(1, groups):
            attn = attn + mm(ctx[g, r], wo[g])
        scaled, inverse = normal(attn + row(ob_ref) + hid[r].astype(F32))
        f = scaled * row(g1_ref) + row(s1_ref)
        first[...] = f
        scaled1[r] = scaled
        inv_ref[r] = inverse
        fl[r] = f.astype(BF)
        x = mm(fl[r], wu[0])
        for g in range(groups):
            now = x + ub_ref[g]
            if g + 1 < groups:
                x = mm(fl[r], wu[g + 1])
            half = 0.5 + 0.5 * lax.erf(now * 0.7071067811865476)
            a = (now * half).astype(BF)
            act[g, r] = a
            ug[g, r] = (half + now * jnp.exp(-0.5 * now * now) * 0.3989422804014327).astype(BF)
            part = mm(a, wd[g])
            if g == 0:
                ffn[...] = part
            else:
                ffn[...] += part

        scaled, inverse = normal(ffn[...] + row(db_ref) + first[...])
        lo[r] = (scaled * row(g2_ref) + row(s2_ref)).astype(BF)

        o = og[r].astype(F32)
        second = normal_back(o * row(g2_ref), scaled, inverse)
        vg_ref[3:4, :] += columns(second)
        vg_ref[4:5, :] += columns(o * scaled)
        vg_ref[5:6, :] += columns(o)
        sl[r] = second.astype(BF)
        second2[r] = second
        for c in stores(i):
            c.start()
        return 0

    lax.fori_loop(0, steps, step, 0)
    for i in range(steps):
        for c in stores(i):
            c.wait()


def run_middle(hidden, og, ctx, weights, ub, vectors, tile):
    rows, d = og.shape
    groups = 4
    q = weights[0].shape[0]
    f = weights[1].shape[1]
    return pl.pallas_call(
        partial(middle_kernel, tile=tile),
        out_shape=[S((rows, d), BF), S((groups, rows, f), BF), S((groups, rows, f), BF), S((rows, d), BF), S((rows, d), BF), S((rows, d), F32), S((rows, d), F32), S((rows, 1), F32), S((8, d), F32)],
        in_specs=[ANY] * 15 + [WHOLE] * 7,
        out_specs=[ANY] * 7 + [WHOLE] * 2,
        scratch_shapes=[
            V((rows, d), BF), V((rows, d), BF), V((groups, rows, q), BF), V((groups, q, d), BF), V((groups, d, f), BF), V((groups, f, d), BF),
            V((groups, rows, f), BF), V((groups, rows, f), BF), V((rows, d), BF), V((rows, d), BF), V((rows, d), BF),
            V((tile, d), F32), V((rows, d), F32), V((rows, d), F32), V((tile, d), F32),
            D((3,)), D((3, groups)), D((7, rows // tile)),
        ],
        compiler_params=pltpu.CompilerParams(vmem_limit_bytes=62 << 20),
        name="middle",
    )(hidden, og, ctx, *weights, ub, *vectors)


class Cube:
    def __init__(self, main, recv, out, sems, group, place, rows, levels):
        self.main, self.recv, self.out, self.sems = main, recv, out, sems
        self.group, self.place, self.rows, self.levels = group, place, rows, levels
        self.steps = 2 * levels - 1

    def bit(self, j, s):
        if s > 1:
            return 2**s
        return jnp.where(lax.rem(j, 4) == 3, 2 - s, 1 + s)

    def side(self, j, s):
        return lax.rem(self.group // self.bit(j, s), 2)

    def partner(self, j, s):
        return (self.group + self.bit(j, s) * (1 - 2 * self.side(j, s)), self.place)

    def low(self, j, s):
        at = j * self.rows
        for t in range(s):
            at = at + self.side(j, t) * (self.rows >> (t + 1))
        return at

    def span(self, start, n):
        return pl.ds(pl.multiple_of(start, 16), n)

    def r_copy(self, j, s):
        n = self.rows >> (s + 1)
        src = self.main.at[self.span(self.low(j, s) + (1 - self.side(j, s)) * n, n)]
        dst = self.recv.at[self.span(j * self.rows + self.rows - (self.rows >> s), n)]
        return remote(src, dst, self.sems.at[0, j, s], self.sems.at[1, j, s], self.partner(j, s))

    def g_copy(self, j, s):
        here = self.span(self.low(j, s + 1), self.rows >> (s + 1))
        src = self.main if s == self.levels - 1 else self.out
        return remote(src.at[here], self.out.at[here], self.sems.at[2, j, s], self.sems.at[3, j, s], self.partner(j, s))

    def keep(self, j):
        here = self.span(self.low(j, self.levels), self.rows >> self.levels)
        return pltpu.make_async_copy(self.main.at[here], self.out.at[here], self.sems.at[0, j, self.levels])

    def start(self, j):
        self.r_copy(j, 0).start()

    def step(self, k, j):
        last = self.levels - 1
        if k <= last:
            self.r_copy(j, k).wait_recv()
            n = self.rows >> (k + 1)
            mine = self.span(self.low(j, k + 1), n)
            got = self.span(j * self.rows + self.rows - (self.rows >> k), n)
            self.main[mine] = self.main[mine] + self.recv[got]
            if k < last:
                self.r_copy(j, k + 1).start()
            else:
                self.keep(j).start()
                self.g_copy(j, last).start()
        else:
            s = 2 * self.levels - 2 - k
            self.g_copy(j, s + 1).wait_recv()
            if s + 1 == last:
                self.keep(j).wait()
            self.g_copy(j, s).start()

    def finish(self, j):
        self.g_copy(j, 0).wait_recv()
        for s in range(self.levels):
            self.r_copy(j, s).wait_send()
            self.g_copy(j, s).wait_send()


SLOTS = 3


def backward_kernel(h_ref, wt_ref, q_ref, k_ref, v_ref, geo_ref, p_ref, inv_ref, vgin_ref, g1_ref,
                    act_any, ug_any, fl_any, sl_any, scaled_any, second_any, ctx_any,
                    o0, u0, n0, o1, u1, n1, o2, u2, n2, o3, u3, n3,
                    fin_any, afin_any, ig_any,
                    act, ug, wd, wo, fl, sl, al, ctx, cs, crecv, gx, xrecv, main, mrecv, amain, arecv, dsrc, dc, dcp, total, btotal, mixed, drecv, dxrecv, ag, acc, vg, ubg,
                    l_sem, w_sem, c_s, c_r, free, x_s, x_r, r_sem, a_sem, e_s, e_r, d_s, d_r, f_s, f_r, o_sem, *, pages, ways, blocks, per, arows):
    i = pl.program_id(0)
    count = 2 * pages
    group, place, core, chip, near, far, cross = seats()
    cols = q_ref.shape[1]
    heads = cols // HEAD
    box = heads * POS
    d = h_ref.shape[1]
    levels = ways.bit_length() - 1
    f = act.shape[2]
    qc = ctx.shape[2]
    downs = f // BLOCK
    ups = downs + d // BLOCK
    chunks = blocks // per
    achunks = amain.shape[0] // arows
    ffn = Cube(main, mrecv, fin_any, r_sem, group, place, per * BLOCK, levels)
    att = Cube(amain, arecv, afin_any, a_sem, group, place, arows, levels)
    second = total.at[pl.ds(0, pages * BLOCK), :]
    loads = [pltpu.make_async_copy(a, b, l_sem.at[n]) for n, (a, b) in enumerate(((sl_any, sl), (fl_any, fl), (ug_any, ug), (scaled_any, ag), (second_any, second), (ctx_any, ctx)))]
    act_loads = [pltpu.make_async_copy(act_any.at[g], act.at[g], w_sem.at[3, g]) for g in range(4)]
    wo_loads = [pltpu.make_async_copy(a, wo.at[g], w_sem.at[0, g]) for g, a in enumerate((o0, o1, o2, o3))]
    wu_loads = [pltpu.make_async_copy(a, act.at[g], w_sem.at[1, g]) for g, a in enumerate((u0, u1, u2, u3))]
    wd_loads = [pltpu.make_async_copy(a, wd.at[g], w_sem.at[2, g]) for g, a in enumerate((n0, n1, n2, n3))]
    spare = lambda which, slot: wd.at[which, pl.ds(slot * HALF, HALF)]

    def e_copy(g, slot):
        return remote(dsrc.at[g - 1, slot], dc.at[g, slot], e_s.at[g - 1, slot], e_r.at[g - 1, slot], (group, (near, far, cross)[g - 1]))

    def c_copy(b):
        return remote(cs.at[lax.rem(b, 2)], crecv.at[lax.rem(b, SLOTS)], c_s.at[b], c_r.at[b], (group, near))

    def x_copy(b):
        return remote(gx.at[b], xrecv.at[b], x_s.at[b], x_r.at[b], (group, far))

    def span(b):
        return pl.ds(pl.multiple_of(b * BLOCK, BLOCK), BLOCK)

    def plus(a, b):
        return a + b

    def put(b, g, value):
        value = value.astype(BF)
        if g == 0:
            main[span(b)] = value
        elif g == 2:
            gx[b] = value
        else:
            cs[lax.rem(b, 2), g // 2] = value

    def c_add(b):
        c_copy(b).wait_recv()
        slot = lax.rem(b, SLOTS)

        main[span(b)] = plus(main[span(b)], crecv[slot, 0])
        gx[b] = plus(gx[b], crecv[slot, 1])
        x_copy(b).start()

        @pl.when(b + SLOTS < blocks)
        def _():
            pl.semaphore_signal(free, inc=1, device_id=(group, near), device_id_type=MESH)

    def block(b, kind):
        @pl.when(b >= 2)
        def _():
            c_copy(b - 2).wait_send()

        if kind == "down":
            r = pl.ds(pl.multiple_of(b * BLOCK, BLOCK), BLOCK)
            for g in range(4):

                @pl.when(b == 0)
                def _():
                    act_loads[g].wait()

                put(b, g, mm_tn(act[g, :, r], sl[...]))
        elif kind == "up":
            r = pl.ds(pl.multiple_of((b - downs) * BLOCK, BLOCK), BLOCK)
            for g in range(4):
                put(b, g, mm_tn(fl[:, r], ug[g]))
        elif kind == "out":
            width = d // 4
            for g, place_g in enumerate((place, near, far, cross)):
                norms = vg[0:6, :width]
                for a in range(1, 4):
                    norms = jnp.where(place_g == a, vg[0:6, a * width : (a + 1) * width], norms)
                norms = jnp.concatenate([norms, jnp.zeros((6, d - width), F32)], axis=1)
                extra = jnp.concatenate([ubg[g, 0:1, :], norms, jnp.zeros((BLOCK - qc - 7, d), F32)], axis=0)
                put(b, g, jnp.concatenate([mm_tn(ctx[g], al[...]), extra], axis=0))
        else:
            for g in range(4):
                put(b, g, jnp.zeros((BLOCK, d), F32))

        @pl.when(b >= SLOTS)
        def _():
            pl.semaphore_wait(free, 1)

        c_copy(b).start()

    def x_add(b):
        x_copy(b).wait_recv()

        main[span(b)] = plus(main[span(b)], xrecv[b])

        @pl.when(lax.rem(b + 1, per) == 0)
        def _():
            ffn.start(b // per)

    def tick(u, low, high=blocks):
        half = u // 2
        odd = lax.rem(u, 2)
        if high == blocks:

            @pl.when((odd == 0) & (half >= low) & (half < high))
            def _():
                x_add(half)

        for k in range(ffn.steps):
            b = (u - k - 1) // 2

            @pl.when((lax.rem(u + k, 2) == 1) & (u > k) & (b >= low) & (b < high) & (lax.rem(b + 1, per) == 0))
            def _():
                ffn.step(k, b // per)

    @pl.when(i == 0)
    def _():
        loads[0].start()
        for c in act_loads:
            c.start()
        peers = [(group, near), (group, far), (group, cross)]
        peers += [(group + 2**n * (1 - 2 * lax.rem(group // 2**n, 2)), place) for n in range(levels)]
        barrier = pltpu.get_barrier_semaphore()
        for device in peers:
            pl.semaphore_signal(barrier, inc=1, device_id=device, device_id_type=MESH)

        for c in wd_loads:
            c.start()
        loads[2].start()
        loads[4].start()
        loads[3].start()
        for c in wo_loads:
            c.start()
        loads[1].start()
        loads[5].start()
        pl.semaphore_wait(barrier, len(peers))
        loads[0].wait()

        def down_block(b, _):
            block(b, "down")

            @pl.when(b >= 1)
            def _():
                c_add(b - 1)

            return 0

        lax.fori_loop(0, downs, down_block, 0)
        for c in wu_loads:
            c.start()
        for c in wd_loads:
            c.wait()
        for n in (2, 3, 4):
            loads[n].wait()
        c_add(downs - 1)
        for c in wo_loads:
            c.wait()
        for n in (1, 5):
            loads[n].wait()
        vg[...] = vgin_ref[...]
        ubg[...] = jnp.zeros_like(ubg)

        def tile(t, _):
            r = pl.ds(pl.multiple_of(t * BLOCK, BLOCK), BLOCK)
            acc[...] = total[r, :]
            for g in range(4):
                u = (mm_nt(sl[r], wd[g]) * ug[g, r].astype(F32)).astype(BF)
                ug[g, r] = u
                ubg[g, 0:1, :] += columns(u.astype(F32))

                @pl.when(t == 0)
                def _():
                    wu_loads[g].wait()

                acc[...] += mm_nt(u, act[g])

            @pl.when(t == 1)
            def _():
                tick(0, 0)

            fg = acc[...]
            scaled = ag[r]
            a = normal_back(fg * row(g1_ref), scaled, inv_ref[r])
            vg[0:1, :] += columns(a)
            vg[1:2, :] += columns(fg * scaled)
            vg[2:3, :] += columns(fg)
            ag[r] = a
            low = a.astype(BF)
            al[r] = low
            for g in (2, 3, 1, 0):
                value = mm_nt(low, wo[g]).astype(BF)
                if g == 0:
                    dc[0, t] = value
                else:
                    dsrc[g - 1, t] = value
                    e_copy(g, t).start()

            @pl.when(t == 2)
            def _():
                tick(1, 0)

            return 0

        lax.fori_loop(0, pages, tile, 0)

        def up_block(b, _):
            block(b, "up")

            @pl.when(b > downs)
            def _():
                c_add(b - 1)

            @pl.when(b == downs + 1)
            def _():
                tick(2, 0)

            return 0

        lax.fori_loop(downs, ups, up_block, 0)
        block(ups, "out")
        c_add(ups - 1)
        for b in range(ups + 1, blocks):
            block(b, "zero")
            c_add(b - 1)
        c_add(blocks - 1)
        for b in (blocks - 2, blocks - 1):
            c_copy(b).wait_send()
        total[...] = jnp.zeros_like(total)
        btotal[...] = jnp.zeros_like(btotal)
        tick(3, 0)
        for slot in range(pages):
            e_copy(1, slot).wait_recv()

    @pl.when(i == pages)
    def _():
        for g in (2, 3):
            for slot in range(pages):
                e_copy(g, slot).wait_recv()

    for k in range(2):
        piece = 2 * lax.rem(i, pages) + k
        g = jnp.where(piece // pages == core, 0, 1) + jnp.where(i < pages, 0, 2)
        dcp[k * HALF : (k + 1) * HALF, :] = dc[g, lax.rem(piece, pages)]
    geo = geo_ref[...]
    co, si = mixing(geo.astype(F32))
    factor = 1.0 / math.sqrt(HEAD)
    for head in range(heads):
        lanes = slice(head * HEAD, (head + 1) * HEAD)
        p = p_ref[head]
        dcl = dcp[:, lanes]
        mixed[:, box + 2 * cols + head * HEAD : box + 2 * cols + (head + 1) * HEAD] = mm_tn(p, dcl).astype(BF)
        dp = mm_nt(dcl, v_ref[:, lanes])
        pf = p.astype(F32)
        delta = jnp.sum(pf * dp, axis=1, keepdims=True)
        ds = (pf * (dp - delta)).astype(BF)
        both = mm(ds, jnp.concatenate([geo, k_ref[:, lanes]], axis=1)) * factor
        mixed[:, box + head * HEAD : box + (head + 1) * HEAD] = both[:, POS:].astype(BF)
        mixed[:, head * POS : (head + 1) * POS] = mix(both[:, :POS], co, si).astype(BF)
        mixed[:, box + cols + head * HEAD : box + cols + (head + 1) * HEAD] = (mm_tn(ds, q_ref[:, lanes]) * factor).astype(BF)
        if head == heads // 2:

            @pl.when(i < 2)
            def _():
                tick(4 + i, 0)

    total[...] += mm_tn(mixed[...], h_ref[...])
    btotal[0:1, :] += columns(mixed[...].astype(F32))

    def d_copy(kind, slot):
        return remote(spare(2 + kind, slot), drecv.at[kind, slot], d_s.at[kind, slot], d_r.at[kind, slot], (group, near))

    def f_copy(slot):
        return remote(spare(0, slot), dxrecv.at[slot], f_s.at[slot], f_r.at[slot], (group, far))

    kind = jnp.where(i < pages, 1, 0)
    for k in range(2):
        piece = 2 * lax.rem(i, pages) + k
        slot = lax.rem(piece, pages)
        value = mm(mixed[k * HALF : (k + 1) * HALF, :], wt_ref[...]).astype(BF)
        mine = piece // pages == core
        r = pl.ds(pl.multiple_of(slot * HALF, HALF), HALF)

        @pl.when(mine)
        def _():
            wd[kind, r] = value

        @pl.when(jnp.logical_not(mine))
        def _():
            wd[2 + kind, r] = value
            remote(wd.at[2 + kind, r], drecv.at[kind, slot], d_s.at[kind, slot], d_r.at[kind, slot], (group, near)).start()

    @pl.when(i >= 1)
    def _():
        tick(5 + i, 0)

    @pl.when(i == count - 1)
    def _():
        bias = btotal[0:1, :]
        bias = jnp.concatenate([bias[:, : box + cols], bias[:, box + 2 * cols :]], axis=1)
        wide = total.shape[0]
        for b in range(0, wide, 64):
            amain[b : b + 64, :] = total[b : b + 64, :].astype(BF)
        ending = jnp.where(lax.broadcasted_iota(jnp.int32, (amain.shape[0] - wide, d), 0) == 0, bias, 0.0)
        amain[wide:, :] = ending.astype(BF)
        for j in range(achunks):
            att.start(j)
        for slot in range(pages):
            d_copy(0, slot).wait_recv()
            here = spare(0, slot)
            here[...] = plus(here[...], drecv[0, slot])
            f_copy(slot).start()
        first = 5 + count
        when = [0, 4, 7, 9, 11, 13]
        ticks = 2 * (blocks - 1) + ffn.steps - first + 1
        when += list(range(14, 14 + ticks - len(when)))
        waves = max(achunks + 2 * (att.steps - 1), when[-1] + 1)

        def wave(w, _):
            u = -100
            for n in range(ticks):
                u = jnp.where(w == when[n], first + n, u)
            tick(u, 0)
            for k in range(att.steps):

                @pl.when((w >= 2 * k) & (w - 2 * k < achunks))
                def _():
                    att.step(k, w - 2 * k)

            return 0

        lax.fori_loop(0, waves, wave, 0)
        outs = [pltpu.make_async_copy(ag.at[pl.ds(slot * HALF, HALF)], ig_any.at[pl.ds(slot * HALF, HALF)], o_sem.at[slot]) for slot in range(pages)]
        for slot in range(pages):
            r = pl.ds(slot * HALF, HALF)
            d_copy(1, slot).wait_recv()
            f_copy(slot).wait_recv()
            ag[r] = ag[r] + wd[1, r].astype(F32) + drecv[1, slot].astype(F32) + dxrecv[slot].astype(F32)
            outs[slot].start()
        for slot in range(pages):
            outs[slot].wait()
            f_copy(slot).wait_send()
            d_copy(0, slot).wait_send()
            d_copy(1, slot).wait_send()
            for g in (1, 2, 3):
                e_copy(g, slot).wait_send()
        lax.fori_loop(0, achunks, lambda j, _: (att.finish(j), 0)[1], 0)
        lax.fori_loop(0, chunks, lambda j, _: (ffn.finish(j), 0)[1], 0)
        lax.fori_loop(0, blocks, lambda b, _: (x_copy(b).wait_send(), 0)[1], 0)


def run_backward(hidden, wt, q, k, v, geo, p, inv, vg, g1, act, ug, fl, sl, scaled, second, ctx, weights):
    count, heads = p.shape[:2]
    pages = count // 2
    cols = q.shape[1]
    wide, d = wt.shape
    f = act.shape[2]
    rows = fl.shape[0]
    ways = lax.axis_size("dp")
    levels = ways.bit_length() - 1
    chunk = max(BLOCK, 16 * ways)
    per = chunk // BLOCK
    blocks = -(-((f + d) // BLOCK + 1) // per) * per
    chunks = blocks // per
    arows = 16 * ways
    achunks = -(-(wide + 1) // arows)
    turn = lambda i: lax.rem(i + pages, count)
    page = lambda n: pl.BlockSpec((PAGE, n), lambda i: (turn(i), 0))
    once = lambda a: pl.BlockSpec(a.shape, lambda i: (0,) * len(a.shape), pipeline_mode=pl.Buffered(1))
    return pl.pallas_call(
        partial(backward_kernel, pages=pages, ways=ways, blocks=blocks, per=per, arows=arows),
        out_shape=[S((blocks * BLOCK, d), BF), S((achunks * arows, d), BF), S((rows, d), F32)],
        grid=(count,),
        in_specs=[
            pl.BlockSpec((PAGE, d), lambda i: (page_of(turn(i), pages), 0)),
            once(wt), page(cols), page(cols), page(cols), page(POS),
            pl.BlockSpec((pl.Squeezed(), heads, PAGE, PAGE), lambda i: (turn(i), 0, 0, 0)),
            once(inv), once(vg), WHOLE,
        ]
        + [ANY] * 19,
        out_specs=[ANY] * 3,
        scratch_shapes=[
            V(act.shape, BF), V(ug.shape, BF), V((4, f, d), BF), V((4, cols, d), BF), V(fl.shape, BF), V(sl.shape, BF), V(fl.shape, BF), V(ctx.shape, BF),
            V((2, 2, BLOCK, d), BF), V((SLOTS, 2, BLOCK, d), BF), V((blocks, BLOCK, d), BF), V((blocks, BLOCK, d), BF),
            V((blocks * BLOCK, d), BF), V((blocks * BLOCK, d), BF), V((achunks * arows, d), BF), V((achunks * arows, d), BF),
            V((3, pages, HALF, cols), BF), V((4, pages, HALF, cols), BF), V((PAGE, cols), BF), V((wide, d), F32), V((8, wide), F32), V((PAGE, wide), BF),
            V((2, pages, HALF, d), BF), V((pages, HALF, d), BF), V((rows, d), F32), V((BLOCK, d), F32), V((8, d), F32), V((4, 8, f), F32),
            D((6,)), D((4, 4)), D((blocks,)), D((blocks,)), pltpu.SemaphoreType.REGULAR, D((blocks,)), D((blocks,)), D((4, chunks, levels + 1)), D((4, achunks, levels + 1)),
            D((3, pages)), D((3, pages)), D((2, pages)), D((2, pages)), D((pages,)), D((pages,)), D((pages,)),
        ],
        compiler_params=pltpu.CompilerParams(vmem_limit_bytes=67043328, collective_id=1, has_side_effects=True),
        name="backward",
    )(hidden, wt, q, k, v, geo, p, inv, vg, g1, act, ug, fl, sl, scaled, second, ctx, *weights)


def finish_kernel(fin_any, afin_any, down_any, up_any, out_any, q_any, k_any, v_any, box_any,
                  ub_ref, qb_ref, vb_ref, bb_ref, n0_ref, n1_ref, n2_ref, n3_ref, n4_ref, n5_ref,
                  low, alow, full, afull, boxt, l_s, o_s):
    d = low.shape[1]
    cols = q_any.shape[0]
    box = box_any.shape[1]
    wide = box + 3 * cols
    f = down_any.shape[0]
    up = up_any.shape[0]
    rows = f + up + cols
    pieces = [(low, fin_any, full, a, BLOCK, (down_any if a < f else up_any), a % f) for a in range(0, f + up, BLOCK)]
    pieces += [(low, fin_any, full, f + up, cols + 16, out_any, 0)]
    pieces += [(alow, afin_any, afull, a, min(cols, wide + 16 - a), None, 0) for a in range(0, box, cols)]
    pieces += [(alow, afin_any, afull, box + n * cols, cols + (16 if n == 2 else 0), x, 0) for n, x in enumerate((q_any, k_any, v_any))]
    loads = [pltpu.make_async_copy(src.at[pl.ds(a, n)], buf.at[pl.ds(a, n)], l_s.at[j]) for j, (buf, src, _, a, n, _, _) in enumerate(pieces)]
    order = list(range(len(pieces) - 3 - box // cols, len(pieces))) + list(range(len(pieces) - 3 - box // cols))
    for j in order:
        loads[j].start()
    stores = []
    for j in order:
        buf, _, wide_buf, a, n, dst, to = pieces[j]
        loads[j].wait()
        wide_buf[a : a + n, :] = buf[a : a + n, :].astype(F32)
        if dst is not None:
            n = min(n, dst.shape[0])
            c = pltpu.make_async_copy(wide_buf.at[pl.ds(a, n)], dst.at[pl.ds(to, n)], o_s.at[len(stores)])
            c.start()
            stores.append(c)
        elif a + n == box:
            boxt[...] = afull[:box, :].T
            c = pltpu.make_async_copy(boxt, box_any, o_s.at[len(stores)])
            c.start()
            stores.append(c)
    tail = full[rows : rows + 8, :]
    ub_ref[...] = tail[0]
    width = d // 4
    for n, ref in enumerate((n0_ref, n1_ref, n2_ref, n3_ref, n4_ref, n5_ref)):
        ref[...] = tail[1 + n, :width]
    bias = afull[wide : wide + 8, :][0]
    bb_ref[...] = bias[:box]
    qb_ref[...] = bias[box : box + cols]
    vb_ref[...] = bias[box + cols : box + 2 * cols]
    for c in stores:
        c.wait()


def run_finish(fin, afin, f, up, cols, box):
    d = fin.shape[1]
    rows = f + up + cols + 16
    wide = box + 3 * cols + 16
    width = d // 4
    vectors = [S((f,), F32), S((cols,), F32), S((cols,), F32), S((box,), F32)] + [S((width,), F32)] * 6
    n = (f + up) // BLOCK + 4 + box // cols
    return pl.pallas_call(
        finish_kernel,
        out_shape=[S((f, d), F32), S((up, d), F32), S((cols, d), F32)] + [S((cols, d), F32)] * 3 + [S((d, box), F32)] + vectors,
        in_specs=[ANY] * 2,
        out_specs=[ANY] * 7 + [WHOLE] * 10,
        scratch_shapes=[V((rows, d), BF), V((wide, d), BF), V((rows, d), F32), V((wide, d), F32), V((d, box), F32), D((n,)), D((n,))],
        compiler_params=pltpu.CompilerParams(vmem_limit_bytes=62 << 20),
        name="finish",
    )(fin, afin)


def body(
    hidden_in, box_coords, page_lengths, query_weight, query_bias, key_weight, value_weight, value_bias, box_weight, box_bias, output_weight, output_bias,
    first_gain, first_shift, up_weight, up_bias, down_weight, down_bias, second_gain, second_shift, output_grad,
):
    rates = jnp.power(1000.0, -jnp.arange(FREQ, dtype=F32) / FREQ)
    rates = jnp.tile(rates, POS // FREQ).reshape(1, POS)
    q, k, v, geo, p, ctx, wt, ups, *gathered = run_forward(
        page_lengths, rates, hidden_in, box_coords, box_weight, query_bias, value_bias, box_bias, up_bias,
        query_weight.T, key_weight.T, value_weight.T, output_weight, up_weight, down_weight,
    )
    rows, d = output_grad.shape
    ctx = ctx.reshape(ctx.shape[0], rows, ctx.shape[3])
    weights = (output_weight, up_weight, down_weight, *gathered)
    layer_out, act, ug, fl, sl, scaled, second, inv, vg = run_middle(
        hidden_in, output_grad, ctx, weights, ups, (output_bias, first_gain, first_shift, down_bias, second_gain, second_shift), tile=384 if rows % 384 == 0 else BLOCK
    )
    fin, afin, input_grad = run_backward(hidden_in, wt, q, k, v, geo, p, inv, vg, first_gain, act, ug, fl, sl, scaled, second, ctx, weights)
    cols = query_weight.shape[1]
    down, up, out, q, k, v, box, ub, qb, vb, bb, *norms = run_finish(fin, afin, up_weight.shape[1], d, cols, box_weight.shape[1])
    return (
        layer_out, input_grad, q.T, qb, k.T, v.T, vb, box, bb, out, norms[0], norms[1], norms[2], up, ub, down, norms[3], norms[4], norms[5],
    )


def solution(mesh):
    shared = P()
    by_column = P(None, "tensor")
    by_row = P("tensor", None)
    vector = P("tensor")
    tokens = P(("dp", "tensor"), None)
    in_specs = (
        P("dp", None), P(None, "dp"), P("dp"), by_column, vector, by_column, by_column, vector, by_column, vector, by_row, shared,
        shared, shared, by_column, vector, by_row, shared, shared, shared, tokens,
    )
    out_specs = (
        tokens, tokens, by_column, vector, by_column, by_column, vector, by_column, vector, by_row, vector, vector, vector,
        by_column, vector, by_row, vector, vector, vector,
    )
    return jax.shard_map(body, mesh=mesh, in_specs=in_specs, out_specs=out_specs, check_vma=False)
```

```python
from functools import partial
import math
import jax
import jax.numpy as jnp
from jax import lax
from jax.experimental import pallas as pl
from jax.experimental.pallas import tpu as pltpu
from jax.sharding import PartitionSpec as P

HEAD = 64
POS = 128
FREQ = 16
PAGE = 512
HALF = PAGE // 2
BLOCK = 256
PART = 192
EPS = 1e-05
LOG2E = 1.4426950408889634
F32 = jnp.float32
BF = jnp.bfloat16
MESH = pl.DeviceIdType.MESH
V = pltpu.VMEM
D = pltpu.SemaphoreType.DMA
S = jax.ShapeDtypeStruct
ANY = pl.BlockSpec(memory_space=pl.ANY)
WHOLE = pl.BlockSpec(memory_space=pltpu.VMEM)


def mm(a, b):
    return jnp.dot(a, b, preferred_element_type=F32)


def mm_nt(a, b):
    return lax.dot_general(a, b, (((1,), (1,)), ((), ())), preferred_element_type=F32)


def mm_tn(a, b):
    return lax.dot_general(a, b, (((0,), (0,)), ((), ())), preferred_element_type=F32)


def columns(x):
    return jnp.sum(x, axis=0, keepdims=True)


def row(ref):
    return ref[...].reshape(1, ref.shape[0])


def normal(z):
    mean = jnp.mean(z, axis=1, keepdims=True)
    centred = z - mean
    inverse = lax.rsqrt(jnp.mean(centred * centred, axis=1, keepdims=True) + EPS)
    return centred * inverse, inverse


def normal_back(inner, scaled, inverse):
    return inverse * (
        inner
        - jnp.mean(inner, axis=1, keepdims=True)
        - scaled * jnp.mean(inner * scaled, axis=1, keepdims=True)
    )


def geometry_of(coords, rates):
    n = coords.shape[1]
    split = jnp.concatenate([coords // 256, coords % 256], axis=0).astype(F32)
    split = jnp.concatenate([split, jnp.zeros_like(split)], axis=0).astype(BF)
    lane = lax.broadcasted_iota(jnp.int32, (16, POS), 1)
    which = lax.broadcasted_iota(jnp.int32, (16, POS), 0)
    spread = jnp.where((lane % (POS // 2)) // FREQ == which % 4, 1.0, 0.0)
    spread = jnp.where(which < 4, 256.0 * spread, spread).astype(BF)
    angle = mm_tn(split, spread) * rates
    turns = jnp.round(angle * 0.6366197723675814)
    r = ((angle - turns * 1.5703125) - turns * 4.837512969970703125e-4) - turns * 7.54978995489188216e-8
    z = r * r
    sine = r + r * z * (-1.6666654611e-1 + z * (8.3321608736e-3 - z * 1.9515295891e-4))
    cosine = 1.0 - 0.5 * z + z * z * (4.166664568298827e-2 + z * (-1.388731625493765e-3 + z * 2.443315711809948e-5))
    quarter = turns.astype(jnp.int32) + jnp.where(lax.broadcasted_iota(jnp.int32, (n, POS), 1) < POS // 2, 1, 0)
    value = jnp.where((quarter & 1) == 1, cosine, sine)
    return jnp.where((quarter & 2) == 2, -value, value).astype(BF)


def mixing(geo):
    half = POS // 2
    c = geo[:, :half]
    s = geo[:, half:]
    return jnp.concatenate([c, -c], axis=1), jnp.concatenate([s, s], axis=1)


def mix(coeff, cos_sign, sin_twice):
    return coeff * cos_sign + pltpu.roll(coeff, POS // 2, 1) * sin_twice


def remote(src, dst, sent, got, device):
    return pltpu.make_async_remote_copy(
        src_ref=src, dst_ref=dst, send_sem=sent, recv_sem=got, device_id=device, device_id_type=MESH
    )


def arrived(ref, sem):
    pltpu.make_async_copy(ref, ref, sem).wait()


def seats():
    group = lax.axis_index("dp")
    place = lax.axis_index("tensor")
    core = lax.rem(place, 2)
    chip = place // 2
    near = place + 1 - 2 * core
    far = place + 2 - 4 * chip
    cross = far + 1 - 2 * core
    return group, place, core, chip, near, far, cross


def page_of(i, pages):
    chip = lax.axis_index("tensor") // 2
    return jnp.where(i < pages, (1 - chip) * pages + i, chip * pages + i - pages)


def weight_chunks(arrays):
    chunks = []
    for a, w in enumerate(arrays):
        n = w.shape[0] // 4
        step = n // 2 if n > PART // 2 else n
        chunks += [(a, s, step) for s in range(0, n, step)]
    return chunks


def splits(chunk):
    return chunk[2] % 32 == 0


def forward_kernel(len_ref, rates_ref, h_ref, coords_ref, wb_ref, qb_ref, vb_ref, bb_ref, ub_ref, wq_any, wk_any, wv_any, wo_any, wu_any, wd_any,
                   q_ref, k_ref, v_ref, geo_ref, p_ref, ctx_any, wt_any, ua_any, no_any, nu_any, nd_any, fo_any, fu_any, fd_any, co_any, cu_any, cd_any,
                   wt, cat_q, cat_k, cpage, ubs, l_s, x_s, x_r, y_s, y_r, z_s, z_r, n_s, n_r, c_s, c_r, u_s, u_r, t_s, t_r, *, pages):
    i = pl.program_id(0)
    cols = q_ref.shape[1]
    heads = cols // HEAD
    box = heads * POS
    group, place, core, chip, near, far, cross = seats()
    y = lax.rem(group, 2)
    z = lax.rem(group // 2, 2)
    beside = group + 1 - 2 * y
    above = group + 2 - 4 * z
    q = y + 2 * z
    quarter = (q, q + 1 - 2 * y, q + 2 - 4 * z, q + 3 - 2 * y - 4 * z)
    own = (wo_any, wu_any, wd_any)
    nears = (no_any, nu_any, nd_any)
    fars = (fo_any, fu_any, fd_any)
    crosses = (co_any, cu_any, cd_any)
    chunks = weight_chunks(own)

    def rows(c, k, part=None):
        a, s, n = chunks[c]
        start = quarter[k] * (own[a].shape[0] // 4) + s
        if part is not None and splits(chunks[c]):
            n //= 2
            start += part * n
        return pl.ds(pl.multiple_of(start, 16), n)

    def hop(c, k, sems, to, part=None, source=fars):
        a = chunks[c][0]
        r = rows(c, k, part)
        return remote(source[a].at[r], fars[a].at[r], sems[0], sems[1], to)

    def x_copy(c):
        return hop(c, 0, (x_s.at[c], x_r.at[c]), (group, far), source=own)

    def y_copy(c, step, k):
        return hop(c, k, (y_s.at[step, c], y_r.at[step, c]), (beside, place), None if step == 0 else 0)

    def z_copy(c, step, k):
        return hop(c, k, (z_s.at[step, c], z_r.at[step, c]), (above, place), None if step == 0 else 1)

    def c_copy(c, k):
        a = chunks[c][0]
        r = rows(c, k)
        return remote(fars[a].at[r], crosses[a].at[r], c_s.at[k, c], c_r.at[k, c], (group, near))

    def stage(n, c):
        if n == 0:
            x_copy(c).wait_recv()
            y_copy(c, 0, 0).start()
            z_copy(c, 0, 0).start()
            c_copy(c, 0).start()
        elif n == 1:
            y_copy(c, 0, 1).wait_recv()
            if splits(chunks[c]):
                z_copy(c, 1, 1).start()
            z_copy(c, 0, 2).wait_recv()
            y_copy(c, 1, 2).start()
            c_copy(c, 1).start()
            c_copy(c, 2).start()
        else:
            y_copy(c, 1, 3).wait_recv()
            if splits(chunks[c]):
                z_copy(c, 1, 3).wait_recv()
            c_copy(c, 3).start()

    n_copies = [remote(own[a], nears[a], n_s.at[a], n_r.at[a], (group, near)) for a in range(3)]
    u_copies = [remote(ubs.at[0], ubs.at[g], u_s.at[g - 1], u_r.at[g - 1], (group, d)) for g, d in ((1, near), (2, far), (3, cross))]
    loads = [pltpu.make_async_copy(w, wt.at[pl.ds(box + n * cols, cols)], l_s.at[n]) for n, w in enumerate((wq_any, wk_any, wv_any))]
    keep_wt = pltpu.make_async_copy(wt, wt_any, l_s.at[3])

    @pl.when(i == 0)
    def _():
        for c in loads:
            c.start()
        ubs[0] = row(ub_ref)
        barrier = pltpu.get_barrier_semaphore()
        peers = [(group, near), (group, far), (group, cross), (beside, place), (above, place)]
        for device in peers:
            pl.semaphore_signal(barrier, inc=1, device_id=device, device_id_type=MESH)
        pl.semaphore_wait(barrier, len(peers))
        for c in range(len(chunks)):
            x_copy(c).start()
        for n in n_copies:
            n.start()
        for u in u_copies:
            u.start()
        wt[:box, :] = wb_ref[...].T
        for c in loads:
            c.wait()
        keep_wt.start()

    length = len_ref[page_of(i, pages)]
    geo = geometry_of(coords_ref[...], rates_ref[...])
    geo_ref[...] = geo
    proj = mm_nt(h_ref[...], wt[...])
    q_ref[...] = (proj[:, box : box + cols] + row(qb_ref)).astype(BF)
    k_ref[...] = proj[:, box + cols : box + 2 * cols].astype(BF)
    v_ref[...] = (proj[:, box + 2 * cols :] + row(vb_ref)).astype(BF)
    co, si = mixing(geo.astype(F32))
    bias = row(bb_ref)
    for head in range(heads):
        wide = slice(head * POS, (head + 1) * POS)
        lanes = slice(head * HEAD, (head + 1) * HEAD)
        cat_q[head, :, :POS] = mix(proj[:, wide] + bias[:, wide], co, si).astype(BF)
        cat_q[head, :, POS:] = q_ref[:, lanes]
        cat_k[head, :, :POS] = geo
        cat_k[head, :, POS:] = k_ref[:, lanes]
    count = 2 * pages
    plan = {0: [(0, 0)], 1: [(0, 1)], 2: [(1, 0)], 3: [(0, 2)], 4: [(1, 1)], 5: [(0, 3), (0, 4)], 7: [(1, 2), (2, 1)], 8: [(1, 3), (1, 4)], 10: [(2, 0), (2, 2)], 11: [(2, 3), (2, 4)]}

    def tick(odd):
        for at, todo in plan.items():
            if at % 2 == odd:

                @pl.when(i == at // 2)
                def _():
                    for n, c in todo:
                        stage(n, c)

    valid = lax.broadcasted_iota(jnp.int32, (PAGE, 1), 0) < length
    scale = LOG2E / math.sqrt(HEAD)
    s = mm_nt(cat_k[0], cat_q[0])
    for head in range(heads):
        lanes = slice(head * HEAD, (head + 1) * HEAD)
        now = s
        if head + 1 < heads:
            s = mm_nt(cat_k[head + 1], cat_q[head + 1])
        now = jnp.where(valid, now, -1e30)
        top = jnp.max(now, axis=0, keepdims=True)
        e = jnp.exp2((now - top) * scale)
        total = jnp.sum(e, axis=0, keepdims=True)
        p = (e * (1.0 / total)).astype(BF)
        p_ref[head] = p
        c = mm_tn(p, v_ref[:, lanes]).astype(BF)
        for k in range(2):
            cpage[2 * i + k, :, lanes] = c[k * HALF : (k + 1) * HALF]
        if head == heads // 2:
            tick(0)
    for k in range(2):
        piece = 2 * lax.rem(i, pages) + k
        oc = piece // pages
        slot = lax.rem(piece, pages)
        mine = oc == core

        @pl.when(i < pages)
        def _():
            g = jnp.where(mine, 2, 3)
            remote(cpage.at[2 * i + k], ctx_any.at[g, slot], t_s.at[2 * i + k], t_r.at[g, slot], (group, 2 * (1 - chip) + oc)).start()

        @pl.when((i >= pages) & jnp.logical_not(mine))
        def _():
            remote(cpage.at[2 * i + k], ctx_any.at[1, slot], t_s.at[2 * i + k], t_r.at[1, slot], (group, near)).start()

        @pl.when((i >= pages) & mine)
        def _():
            pltpu.make_async_copy(cpage.at[2 * i + k], ctx_any.at[0, slot], t_r.at[0, slot]).start()

    tick(1)

    @pl.when(i == count - 1)
    def _():
        keep_wt.wait()
        for u in u_copies:
            u.wait()
        keep_ub = pltpu.make_async_copy(ubs, ua_any, u_s.at[3])
        keep_ub.start()
        for n in n_copies:
            n.wait()
        keep_ub.wait()
        for slot in range(pages):
            for g in range(4):
                arrived(ctx_any.at[g, slot], t_r.at[g, slot])
        for j in range(2 * count):
            if j < count:
                arrived(cpage.at[j], t_s.at[j])
            else:

                @pl.when((j - count) // pages != core)
                def _():
                    arrived(cpage.at[j], t_s.at[j])

        for c in range(len(chunks)):
            x_copy(c).wait_send()
            for step in range(2):
                y_copy(c, step, 2 * step).wait_send()
                if step == 0 or splits(chunks[c]):
                    z_copy(c, step, step).wait_send()
            for k in range(4):
                c_copy(c, k).wait()


def run_forward(lengths, rates, hidden, coords, wb, qb, vb, bb, ub, wq, wk, wv, wo, wu, wd):
    cols, d = wq.shape
    heads = cols // HEAD
    pages = lengths.shape[0] // 2
    wide = wb.shape[1] + 3 * cols
    own = (wo, wu, wd)
    n = len(weight_chunks(own))
    page_out = lambda w: pl.BlockSpec((PAGE, w), lambda i: (i, 0))
    rows = 2 * pages * PAGE
    return pl.pallas_call(
        partial(forward_kernel, pages=pages),
        out_shape=[S((rows, cols), BF)] * 3
        + [S((rows, POS), BF), S((2 * pages, heads, PAGE, PAGE), BF), S((4, pages, HALF, cols), BF), S((wide, d), BF), S((4, 1, ub.shape[0]), F32)]
        + [S(x.shape, BF) for x in own] * 3,
        grid=(2 * pages,),
        in_specs=[
            pl.BlockSpec(memory_space=pltpu.SMEM),
            WHOLE,
            pl.BlockSpec((PAGE, d), lambda i: (page_of(i, pages), 0)),
            pl.BlockSpec((4, PAGE), lambda i: (0, page_of(i, pages))),
        ]
        + [WHOLE] * 5
        + [ANY] * 6,
        out_specs=[page_out(cols)] * 3
        + [page_out(POS), pl.BlockSpec((pl.Squeezed(), heads, PAGE, PAGE), lambda i: (i, 0, 0, 0))]
        + [ANY] * 12,
        scratch_shapes=[V((wide, d), BF), V((heads, PAGE, POS + HEAD), BF), V((heads, PAGE, POS + HEAD), BF), V((4 * pages, HALF, cols), BF), V((4, 1, ub.shape[0]), F32)]
        + [D((4,)), D((n,)), D((n,)), D((2, n)), D((2, n)), D((2, n)), D((2, n)), D((3,)), D((3,)), D((4, n)), D((4, n)), D((4,)), D((3,)), D((4 * pages,)), D((4, pages))],
        compiler_params=pltpu.CompilerParams(vmem_limit_bytes=56 << 20, collective_id=0, has_side_effects=True),
        name="forward",
    )(lengths, rates, hidden, coords, wb, qb, vb, bb, ub, wq, wk, wv, wo, wu, wd)


def middle_kernel(hid_any, og_any, ctx_any, w0, w1, w2, w3, w4, w5, w6, w7, w8, w9, w10, w11, ub_ref, ob_ref, g1_ref, s1_ref, db_ref, g2_ref, s2_ref,
                  out_any, act_any, ug_any, fl_any, sl_any, scaled_any, second_any, inv_ref, vg_ref,
                  hid, og, ctx, wo, wu, wd, act, ug, fl, sl, lo, first, scaled1, second2, ffn, sem_in, sem_w, sem_out, *, tile):
    rows, d = og.shape
    groups = wu.shape[0]
    weights = (w0, w1, w2, w3, w4, w5, w6, w7, w8, w9, w10, w11)
    place = lax.axis_index("tensor")
    head_loads = [
        pltpu.make_async_copy(ctx_any, ctx, sem_in.at[0]),
        pltpu.make_async_copy(hid_any.at[pl.ds(place * rows, rows)], hid, sem_in.at[1]),
        pltpu.make_async_copy(og_any, og, sem_in.at[2]),
    ]
    loads = [[pltpu.make_async_copy(weights[3 * g + k], (wo, wu, wd)[k].at[g], sem_w.at[k, g]) for g in range(groups)] for k in range(3)]
    head_loads[0].start()
    for c in loads[0]:
        c.start()
    head_loads[1].start()
    for g in range(groups):
        loads[1][g].start()
        loads[2][g].start()
    head_loads[2].start()
    head_loads[0].wait()
    for c in loads[0]:
        c.wait()
    head_loads[1].wait()
    vg_ref[...] = jnp.zeros_like(vg_ref)
    for g in range(groups):
        loads[1][g].wait()
        loads[2][g].wait()
    head_loads[2].wait()
    steps = rows // tile

    def stores(i):
        r = pl.ds(pl.multiple_of(i * tile, tile), tile)
        pairs = ((act.at[:, r], act_any.at[:, r]), (ug.at[:, r], ug_any.at[:, r]), (fl.at[r], fl_any.at[r]), (sl.at[r], sl_any.at[r]),
                 (lo.at[r], out_any.at[r]), (scaled1.at[r], scaled_any.at[r]), (second2.at[r], second_any.at[r]))
        return [pltpu.make_async_copy(a, b, sem_out.at[n, i]) for n, (a, b) in enumerate(pairs)]

    def step(i, _):
        r = pl.ds(pl.multiple_of(i * tile, tile), tile)
        attn = mm(ctx[0, r], wo[0])
        for g in range(1, groups):
            attn = attn + mm(ctx[g, r], wo[g])
        scaled, inverse = normal(attn + row(ob_ref) + hid[r].astype(F32))
        f = scaled * row(g1_ref) + row(s1_ref)
        first[...] = f
        scaled1[r] = scaled
        inv_ref[r] = inverse
        fl[r] = f.astype(BF)
        x = mm(fl[r], wu[0])
        for g in range(groups):
            now = x + ub_ref[g]
            if g + 1 < groups:
                x = mm(fl[r], wu[g + 1])
            half = 0.5 + 0.5 * lax.erf(now * 0.7071067811865476)
            a = (now * half).astype(BF)
            act[g, r] = a
            ug[g, r] = (half + now * jnp.exp(-0.5 * now * now) * 0.3989422804014327).astype(BF)
            part = mm(a, wd[g])
            if g == 0:
                ffn[...] = part
            else:
                ffn[...] += part

        scaled, inverse = normal(ffn[...] + row(db_ref) + first[...])
        lo[r] = (scaled * row(g2_ref) + row(s2_ref)).astype(BF)

        o = og[r].astype(F32)
        second = normal_back(o * row(g2_ref), scaled, inverse)
        vg_ref[3:4, :] += columns(second)
        vg_ref[4:5, :] += columns(o * scaled)
        vg_ref[5:6, :] += columns(o)
        sl[r] = second.astype(BF)
        second2[r] = second
        for c in stores(i):
            c.start()
        return 0

    lax.fori_loop(0, steps, step, 0)
    for i in range(steps):
        for c in stores(i):
            c.wait()


def run_middle(hidden, og, ctx, weights, ub, vectors, tile):
    rows, d = og.shape
    groups = 4
    q = weights[0].shape[0]
    f = weights[1].shape[1]
    return pl.pallas_call(
        partial(middle_kernel, tile=tile),
        out_shape=[S((rows, d), BF), S((groups, rows, f), BF), S((groups, rows, f), BF), S((rows, d), BF), S((rows, d), BF), S((rows, d), F32), S((rows, d), F32), S((rows, 1), F32), S((8, d), F32)],
        in_specs=[ANY] * 15 + [WHOLE] * 7,
        out_specs=[ANY] * 7 + [WHOLE] * 2,
        scratch_shapes=[
            V((rows, d), BF), V((rows, d), BF), V((groups, rows, q), BF), V((groups, q, d), BF), V((groups, d, f), BF), V((groups, f, d), BF),
            V((groups, rows, f), BF), V((groups, rows, f), BF), V((rows, d), BF), V((rows, d), BF), V((rows, d), BF),
            V((tile, d), F32), V((rows, d), F32), V((rows, d), F32), V((tile, d), F32),
            D((3,)), D((3, groups)), D((7, rows // tile)),
        ],
        compiler_params=pltpu.CompilerParams(vmem_limit_bytes=62 << 20),
        name="middle",
    )(hidden, og, ctx, *weights, ub, *vectors)


class Cube:
    def __init__(self, main, recv, out, sems, group, place, rows, levels):
        self.main, self.recv, self.out, self.sems = main, recv, out, sems
        self.group, self.place, self.rows, self.levels = group, place, rows, levels
        self.steps = 2 * levels - 1
        self.sides = [lax.rem(group // 2**n, 2) for n in range(levels)]
        self.mates = [group + 2**n * (1 - 2 * side) for n, side in enumerate(self.sides)]

    def pick(self, j, s, values):
        if s > 1:
            return values[s]
        return jnp.where((j & 3) == 3, values[1 - s], values[s])

    def side(self, j, s):
        return self.pick(j, s, self.sides)

    def partner(self, j, s):
        return (self.pick(j, s, self.mates), self.place)

    def got(self, n, sem, j, s):
        arrived(self.recv.at[pl.ds(0, n)], self.sems.at[sem, j, s])

    def low(self, j, s):
        at = j * self.rows
        for t in range(s):
            at = at + self.side(j, t) * (self.rows >> (t + 1))
        return at

    def span(self, start, n):
        return pl.ds(pl.multiple_of(start, 16), n)

    def r_copy(self, j, s):
        n = self.rows >> (s + 1)
        src = self.main.at[self.span(self.low(j, s) + (1 - self.side(j, s)) * n, n)]
        dst = self.recv.at[self.span(j * self.rows + self.rows - (self.rows >> s), n)]
        return remote(src, dst, self.sems.at[0, j, s], self.sems.at[1, j, s], self.partner(j, s))

    def g_copy(self, j, s):
        here = self.span(self.low(j, s + 1), self.rows >> (s + 1))
        src = self.main if s == self.levels - 1 else self.out
        return remote(src.at[here], self.out.at[here], self.sems.at[2, j, s], self.sems.at[3, j, s], self.partner(j, s))

    def keep(self, j):
        here = self.span(self.low(j, self.levels), self.rows >> self.levels)
        return pltpu.make_async_copy(self.main.at[here], self.out.at[here], self.sems.at[0, j, self.levels])

    def start(self, j):
        self.r_copy(j, 0).start()

    def step(self, k, j):
        last = self.levels - 1
        if k <= last:
            n = self.rows >> (k + 1)
            self.got(n, 1, j, k)
            mine = self.span(self.low(j, k + 1), n)
            got = self.span(j * self.rows + self.rows - (self.rows >> k), n)
            self.main[mine] = self.main[mine] + self.recv[got]
            if k < last:
                self.r_copy(j, k + 1).start()
            else:
                self.keep(j).start()
                self.g_copy(j, last).start()
        else:
            s = 2 * self.levels - 2 - k
            self.got(self.rows >> (s + 2), 3, j, s + 1)
            if s + 1 == last:
                self.got(self.rows >> self.levels, 0, j, self.levels)
            self.g_copy(j, s).start()

    def finish(self, j):
        self.got(self.rows >> 1, 3, j, 0)
        for s in range(self.levels):
            self.got(self.rows >> (s + 1), 0, j, s)
            self.got(self.rows >> (s + 1), 2, j, s)


SLOTS = 3


def backward_kernel(h_ref, wt_ref, q_ref, k_ref, v_ref, geo_ref, p_ref, inv_ref, vgin_ref, g1_ref,
                    act_any, ug_any, fl_any, sl_any, scaled_any, second_any, ctx_any,
                    o0, u0, n0, o1, u1, n1, o2, u2, n2, o3, u3, n3,
                    fin_any, afin_any, ig_any,
                    act, ug, wd, wo, fl, sl, al, ctx, cs, crecv, gx, xrecv, main, mrecv, amain, arecv, dsrc, dc, dcp, total, btotal, mixed, drecv, dxrecv, ag, acc, vg, ubg,
                    l_sem, w_sem, c_s, c_r, free, x_s, x_r, r_sem, a_sem, e_s, e_r, d_s, d_r, f_s, f_r, o_sem, *, pages, ways, blocks, per, arows):
    i = pl.program_id(0)
    count = 2 * pages
    group, place, core, chip, near, far, cross = seats()
    cols = q_ref.shape[1]
    heads = cols // HEAD
    box = heads * POS
    d = h_ref.shape[1]
    levels = ways.bit_length() - 1
    f = act.shape[2]
    qc = ctx.shape[2]
    downs = f // BLOCK
    ups = downs + d // BLOCK
    chunks = blocks // per
    achunks = amain.shape[0] // arows
    ffn = Cube(main, mrecv, fin_any, r_sem, group, place, per * BLOCK, levels)
    att = Cube(amain, arecv, afin_any, a_sem, group, place, arows, levels)
    second = total.at[pl.ds(0, pages * BLOCK), :]
    loads = [pltpu.make_async_copy(a, b, l_sem.at[n]) for n, (a, b) in enumerate(((sl_any, sl), (fl_any, fl), (ug_any, ug), (scaled_any, ag), (second_any, second), (ctx_any, ctx)))]
    act_loads = [pltpu.make_async_copy(act_any.at[g], act.at[g], w_sem.at[3, g]) for g in range(4)]
    wo_loads = [pltpu.make_async_copy(a, wo.at[g], w_sem.at[0, g]) for g, a in enumerate((o0, o1, o2, o3))]
    wu_loads = [pltpu.make_async_copy(a, act.at[g], w_sem.at[1, g]) for g, a in enumerate((u0, u1, u2, u3))]
    wd_loads = [pltpu.make_async_copy(a, wd.at[g], w_sem.at[2, g]) for g, a in enumerate((n0, n1, n2, n3))]
    spare = lambda which, slot: wd.at[which, pl.ds(slot * HALF, HALF)]

    def e_copy(g, slot):
        return remote(dsrc.at[g - 1, slot], dc.at[g, slot], e_s.at[g - 1, slot], e_r.at[g - 1, slot], (group, (near, far, cross)[g - 1]))

    def c_copy(b):
        return remote(cs.at[lax.rem(b, 2)], crecv.at[lax.rem(b, SLOTS)], c_s.at[b], c_r.at[b], (group, near))

    def x_copy(b):
        return remote(gx.at[b], xrecv.at[b], x_s.at[b], x_r.at[b], (group, far))

    def span(b):
        return pl.ds(pl.multiple_of(b * BLOCK, BLOCK), BLOCK)

    def plus(a, b):
        return a + b

    def put(b, g, value):
        value = value.astype(BF)
        if g == 0:
            main[span(b)] = value
        elif g == 2:
            gx[b] = value
        else:
            cs[lax.rem(b, 2), g // 2] = value

    def c_add(b):
        c_copy(b).wait_recv()
        slot = lax.rem(b, SLOTS)

        main[span(b)] = plus(main[span(b)], crecv[slot, 0])
        gx[b] = plus(gx[b], crecv[slot, 1])
        x_copy(b).start()

        @pl.when(b + SLOTS < blocks)
        def _():
            pl.semaphore_signal(free, inc=1, device_id=(group, near), device_id_type=MESH)

    def block(b, kind):
        @pl.when(b >= 2)
        def _():
            c_copy(b - 2).wait_send()

        if kind == "down":
            r = pl.ds(pl.multiple_of(b * BLOCK, BLOCK), BLOCK)
            for g in range(4):

                @pl.when(b == 0)
                def _():
                    act_loads[g].wait()

                put(b, g, mm_tn(act[g, :, r], sl[...]))
        elif kind == "up":
            r = pl.ds(pl.multiple_of((b - downs) * BLOCK, BLOCK), BLOCK)
            for g in range(4):
                put(b, g, mm_tn(fl[:, r], ug[g]))
        elif kind == "out":
            width = d // 4
            for g, place_g in enumerate((place, near, far, cross)):
                norms = vg[0:6, :width]
                for a in range(1, 4):
                    norms = jnp.where(place_g == a, vg[0:6, a * width : (a + 1) * width], norms)
                norms = jnp.concatenate([norms, jnp.zeros((6, d - width), F32)], axis=1)
                extra = jnp.concatenate([ubg[g, 0:1, :], norms, jnp.zeros((BLOCK - qc - 7, d), F32)], axis=0)
                put(b, g, jnp.concatenate([mm_tn(ctx[g], al[...]), extra], axis=0))
        else:
            for g in range(4):
                put(b, g, jnp.zeros((BLOCK, d), F32))

        @pl.when(b >= SLOTS)
        def _():
            pl.semaphore_wait(free, 1)

        c_copy(b).start()

    def x_add(b):
        x_copy(b).wait_recv()

        main[span(b)] = plus(main[span(b)], xrecv[b])

        @pl.when(lax.rem(b + 1, per) == 0)
        def _():
            ffn.start(b // per)

    def tick(u, low, high=blocks):
        half = u // 2
        odd = lax.rem(u, 2)
        if high == blocks:

            @pl.when((odd == 0) & (half >= low) & (half < high))
            def _():
                x_add(half)

        for k in range(ffn.steps):
            b = (u - k - 1) // 2

            @pl.when((lax.rem(u + k, 2) == 1) & (u > k) & (b >= low) & (b < high) & (lax.rem(b + 1, per) == 0))
            def _():
                ffn.step(k, b // per)

    @pl.when(i == 0)
    def _():
        loads[0].start()
        for c in act_loads:
            c.start()
        peers = [(group, near), (group, far), (group, cross)]
        peers += [(group + 2**n * (1 - 2 * lax.rem(group // 2**n, 2)), place) for n in range(levels)]
        barrier = pltpu.get_barrier_semaphore()
        for device in peers:
            pl.semaphore_signal(barrier, inc=1, device_id=device, device_id_type=MESH)

        for c in wd_loads:
            c.start()
        loads[2].start()
        loads[4].start()
        loads[3].start()
        for c in wo_loads:
            c.start()
        loads[1].start()
        loads[5].start()
        pl.semaphore_wait(barrier, len(peers))
        loads[0].wait()

        def down_block(b, _):
            block(b, "down")

            @pl.when(b >= 1)
            def _():
                c_add(b - 1)

            return 0

        lax.fori_loop(0, downs, down_block, 0)
        for c in wu_loads:
            c.start()
        for c in wd_loads:
            c.wait()
        for n in (2, 3, 4):
            loads[n].wait()
        c_add(downs - 1)
        for c in wo_loads:
            c.wait()
        vg[...] = vgin_ref[...]
        ubg[...] = jnp.zeros_like(ubg)

        def tile(t, _):
            r = pl.ds(pl.multiple_of(t * BLOCK, BLOCK), BLOCK)
            acc[...] = total[r, :]
            for g in range(4):
                u = (mm_nt(sl[r], wd[g]) * ug[g, r].astype(F32)).astype(BF)
                ug[g, r] = u
                ubg[g, 0:1, :] += columns(u.astype(F32))

                @pl.when(t == 0)
                def _():
                    wu_loads[g].wait()

                acc[...] += mm_nt(u, act[g])

            @pl.when(t == 1)
            def _():
                tick(0, 0)

            fg = acc[...]
            scaled = ag[r]
            a = normal_back(fg * row(g1_ref), scaled, inv_ref[r])
            vg[0:1, :] += columns(a)
            vg[1:2, :] += columns(fg * scaled)
            vg[2:3, :] += columns(fg)
            ag[r] = a
            low = a.astype(BF)
            al[r] = low
            for g in (2, 3, 1, 0):
                value = mm_nt(low, wo[g]).astype(BF)
                if g == 0:
                    dc[0, t] = value
                else:
                    dsrc[g - 1, t] = value
                    e_copy(g, t).start()

            @pl.when(t == 2)
            def _():
                tick(1, 0)

            return 0

        lax.fori_loop(0, pages, tile, 0)

        def up_block(b, _):
            block(b, "up")

            @pl.when(b > downs)
            def _():
                c_add(b - 1)

            @pl.when(b == downs + 1)
            def _():
                tick(2, 0)

            return 0

        for n in (1, 5):
            loads[n].wait()
        lax.fori_loop(downs, ups, up_block, 0)
        block(ups, "out")
        c_add(ups - 1)
        for b in range(ups + 1, blocks):
            block(b, "zero")
            c_add(b - 1)
        c_add(blocks - 1)
        for b in (blocks - 2, blocks - 1):
            c_copy(b).wait_send()
        total[...] = jnp.zeros_like(total)
        btotal[...] = jnp.zeros_like(btotal)
        tick(3, 0)
        for slot in range(pages):
            e_copy(1, slot).wait_recv()

    @pl.when(i == pages)
    def _():
        for g in (2, 3):
            for slot in range(pages):
                e_copy(g, slot).wait_recv()

    for k in range(2):
        piece = 2 * lax.rem(i, pages) + k
        g = jnp.where(piece // pages == core, 0, 1) + jnp.where(i < pages, 0, 2)
        dcp[k * HALF : (k + 1) * HALF, :] = dc[g, lax.rem(piece, pages)]
    geo = geo_ref[...]
    co, si = mixing(geo.astype(F32))
    factor = 1.0 / math.sqrt(HEAD)
    lanes = [slice(head * HEAD, (head + 1) * HEAD) for head in range(heads)]
    dp = mm_nt(v_ref[:, lanes[0]], dcp[:, lanes[0]])
    for head in range(heads):
        now = dp
        if head + 1 < heads:
            dp = mm_nt(v_ref[:, lanes[head + 1]], dcp[:, lanes[head + 1]])
        p = p_ref[head]
        mixed[:, box + 2 * cols + head * HEAD : box + 2 * cols + (head + 1) * HEAD] = mm(p, dcp[:, lanes[head]]).astype(BF)
        pf = p.astype(F32)
        delta = jnp.sum(pf * now, axis=0, keepdims=True)
        ds = (pf * (now - delta)).astype(BF)
        both = mm_tn(ds, jnp.concatenate([geo, k_ref[:, lanes[head]]], axis=1)) * factor
        mixed[:, box + head * HEAD : box + (head + 1) * HEAD] = both[:, POS:].astype(BF)
        mixed[:, head * POS : (head + 1) * POS] = mix(both[:, :POS], co, si).astype(BF)
        mixed[:, box + cols + head * HEAD : box + cols + (head + 1) * HEAD] = (mm(ds, q_ref[:, lanes[head]]) * factor).astype(BF)

    total[...] += mm_tn(mixed[...], h_ref[...])
    btotal[0:1, :] += columns(mixed[...].astype(F32))

    def d_copy(kind, slot):
        return remote(spare(2 + kind, slot), drecv.at[kind, slot], d_s.at[kind, slot], d_r.at[kind, slot], (group, near))

    def f_copy(slot):
        return remote(spare(0, slot), dxrecv.at[slot], f_s.at[slot], f_r.at[slot], (group, far))

    kind = jnp.where(i < pages, 1, 0)
    dx = mm(mixed[...], wt_ref[...]).astype(BF)
    for k in range(2):
        piece = 2 * lax.rem(i, pages) + k
        slot = lax.rem(piece, pages)
        value = dx[k * HALF : (k + 1) * HALF]
        mine = piece // pages == core
        r = pl.ds(pl.multiple_of(slot * HALF, HALF), HALF)

        @pl.when(mine)
        def _():
            wd[kind, r] = value

        @pl.when(jnp.logical_not(mine))
        def _():
            wd[2 + kind, r] = value
            remote(wd.at[2 + kind, r], drecv.at[kind, slot], d_s.at[kind, slot], d_r.at[kind, slot], (group, near)).start()

    @pl.when(i < 2)
    def _():
        tick(4 + i, 0)

    @pl.when(i >= 1)
    def _():
        tick(5 + i, 0)

    @pl.when(i == count - 1)
    def _():
        bias = btotal[0:1, :]
        bias = jnp.concatenate([bias[:, : box + cols], bias[:, box + 2 * cols :]], axis=1)
        wide = total.shape[0]
        for b in range(0, wide, 64):
            amain[b : b + 64, :] = total[b : b + 64, :].astype(BF)
        ending = jnp.where(lax.broadcasted_iota(jnp.int32, (amain.shape[0] - wide, d), 0) == 0, bias, 0.0)
        amain[wide:, :] = ending.astype(BF)
        for j in range(achunks):
            att.start(j)
        for slot in range(pages):
            d_copy(0, slot).wait_recv()
            here = spare(0, slot)
            here[...] = plus(here[...], drecv[0, slot])
            f_copy(slot).start()
        first = 5 + count
        when = [0, 4, 7, 9, 11, 13]
        ticks = 2 * (blocks - 1) + ffn.steps - first + 1
        when += list(range(14, 14 + ticks - len(when)))
        waves = max(achunks + 2 * (att.steps - 1), when[-1] + 1)

        def wave(w, _):
            u = -100
            for n in range(ticks):
                u = jnp.where(w == when[n], first + n, u)
            tick(u, 0)
            for k in range(att.steps):

                @pl.when((w >= 2 * k) & (w - 2 * k < achunks))
                def _():
                    att.step(k, w - 2 * k)

            return 0

        lax.fori_loop(0, waves, wave, 0)
        outs = [pltpu.make_async_copy(ag.at[pl.ds(slot * HALF, HALF)], ig_any.at[pl.ds(slot * HALF, HALF)], o_sem.at[slot]) for slot in range(pages)]
        for slot in range(pages):
            r = pl.ds(slot * HALF, HALF)
            d_copy(1, slot).wait_recv()
            f_copy(slot).wait_recv()
            ag[r] = ag[r] + wd[1, r].astype(F32) + drecv[1, slot].astype(F32) + dxrecv[slot].astype(F32)
            outs[slot].start()
        for slot in range(pages):
            outs[slot].wait()
            f_copy(slot).wait_send()
            d_copy(0, slot).wait_send()
            d_copy(1, slot).wait_send()
            for g in (1, 2, 3):
                e_copy(g, slot).wait_send()
        lax.fori_loop(0, achunks, lambda j, _: (att.finish(j), 0)[1], 0)
        lax.fori_loop(0, chunks, lambda j, _: (ffn.finish(j), 0)[1], 0)
        lax.fori_loop(0, blocks, lambda b, _: (x_copy(b).wait_send(), 0)[1], 0)


def run_backward(hidden, wt, q, k, v, geo, p, inv, vg, g1, act, ug, fl, sl, scaled, second, ctx, weights):
    count, heads = p.shape[:2]
    pages = count // 2
    cols = q.shape[1]
    wide, d = wt.shape
    f = act.shape[2]
    rows = fl.shape[0]
    ways = lax.axis_size("dp")
    levels = ways.bit_length() - 1
    chunk = max(BLOCK, 16 * ways)
    per = chunk // BLOCK
    blocks = -(-((f + d) // BLOCK + 1) // per) * per
    chunks = blocks // per
    arows = 16 * ways
    achunks = -(-(wide + 1) // arows)
    turn = lambda i: lax.rem(i + pages, count)
    page = lambda n: pl.BlockSpec((PAGE, n), lambda i: (turn(i), 0))
    once = lambda a: pl.BlockSpec(a.shape, lambda i: (0,) * len(a.shape), pipeline_mode=pl.Buffered(1))
    return pl.pallas_call(
        partial(backward_kernel, pages=pages, ways=ways, blocks=blocks, per=per, arows=arows),
        out_shape=[S((blocks * BLOCK, d), BF), S((achunks * arows, d), BF), S((rows, d), F32)],
        grid=(count,),
        in_specs=[
            pl.BlockSpec((PAGE, d), lambda i: (page_of(turn(i), pages), 0)),
            once(wt), page(cols), page(cols), page(cols), page(POS),
            pl.BlockSpec((pl.Squeezed(), heads, PAGE, PAGE), lambda i: (turn(i), 0, 0, 0)),
            once(inv), once(vg), WHOLE,
        ]
        + [ANY] * 19,
        out_specs=[ANY] * 3,
        scratch_shapes=[
            V(act.shape, BF), V(ug.shape, BF), V((4, f, d), BF), V((4, cols, d), BF), V(fl.shape, BF), V(sl.shape, BF), V(fl.shape, BF), V(ctx.shape, BF),
            V((2, 2, BLOCK, d), BF), V((SLOTS, 2, BLOCK, d), BF), V((blocks, BLOCK, d), BF), V((blocks, BLOCK, d), BF),
            V((blocks * BLOCK, d), BF), V((blocks * BLOCK, d), BF), V((achunks * arows, d), BF), V((achunks * arows, d), BF),
            V((3, pages, HALF, cols), BF), V((4, pages, HALF, cols), BF), V((PAGE, cols), BF), V((wide, d), F32), V((8, wide), F32), V((PAGE, wide), BF),
            V((2, pages, HALF, d), BF), V((pages, HALF, d), BF), V((rows, d), F32), V((BLOCK, d), F32), V((8, d), F32), V((4, 8, f), F32),
            D((6,)), D((4, 4)), D((blocks,)), D((blocks,)), pltpu.SemaphoreType.REGULAR, D((blocks,)), D((blocks,)), D((4, chunks, levels + 1)), D((4, achunks, levels + 1)),
            D((3, pages)), D((3, pages)), D((2, pages)), D((2, pages)), D((pages,)), D((pages,)), D((pages,)),
        ],
        compiler_params=pltpu.CompilerParams(vmem_limit_bytes=67043328, collective_id=1, has_side_effects=True),
        name="backward",
    )(hidden, wt, q, k, v, geo, p, inv, vg, g1, act, ug, fl, sl, scaled, second, ctx, *weights)


def finish_kernel(fin_any, afin_any, grad_any, down_any, up_any, out_any, q_any, k_any, v_any, box_any, ig_any,
                  ub_ref, qb_ref, vb_ref, bb_ref, n0_ref, n1_ref, n2_ref, n3_ref, n4_ref, n5_ref,
                  low, alow, full, afull, boxt, grad, l_s, o_s):
    d = low.shape[1]
    cols = q_any.shape[0]
    box = box_any.shape[1]
    wide = box + 3 * cols
    f = down_any.shape[0]
    up = up_any.shape[0]
    rows = f + up + cols
    pieces = [(low, fin_any, full, a, BLOCK, (down_any if a < f else up_any), a % f) for a in range(0, f + up, BLOCK)]
    pieces += [(low, fin_any, full, f + up, cols + 16, out_any, 0)]
    pieces += [(alow, afin_any, afull, a, min(cols, wide + 16 - a), None, 0) for a in range(0, box, cols)]
    pieces += [(alow, afin_any, afull, box + n * cols, cols + (16 if n == 2 else 0), x, 0) for n, x in enumerate((q_any, k_any, v_any))]
    loads = [pltpu.make_async_copy(src.at[pl.ds(a, n)], buf.at[pl.ds(a, n)], l_s.at[j]) for j, (buf, src, _, a, n, _, _) in enumerate(pieces)]
    order = list(range(len(pieces) - 3 - box // cols, len(pieces))) + list(range(len(pieces) - 3 - box // cols))
    for j in order:
        loads[j].start()
    grad_in = pltpu.make_async_copy(grad_any, grad, l_s.at[len(pieces)])
    grad_out = pltpu.make_async_copy(grad, ig_any, o_s.at[len(pieces)])
    grad_in.start()
    stores = []
    for j in order:
        buf, _, wide_buf, a, n, dst, to = pieces[j]
        loads[j].wait()
        wide_buf[a : a + n, :] = buf[a : a + n, :].astype(F32)
        if dst is not None:
            n = min(n, dst.shape[0])
            c = pltpu.make_async_copy(wide_buf.at[pl.ds(a, n)], dst.at[pl.ds(to, n)], o_s.at[len(stores)])
            c.start()
            stores.append(c)
        elif a + n == box:
            boxt[...] = afull[:box, :].T
            c = pltpu.make_async_copy(boxt, box_any, o_s.at[len(stores)])
            c.start()
            stores.append(c)
    grad_in.wait()
    grad_out.start()
    stores.append(grad_out)
    tail = full[rows : rows + 8, :]
    ub_ref[...] = tail[0]
    width = d // 4
    for n, ref in enumerate((n0_ref, n1_ref, n2_ref, n3_ref, n4_ref, n5_ref)):
        ref[...] = tail[1 + n, :width]
    bias = afull[wide : wide + 8, :][0]
    bb_ref[...] = bias[:box]
    qb_ref[...] = bias[box : box + cols]
    vb_ref[...] = bias[box + cols : box + 2 * cols]
    for c in stores:
        c.wait()


def run_finish(fin, afin, grad, f, up, cols, box):
    d = fin.shape[1]
    rows = f + up + cols + 16
    wide = box + 3 * cols + 16
    width = d // 4
    vectors = [S((f,), F32), S((cols,), F32), S((cols,), F32), S((box,), F32)] + [S((width,), F32)] * 6
    n = (f + up) // BLOCK + 5 + box // cols
    return pl.pallas_call(
        finish_kernel,
        out_shape=[S((f, d), F32), S((up, d), F32), S((cols, d), F32)] + [S((cols, d), F32)] * 3 + [S((d, box), F32), S(grad.shape, F32)] + vectors,
        in_specs=[ANY] * 3,
        out_specs=[ANY] * 8 + [WHOLE] * 10,
        scratch_shapes=[V((rows, d), BF), V((wide, d), BF), V((rows, d), F32), V((wide, d), F32), V((d, box), F32), V(grad.shape, F32), D((n,)), D((n,))],
        compiler_params=pltpu.CompilerParams(vmem_limit_bytes=62 << 20),
        name="finish",
    )(fin, afin, grad)


def body(
    hidden_in, box_coords, page_lengths, query_weight, query_bias, key_weight, value_weight, value_bias, box_weight, box_bias, output_weight, output_bias,
    first_gain, first_shift, up_weight, up_bias, down_weight, down_bias, second_gain, second_shift, output_grad,
):
    rates = jnp.power(1000.0, -jnp.arange(FREQ, dtype=F32) / FREQ)
    rates = jnp.tile(rates, POS // FREQ).reshape(1, POS)
    q, k, v, geo, p, ctx, wt, ups, *gathered = run_forward(
        page_lengths, rates, hidden_in, box_coords, box_weight, query_bias, value_bias, box_bias, up_bias,
        query_weight.T, key_weight.T, value_weight.T, output_weight, up_weight, down_weight,
    )
    rows, d = output_grad.shape
    ctx = ctx.reshape(ctx.shape[0], rows, ctx.shape[3])
    weights = (output_weight, up_weight, down_weight, *gathered)
    layer_out, act, ug, fl, sl, scaled, second, inv, vg = run_middle(
        hidden_in, output_grad, ctx, weights, ups, (output_bias, first_gain, first_shift, down_bias, second_gain, second_shift), tile=384 if rows % 384 == 0 else BLOCK
    )
    fin, afin, grad = run_backward(hidden_in, wt, q, k, v, geo, p, inv, vg, first_gain, act, ug, fl, sl, scaled, second, ctx, weights)
    cols = query_weight.shape[1]
    down, up, out, q, k, v, box, input_grad, ub, qb, vb, bb, *norms = run_finish(fin, afin, grad, up_weight.shape[1], d, cols, box_weight.shape[1])
    return (
        layer_out, input_grad, q.T, qb, k.T, v.T, vb, box, bb, out, norms[0], norms[1], norms[2], up, ub, down, norms[3], norms[4], norms[5],
    )


def solution(mesh):
    shared = P()
    by_column = P(None, "tensor")
    by_row = P("tensor", None)
    vector = P("tensor")
    tokens = P(("dp", "tensor"), None)
    in_specs = (
        P("dp", None), P(None, "dp"), P("dp"), by_column, vector, by_column, by_column, vector, by_column, vector, by_row, shared,
        shared, shared, by_column, vector, by_row, shared, shared, shared, tokens,
    )
    out_specs = (
        tokens, tokens, by_column, vector, by_column, by_column, vector, by_column, vector, by_row, vector, vector, vector,
        by_column, vector, by_row, vector, vector, vector,
    )
    return jax.shard_map(body, mesh=mesh, in_specs=in_specs, out_specs=out_specs, check_vma=False)
```

```python
from functools import partial
import math
import jax
import jax.numpy as jnp
from jax import lax
from jax.experimental import pallas as pl
from jax.experimental.pallas import tpu as pltpu
from jax.sharding import PartitionSpec as P

HEAD = 64
POS = 128
FREQ = 16
PAGE = 512
HALF = PAGE // 2
BLOCK = 256
PART = 192
EPS = 1e-05
LOG2E = 1.4426950408889634
F32 = jnp.float32
BF = jnp.bfloat16
MESH = pl.DeviceIdType.MESH
V = pltpu.VMEM
D = pltpu.SemaphoreType.DMA
S = jax.ShapeDtypeStruct
ANY = pl.BlockSpec(memory_space=pl.ANY)
WHOLE = pl.BlockSpec(memory_space=pltpu.VMEM)


def mm(a, b):
    return jnp.dot(a, b, preferred_element_type=F32)


def mm_nt(a, b):
    return lax.dot_general(a, b, (((1,), (1,)), ((), ())), preferred_element_type=F32)


def mm_tn(a, b):
    return lax.dot_general(a, b, (((0,), (0,)), ((), ())), preferred_element_type=F32)


def columns(x):
    return jnp.sum(x, axis=0, keepdims=True)


def row(ref):
    return ref[...].reshape(1, ref.shape[0])


def normal(z):
    mean = jnp.mean(z, axis=1, keepdims=True)
    centred = z - mean
    inverse = lax.rsqrt(jnp.mean(centred * centred, axis=1, keepdims=True) + EPS)
    return centred * inverse, inverse


def normal_back(inner, scaled, inverse):
    return inverse * (
        inner
        - jnp.mean(inner, axis=1, keepdims=True)
        - scaled * jnp.mean(inner * scaled, axis=1, keepdims=True)
    )


def geometry_of(coords, rates):
    n = coords.shape[1]
    split = jnp.concatenate([coords // 256, coords % 256], axis=0).astype(F32)
    split = jnp.concatenate([split, jnp.zeros_like(split)], axis=0).astype(BF)
    lane = lax.broadcasted_iota(jnp.int32, (16, POS), 1)
    which = lax.broadcasted_iota(jnp.int32, (16, POS), 0)
    spread = jnp.where((lane % (POS // 2)) // FREQ == which % 4, 1.0, 0.0)
    spread = jnp.where(which < 4, 256.0 * spread, spread).astype(BF)
    angle = mm_tn(split, spread) * rates
    turns = jnp.round(angle * 0.6366197723675814)
    r = ((angle - turns * 1.5703125) - turns * 4.837512969970703125e-4) - turns * 7.54978995489188216e-8
    z = r * r
    sine = r + r * z * (-1.6666654611e-1 + z * (8.3321608736e-3 - z * 1.9515295891e-4))
    cosine = 1.0 - 0.5 * z + z * z * (4.166664568298827e-2 + z * (-1.388731625493765e-3 + z * 2.443315711809948e-5))
    quarter = turns.astype(jnp.int32) + jnp.where(lax.broadcasted_iota(jnp.int32, (n, POS), 1) < POS // 2, 1, 0)
    value = jnp.where((quarter & 1) == 1, cosine, sine)
    return jnp.where((quarter & 2) == 2, -value, value).astype(BF)


def mixing(geo):
    half = POS // 2
    c = geo[:, :half]
    s = geo[:, half:]
    return jnp.concatenate([c, -c], axis=1), jnp.concatenate([s, s], axis=1)


def mix(coeff, cos_sign, sin_twice):
    return coeff * cos_sign + pltpu.roll(coeff, POS // 2, 1) * sin_twice


def remote(src, dst, sent, got, device):
    return pltpu.make_async_remote_copy(
        src_ref=src, dst_ref=dst, send_sem=sent, recv_sem=got, device_id=device, device_id_type=MESH
    )


def arrived(ref, sem):
    pltpu.make_async_copy(ref, ref, sem).wait()


def seats():
    group = lax.axis_index("dp")
    place = lax.axis_index("tensor")
    core = lax.rem(place, 2)
    chip = place // 2
    near = place + 1 - 2 * core
    far = place + 2 - 4 * chip
    cross = far + 1 - 2 * core
    return group, place, core, chip, near, far, cross


def page_of(i, pages):
    chip = lax.axis_index("tensor") // 2
    return jnp.where(i < pages, (1 - chip) * pages + i, chip * pages + i - pages)


def weight_chunks(arrays):
    chunks = []
    for a, w in enumerate(arrays):
        n = w.shape[0] // 4
        step = n // 2 if n > PART // 2 else n
        chunks += [(a, s, step) for s in range(0, n, step)]
    return chunks


def splits(chunk):
    return chunk[2] % 32 == 0


def forward_kernel(len_ref, rates_ref, h_ref, coords_ref, wb_ref, qb_ref, vb_ref, bb_ref, ub_ref, wq_any, wk_any, wv_any, wo_any, wu_any, wd_any,
                   q_ref, k_ref, v_ref, geo_ref, p_ref, ctx_any, wt_any, ua_any, no_any, nu_any, nd_any, fo_any, fu_any, fd_any, co_any, cu_any, cd_any,
                   wt, cat_q, cat_k, cpage, ubs, l_s, x_s, x_r, y_s, y_r, z_s, z_r, n_s, n_r, c_s, c_r, u_s, u_r, t_s, t_r, *, pages):
    i = pl.program_id(0)
    cols = q_ref.shape[1]
    heads = cols // HEAD
    box = heads * POS
    group, place, core, chip, near, far, cross = seats()
    y = lax.rem(group, 2)
    z = lax.rem(group // 2, 2)
    beside = group + 1 - 2 * y
    above = group + 2 - 4 * z
    q = y + 2 * z
    quarter = (q, q + 1 - 2 * y, q + 2 - 4 * z, q + 3 - 2 * y - 4 * z)
    own = (wo_any, wu_any, wd_any)
    nears = (no_any, nu_any, nd_any)
    fars = (fo_any, fu_any, fd_any)
    crosses = (co_any, cu_any, cd_any)
    chunks = weight_chunks(own)

    def rows(c, k, part=None):
        a, s, n = chunks[c]
        start = quarter[k] * (own[a].shape[0] // 4) + s
        if part is not None and splits(chunks[c]):
            n //= 2
            start += part * n
        return pl.ds(pl.multiple_of(start, 16), n)

    def hop(c, k, sems, to, part=None, source=fars):
        a = chunks[c][0]
        r = rows(c, k, part)
        return remote(source[a].at[r], fars[a].at[r], sems[0], sems[1], to)

    def x_copy(c):
        return hop(c, 0, (x_s.at[c], x_r.at[c]), (group, far), source=own)

    def y_copy(c, step, k):
        return hop(c, k, (y_s.at[step, c], y_r.at[step, c]), (beside, place), None if step == 0 else 0)

    def z_copy(c, step, k):
        return hop(c, k, (z_s.at[step, c], z_r.at[step, c]), (above, place), None if step == 0 else 1)

    def c_copy(c, k):
        a = chunks[c][0]
        r = rows(c, k)
        return remote(fars[a].at[r], crosses[a].at[r], c_s.at[k, c], c_r.at[k, c], (group, near))

    def stage(n, c):
        if n == 0:
            x_copy(c).wait_recv()
            y_copy(c, 0, 0).start()
            z_copy(c, 0, 0).start()
            c_copy(c, 0).start()
        elif n == 1:
            y_copy(c, 0, 1).wait_recv()
            if splits(chunks[c]):
                z_copy(c, 1, 1).start()
            z_copy(c, 0, 2).wait_recv()
            y_copy(c, 1, 2).start()
            c_copy(c, 1).start()
            c_copy(c, 2).start()
        else:
            y_copy(c, 1, 3).wait_recv()
            if splits(chunks[c]):
                z_copy(c, 1, 3).wait_recv()
            c_copy(c, 3).start()

    n_copies = [remote(own[a], nears[a], n_s.at[a], n_r.at[a], (group, near)) for a in range(3)]
    u_copies = [remote(ubs.at[0], ubs.at[g], u_s.at[g - 1], u_r.at[g - 1], (group, d)) for g, d in ((1, near), (2, far), (3, cross))]
    loads = [pltpu.make_async_copy(w, wt.at[pl.ds(box + n * cols, cols)], l_s.at[n]) for n, w in enumerate((wq_any, wk_any, wv_any))]
    keep_wt = pltpu.make_async_copy(wt, wt_any, l_s.at[3])

    @pl.when(i == 0)
    def _():
        for c in loads:
            c.start()
        ubs[0] = row(ub_ref)
        barrier = pltpu.get_barrier_semaphore()
        peers = [(group, near), (group, far), (group, cross), (beside, place), (above, place)]
        for device in peers:
            pl.semaphore_signal(barrier, inc=1, device_id=device, device_id_type=MESH)
        pl.semaphore_wait(barrier, len(peers))
        for c in range(len(chunks)):
            x_copy(c).start()
        for n in n_copies:
            n.start()
        for u in u_copies:
            u.start()
        wt[:box, :] = wb_ref[...].T
        for c in loads:
            c.wait()
        keep_wt.start()

    length = len_ref[page_of(i, pages)]
    geo = geometry_of(coords_ref[...], rates_ref[...])
    geo_ref[...] = geo
    proj = mm_nt(h_ref[...], wt[...])
    q_ref[...] = (proj[:, box : box + cols] + row(qb_ref)).astype(BF)
    k_ref[...] = proj[:, box + cols : box + 2 * cols].astype(BF)
    v_ref[...] = (proj[:, box + 2 * cols :] + row(vb_ref)).astype(BF)
    co, si = mixing(geo.astype(F32))
    bias = row(bb_ref)
    for head in range(heads):
        wide = slice(head * POS, (head + 1) * POS)
        lanes = slice(head * HEAD, (head + 1) * HEAD)
        cat_q[head, :, :POS] = mix(proj[:, wide] + bias[:, wide], co, si).astype(BF)
        cat_q[head, :, POS:] = q_ref[:, lanes]
        cat_k[head, :, :POS] = geo
        cat_k[head, :, POS:] = k_ref[:, lanes]
    count = 2 * pages
    plan = {1: [(0, 0)], 3: [(0, 1), (0, 2), (1, 0)], 5: [(0, 3), (0, 4), (1, 1)], 7: [(1, 2)], 9: [(1, 3), (1, 4), (2, 0), (2, 1)], 11: [(2, 2), (2, 3), (2, 4)]}

    def tick(odd):
        for at, todo in plan.items():
            if at % 2 == odd:

                @pl.when(i == at // 2)
                def _():
                    for n, c in todo:
                        stage(n, c)

    valid = lax.broadcasted_iota(jnp.int32, (PAGE, 1), 0) < length
    scale = LOG2E / math.sqrt(HEAD)
    s = mm_nt(cat_k[0], cat_q[0])
    for head in range(heads):
        lanes = slice(head * HEAD, (head + 1) * HEAD)
        now = s
        if head + 1 < heads:
            s = mm_nt(cat_k[head + 1], cat_q[head + 1])
        now = jnp.where(valid, now, -1e30)
        top = jnp.max(now, axis=0, keepdims=True)
        e = jnp.exp2((now - top) * scale)
        total = jnp.sum(e, axis=0, keepdims=True)
        p = (e * (1.0 / total)).astype(BF)
        p_ref[head] = p
        c = mm_tn(p, v_ref[:, lanes]).astype(BF)
        for k in range(2):
            cpage[2 * i + k, :, lanes] = c[k * HALF : (k + 1) * HALF]
        if head == heads // 2:
            tick(0)
    for k in range(2):
        piece = 2 * lax.rem(i, pages) + k
        oc = piece // pages
        slot = lax.rem(piece, pages)
        mine = oc == core

        @pl.when(i < pages)
        def _():
            g = jnp.where(mine, 2, 3)
            remote(cpage.at[2 * i + k], ctx_any.at[g, slot], t_s.at[2 * i + k], t_r.at[g, slot], (group, 2 * (1 - chip) + oc)).start()

        @pl.when((i >= pages) & jnp.logical_not(mine))
        def _():
            remote(cpage.at[2 * i + k], ctx_any.at[1, slot], t_s.at[2 * i + k], t_r.at[1, slot], (group, near)).start()

        @pl.when((i >= pages) & mine)
        def _():
            pltpu.make_async_copy(cpage.at[2 * i + k], ctx_any.at[0, slot], t_r.at[0, slot]).start()

    tick(1)

    @pl.when(i == count - 1)
    def _():
        keep_wt.wait()
        for u in u_copies:
            u.wait()
        keep_ub = pltpu.make_async_copy(ubs, ua_any, u_s.at[3])
        keep_ub.start()
        for n in n_copies:
            n.wait()
        keep_ub.wait()
        for slot in range(pages):
            for g in range(4):
                arrived(ctx_any.at[g, slot], t_r.at[g, slot])
        for j in range(2 * count):
            if j < count:
                arrived(cpage.at[j], t_s.at[j])
            else:

                @pl.when((j - count) // pages != core)
                def _():
                    arrived(cpage.at[j], t_s.at[j])

        for c in range(len(chunks)):
            x_copy(c).wait_send()
            for step in range(2):
                y_copy(c, step, 2 * step).wait_send()
                if step == 0 or splits(chunks[c]):
                    z_copy(c, step, step).wait_send()
            for k in range(4):
                c_copy(c, k).wait()


def run_forward(lengths, rates, hidden, coords, wb, qb, vb, bb, ub, wq, wk, wv, wo, wu, wd):
    cols, d = wq.shape
    heads = cols // HEAD
    pages = lengths.shape[0] // 2
    wide = wb.shape[1] + 3 * cols
    own = (wo, wu, wd)
    n = len(weight_chunks(own))
    page_out = lambda w: pl.BlockSpec((PAGE, w), lambda i: (i, 0))
    rows = 2 * pages * PAGE
    return pl.pallas_call(
        partial(forward_kernel, pages=pages),
        out_shape=[S((rows, cols), BF)] * 3
        + [S((rows, POS), BF), S((2 * pages, heads, PAGE, PAGE), BF), S((4, pages, HALF, cols), BF), S((wide, d), BF), S((4, 1, ub.shape[0]), F32)]
        + [S(x.shape, BF) for x in own] * 3,
        grid=(2 * pages,),
        in_specs=[
            pl.BlockSpec(memory_space=pltpu.SMEM),
            WHOLE,
            pl.BlockSpec((PAGE, d), lambda i: (page_of(i, pages), 0)),
            pl.BlockSpec((4, PAGE), lambda i: (0, page_of(i, pages))),
        ]
        + [WHOLE] * 5
        + [ANY] * 6,
        out_specs=[page_out(cols)] * 3
        + [page_out(POS), pl.BlockSpec((pl.Squeezed(), heads, PAGE, PAGE), lambda i: (i, 0, 0, 0))]
        + [ANY] * 12,
        scratch_shapes=[V((wide, d), BF), V((heads, PAGE, POS + HEAD), BF), V((heads, PAGE, POS + HEAD), BF), V((4 * pages, HALF, cols), BF), V((4, 1, ub.shape[0]), F32)]
        + [D((4,)), D((n,)), D((n,)), D((2, n)), D((2, n)), D((2, n)), D((2, n)), D((3,)), D((3,)), D((4, n)), D((4, n)), D((4,)), D((3,)), D((4 * pages,)), D((4, pages))],
        compiler_params=pltpu.CompilerParams(vmem_limit_bytes=56 << 20, collective_id=0, has_side_effects=True),
        name="forward",
    )(lengths, rates, hidden, coords, wb, qb, vb, bb, ub, wq, wk, wv, wo, wu, wd)


def middle_kernel(hid_any, og_any, ctx_any, w0, w1, w2, w3, w4, w5, w6, w7, w8, w9, w10, w11, ub_ref, ob_ref, g1_ref, s1_ref, db_ref, g2_ref, s2_ref,
                  out_any, act_any, ug_any, fl_any, sl_any, scaled_any, second_any, inv_ref, vg_ref,
                  hid, og, ctx, wo, wu, wd, act, ug, fl, sl, lo, first, scaled1, second2, ffn, sem_in, sem_w, sem_out, *, tile):
    rows, d = og.shape
    groups = wu.shape[0]
    weights = (w0, w1, w2, w3, w4, w5, w6, w7, w8, w9, w10, w11)
    place = lax.axis_index("tensor")
    head_loads = [
        pltpu.make_async_copy(ctx_any, ctx, sem_in.at[0]),
        pltpu.make_async_copy(hid_any.at[pl.ds(place * rows, rows)], hid, sem_in.at[1]),
        pltpu.make_async_copy(og_any, og, sem_in.at[2]),
    ]
    loads = [[pltpu.make_async_copy(weights[3 * g + k], (wo, wu, wd)[k].at[g], sem_w.at[k, g]) for g in range(groups)] for k in range(3)]
    head_loads[0].start()
    for c in loads[0]:
        c.start()
    head_loads[1].start()
    for g in range(groups):
        loads[1][g].start()
        loads[2][g].start()
    head_loads[2].start()
    head_loads[0].wait()
    for c in loads[0]:
        c.wait()
    head_loads[1].wait()
    vg_ref[...] = jnp.zeros_like(vg_ref)
    for g in range(groups):
        loads[1][g].wait()
        loads[2][g].wait()
    head_loads[2].wait()
    steps = rows // tile

    def stores(i):
        r = pl.ds(pl.multiple_of(i * tile, tile), tile)
        pairs = ((act.at[:, r], act_any.at[:, r]), (ug.at[:, r], ug_any.at[:, r]), (fl.at[r], fl_any.at[r]), (sl.at[r], sl_any.at[r]),
                 (lo.at[r], out_any.at[r]), (scaled1.at[r], scaled_any.at[r]), (second2.at[r], second_any.at[r]))
        return [pltpu.make_async_copy(a, b, sem_out.at[n, i]) for n, (a, b) in enumerate(pairs)]

    def step(i, _):
        r = pl.ds(pl.multiple_of(i * tile, tile), tile)
        attn = mm(ctx[0, r], wo[0])
        for g in range(1, groups):
            attn = attn + mm(ctx[g, r], wo[g])
        scaled, inverse = normal(attn + row(ob_ref) + hid[r].astype(F32))
        f = scaled * row(g1_ref) + row(s1_ref)
        first[...] = f
        scaled1[r] = scaled
        inv_ref[r] = inverse
        fl[r] = f.astype(BF)
        x = mm(fl[r], wu[0])
        for g in range(groups):
            now = x + ub_ref[g]
            if g + 1 < groups:
                x = mm(fl[r], wu[g + 1])
            half = 0.5 + 0.5 * lax.erf(now * 0.7071067811865476)
            a = (now * half).astype(BF)
            act[g, r] = a
            ug[g, r] = (half + now * jnp.exp(-0.5 * now * now) * 0.3989422804014327).astype(BF)
            part = mm(a, wd[g])
            if g == 0:
                ffn[...] = part
            else:
                ffn[...] += part

        scaled, inverse = normal(ffn[...] + row(db_ref) + first[...])
        lo[r] = (scaled * row(g2_ref) + row(s2_ref)).astype(BF)

        o = og[r].astype(F32)
        second = normal_back(o * row(g2_ref), scaled, inverse)
        vg_ref[3:4, :] += columns(second)
        vg_ref[4:5, :] += columns(o * scaled)
        vg_ref[5:6, :] += columns(o)
        sl[r] = second.astype(BF)
        second2[r] = second
        for c in stores(i):
            c.start()
        return 0

    lax.fori_loop(0, steps, step, 0)
    for i in range(steps):
        for c in stores(i):
            c.wait()


def run_middle(hidden, og, ctx, weights, ub, vectors, tile):
    rows, d = og.shape
    groups = 4
    q = weights[0].shape[0]
    f = weights[1].shape[1]
    return pl.pallas_call(
        partial(middle_kernel, tile=tile),
        out_shape=[S((rows, d), BF), S((groups, rows, f), BF), S((groups, rows, f), BF), S((rows, d), BF), S((rows, d), BF), S((rows, d), F32), S((rows, d), F32), S((rows, 1), F32), S((8, d), F32)],
        in_specs=[ANY] * 15 + [WHOLE] * 7,
        out_specs=[ANY] * 7 + [WHOLE] * 2,
        scratch_shapes=[
            V((rows, d), BF), V((rows, d), BF), V((groups, rows, q), BF), V((groups, q, d), BF), V((groups, d, f), BF), V((groups, f, d), BF),
            V((groups, rows, f), BF), V((groups, rows, f), BF), V((rows, d), BF), V((rows, d), BF), V((rows, d), BF),
            V((tile, d), F32), V((rows, d), F32), V((rows, d), F32), V((tile, d), F32),
            D((3,)), D((3, groups)), D((7, rows // tile)),
        ],
        compiler_params=pltpu.CompilerParams(vmem_limit_bytes=62 << 20),
        name="middle",
    )(hidden, og, ctx, *weights, ub, *vectors)


class Cube:
    def __init__(self, main, recv, out, sems, group, place, rows, levels):
        self.main, self.recv, self.out, self.sems = main, recv, out, sems
        self.group, self.place, self.rows, self.levels = group, place, rows, levels
        self.steps = 2 * levels - 1
        self.sides = [lax.rem(group // 2**n, 2) for n in range(levels)]
        self.mates = [group + 2**n * (1 - 2 * side) for n, side in enumerate(self.sides)]

    def pick(self, j, s, values):
        if s > 1:
            return values[s]
        return jnp.where((j & 3) == 3, values[1 - s], values[s])

    def side(self, j, s):
        return self.pick(j, s, self.sides)

    def partner(self, j, s):
        return (self.pick(j, s, self.mates), self.place)

    def got(self, n, sem, j, s):
        arrived(self.recv.at[pl.ds(0, n)], self.sems.at[sem, j, s])

    def low(self, j, s):
        at = j * self.rows
        for t in range(s):
            at = at + self.side(j, t) * (self.rows >> (t + 1))
        return at

    def span(self, start, n):
        return pl.ds(pl.multiple_of(start, 16), n)

    def r_copy(self, j, s):
        n = self.rows >> (s + 1)
        src = self.main.at[self.span(self.low(j, s) + (1 - self.side(j, s)) * n, n)]
        dst = self.recv.at[self.span(j * self.rows + self.rows - (self.rows >> s), n)]
        return remote(src, dst, self.sems.at[0, j, s], self.sems.at[1, j, s], self.partner(j, s))

    def g_copy(self, j, s):
        here = self.span(self.low(j, s + 1), self.rows >> (s + 1))
        src = self.main if s == self.levels - 1 else self.out
        return remote(src.at[here], self.out.at[here], self.sems.at[2, j, s], self.sems.at[3, j, s], self.partner(j, s))

    def keep(self, j):
        here = self.span(self.low(j, self.levels), self.rows >> self.levels)
        return pltpu.make_async_copy(self.main.at[here], self.out.at[here], self.sems.at[0, j, self.levels])

    def start(self, j):
        self.r_copy(j, 0).start()

    def step(self, k, j):
        last = self.levels - 1
        if k <= last:
            n = self.rows >> (k + 1)
            self.got(n, 1, j, k)
            mine = self.span(self.low(j, k + 1), n)
            got = self.span(j * self.rows + self.rows - (self.rows >> k), n)
            self.main[mine] = self.main[mine] + self.recv[got]
            if k < last:
                self.r_copy(j, k + 1).start()
            else:
                self.keep(j).start()
                self.g_copy(j, last).start()
        else:
            s = 2 * self.levels - 2 - k
            self.got(self.rows >> (s + 2), 3, j, s + 1)
            if s + 1 == last:
                self.got(self.rows >> self.levels, 0, j, self.levels)
            self.g_copy(j, s).start()

    def finish(self, j):
        self.got(self.rows >> 1, 3, j, 0)
        for s in range(self.levels):
            self.got(self.rows >> (s + 1), 0, j, s)
            self.got(self.rows >> (s + 1), 2, j, s)


SLOTS = 3


def backward_kernel(h_ref, wt_ref, q_ref, k_ref, v_ref, geo_ref, p_ref, inv_ref, vgin_ref, g1_ref,
                    act_any, ug_any, fl_any, sl_any, scaled_any, second_any, ctx_any,
                    o0, u0, n0, o1, u1, n1, o2, u2, n2, o3, u3, n3,
                    fin_any, afin_any, ig_any,
                    act, ug, wd, wo, fl, sl, al, ctx, cs, crecv, gx, xrecv, main, mrecv, amain, arecv, dsrc, dc, dcp, total, btotal, mixed, drecv, dxrecv, ag, acc, vg, ubg,
                    l_sem, w_sem, c_s, c_r, free, x_s, x_r, r_sem, a_sem, e_s, e_r, d_s, d_r, f_s, f_r, o_sem, *, pages, ways, blocks, per, arows):
    i = pl.program_id(0)
    count = 2 * pages
    group, place, core, chip, near, far, cross = seats()
    cols = q_ref.shape[1]
    heads = cols // HEAD
    box = heads * POS
    d = h_ref.shape[1]
    levels = ways.bit_length() - 1
    f = act.shape[2]
    qc = ctx.shape[2]
    downs = f // BLOCK
    ups = downs + d // BLOCK
    chunks = blocks // per
    achunks = amain.shape[0] // arows
    ffn = Cube(main, mrecv, fin_any, r_sem, group, place, per * BLOCK, levels)
    att = Cube(amain, arecv, afin_any, a_sem, group, place, arows, levels)
    second = total.at[pl.ds(0, pages * BLOCK), :]
    loads = [pltpu.make_async_copy(a, b, l_sem.at[n]) for n, (a, b) in enumerate(((sl_any, sl), (fl_any, fl), (ug_any, ug), (scaled_any, ag), (second_any, second), (ctx_any, ctx)))]
    act_loads = [pltpu.make_async_copy(act_any.at[g], act.at[g], w_sem.at[3, g]) for g in range(4)]
    wo_loads = [pltpu.make_async_copy(a, wo.at[g], w_sem.at[0, g]) for g, a in enumerate((o0, o1, o2, o3))]
    wu_loads = [pltpu.make_async_copy(a, act.at[g], w_sem.at[1, g]) for g, a in enumerate((u0, u1, u2, u3))]
    wd_loads = [pltpu.make_async_copy(a, wd.at[g], w_sem.at[2, g]) for g, a in enumerate((n0, n1, n2, n3))]
    spare = lambda which, slot: wd.at[which, pl.ds(slot * HALF, HALF)]

    def e_copy(g, slot):
        return remote(dsrc.at[g - 1, slot], dc.at[g, slot], e_s.at[g - 1, slot], e_r.at[g - 1, slot], (group, (near, far, cross)[g - 1]))

    def c_copy(b):
        return remote(cs.at[lax.rem(b, 2)], crecv.at[lax.rem(b, SLOTS)], c_s.at[b], c_r.at[b], (group, near))

    def x_copy(b):
        return remote(gx.at[b], xrecv.at[b], x_s.at[b], x_r.at[b], (group, far))

    def span(b):
        return pl.ds(pl.multiple_of(b * BLOCK, BLOCK), BLOCK)

    def plus(a, b):
        return a + b

    def put(b, g, value):
        value = value.astype(BF)
        if g == 0:
            main[span(b)] = value
        elif g == 2:
            gx[b] = value
        else:
            cs[lax.rem(b, 2), g // 2] = value

    def c_add(b):
        c_copy(b).wait_recv()
        slot = lax.rem(b, SLOTS)

        main[span(b)] = plus(main[span(b)], crecv[slot, 0])
        gx[b] = plus(gx[b], crecv[slot, 1])
        x_copy(b).start()

        @pl.when(b + SLOTS < blocks)
        def _():
            pl.semaphore_signal(free, inc=1, device_id=(group, near), device_id_type=MESH)

    def block(b, kind):
        @pl.when(b >= 2)
        def _():
            c_copy(b - 2).wait_send()

        if kind == "down":
            r = pl.ds(pl.multiple_of(b * BLOCK, BLOCK), BLOCK)
            for g in range(4):

                @pl.when(b == 0)
                def _():
                    act_loads[g].wait()

                put(b, g, mm_tn(act[g, :, r], sl[...]))
        elif kind == "up":
            r = pl.ds(pl.multiple_of((b - downs) * BLOCK, BLOCK), BLOCK)
            for g in range(4):
                put(b, g, mm_tn(fl[:, r], ug[g]))
        elif kind == "out":
            width = d // 4
            for g, place_g in enumerate((place, near, far, cross)):
                norms = vg[0:6, :width]
                for a in range(1, 4):
                    norms = jnp.where(place_g == a, vg[0:6, a * width : (a + 1) * width], norms)
                norms = jnp.concatenate([norms, jnp.zeros((6, d - width), F32)], axis=1)
                extra = jnp.concatenate([ubg[g, 0:1, :], norms, jnp.zeros((BLOCK - qc - 7, d), F32)], axis=0)
                put(b, g, jnp.concatenate([mm_tn(ctx[g], al[...]), extra], axis=0))
        else:
            for g in range(4):
                put(b, g, jnp.zeros((BLOCK, d), F32))

        @pl.when(b >= SLOTS)
        def _():
            pl.semaphore_wait(free, 1)

        c_copy(b).start()

    def x_add(b):
        x_copy(b).wait_recv()

        main[span(b)] = plus(main[span(b)], xrecv[b])

        @pl.when(lax.rem(b + 1, per) == 0)
        def _():
            ffn.start(b // per)

    def tick(u, low, high=blocks):
        half = u // 2
        odd = lax.rem(u, 2)
        if high == blocks:

            @pl.when((odd == 0) & (half >= low) & (half < high))
            def _():
                x_add(half)

        for k in range(ffn.steps):
            b = (u - k - 1) // 2

            @pl.when((lax.rem(u + k, 2) == 1) & (u > k) & (b >= low) & (b < high) & (lax.rem(b + 1, per) == 0))
            def _():
                ffn.step(k, b // per)

    @pl.when(i == 0)
    def _():
        loads[0].start()
        for c in act_loads:
            c.start()
        peers = [(group, near), (group, far), (group, cross)]
        peers += [(group + 2**n * (1 - 2 * lax.rem(group // 2**n, 2)), place) for n in range(levels)]
        barrier = pltpu.get_barrier_semaphore()
        for device in peers:
            pl.semaphore_signal(barrier, inc=1, device_id=device, device_id_type=MESH)

        for c in wd_loads:
            c.start()
        loads[2].start()
        loads[4].start()
        loads[3].start()
        for c in wo_loads:
            c.start()
        loads[1].start()
        loads[5].start()
        pl.semaphore_wait(barrier, len(peers))
        loads[0].wait()

        def down_block(b, _):
            block(b, "down")

            @pl.when(b >= 1)
            def _():
                c_add(b - 1)

            return 0

        lax.fori_loop(0, downs, down_block, 0)
        for c in wu_loads:
            c.start()
        for c in wd_loads:
            c.wait()
        for n in (2, 3, 4):
            loads[n].wait()
        c_add(downs - 1)
        for c in wo_loads:
            c.wait()
        vg[...] = vgin_ref[...]
        ubg[...] = jnp.zeros_like(ubg)

        def tile(t, _):
            r = pl.ds(pl.multiple_of(t * BLOCK, BLOCK), BLOCK)
            acc[...] = total[r, :]
            for g in range(4):
                u = (mm_nt(sl[r], wd[g]) * ug[g, r].astype(F32)).astype(BF)
                ug[g, r] = u
                ubg[g, 0:1, :] += columns(u.astype(F32))

                @pl.when(t == 0)
                def _():
                    wu_loads[g].wait()

                acc[...] += mm_nt(u, act[g])

            @pl.when(t == 1)
            def _():
                tick(0, 0)

            fg = acc[...]
            scaled = ag[r]
            a = normal_back(fg * row(g1_ref), scaled, inv_ref[r])
            vg[0:1, :] += columns(a)
            vg[1:2, :] += columns(fg * scaled)
            vg[2:3, :] += columns(fg)
            ag[r] = a
            low = a.astype(BF)
            al[r] = low
            for g in (2, 3, 1, 0):
                value = mm_nt(low, wo[g]).astype(BF)
                if g == 0:
                    dc[0, t] = value
                else:
                    dsrc[g - 1, t] = value
                    e_copy(g, t).start()

            @pl.when(t == 2)
            def _():
                tick(1, 0)

            return 0

        lax.fori_loop(0, pages, tile, 0)

        def up_block(b, _):
            block(b, "up")

            @pl.when(b > downs)
            def _():
                c_add(b - 1)

            @pl.when(b == downs + 1)
            def _():
                tick(2, 0)

            return 0

        for n in (1, 5):
            loads[n].wait()
        lax.fori_loop(downs, ups, up_block, 0)
        block(ups, "out")
        c_add(ups - 1)
        for b in range(ups + 1, blocks):
            block(b, "zero")
            c_add(b - 1)
        c_add(blocks - 1)
        for b in (blocks - 2, blocks - 1):
            c_copy(b).wait_send()
        total[...] = jnp.zeros_like(total)
        btotal[...] = jnp.zeros_like(btotal)
        tick(3, 0)
        for slot in range(pages):
            e_copy(1, slot).wait_recv()

    @pl.when(i == pages)
    def _():
        for g in (2, 3):
            for slot in range(pages):
                e_copy(g, slot).wait_recv()

    for k in range(2):
        piece = 2 * lax.rem(i, pages) + k
        g = jnp.where(piece // pages == core, 0, 1) + jnp.where(i < pages, 0, 2)
        dcp[k * HALF : (k + 1) * HALF, :] = dc[g, lax.rem(piece, pages)]
    geo = geo_ref[...]
    co, si = mixing(geo.astype(F32))
    factor = 1.0 / math.sqrt(HEAD)
    lanes = [slice(head * HEAD, (head + 1) * HEAD) for head in range(heads)]
    dp = mm_nt(v_ref[:, lanes[0]], dcp[:, lanes[0]])
    for head in range(heads):
        now = dp
        if head + 1 < heads:
            dp = mm_nt(v_ref[:, lanes[head + 1]], dcp[:, lanes[head + 1]])
        p = p_ref[head]
        mixed[:, box + 2 * cols + head * HEAD : box + 2 * cols + (head + 1) * HEAD] = mm(p, dcp[:, lanes[head]]).astype(BF)
        pf = p.astype(F32)
        delta = jnp.sum(pf * now, axis=0, keepdims=True)
        ds = (pf * (now - delta)).astype(BF)
        both = mm_tn(ds, jnp.concatenate([geo, k_ref[:, lanes[head]]], axis=1)) * factor
        mixed[:, box + head * HEAD : box + (head + 1) * HEAD] = both[:, POS:].astype(BF)
        mixed[:, head * POS : (head + 1) * POS] = mix(both[:, :POS], co, si).astype(BF)
        mixed[:, box + cols + head * HEAD : box + cols + (head + 1) * HEAD] = (mm(ds, q_ref[:, lanes[head]]) * factor).astype(BF)

    total[...] += mm_tn(mixed[...], h_ref[...])
    btotal[0:1, :] += columns(mixed[...].astype(F32))

    def d_copy(kind, slot):
        return remote(spare(2 + kind, slot), drecv.at[kind, slot], d_s.at[kind, slot], d_r.at[kind, slot], (group, near))

    def f_copy(slot):
        return remote(spare(0, slot), dxrecv.at[slot], f_s.at[slot], f_r.at[slot], (group, far))

    kind = jnp.where(i < pages, 1, 0)
    dx = mm(mixed[...], wt_ref[...]).astype(BF)
    for k in range(2):
        piece = 2 * lax.rem(i, pages) + k
        slot = lax.rem(piece, pages)
        value = dx[k * HALF : (k + 1) * HALF]
        mine = piece // pages == core
        r = pl.ds(pl.multiple_of(slot * HALF, HALF), HALF)

        @pl.when(mine)
        def _():
            wd[kind, r] = value

        @pl.when(jnp.logical_not(mine))
        def _():
            wd[2 + kind, r] = value
            remote(wd.at[2 + kind, r], drecv.at[kind, slot], d_s.at[kind, slot], d_r.at[kind, slot], (group, near)).start()

    @pl.when(i < 2)
    def _():
        tick(4 + i, 0)

    @pl.when(i >= 1)
    def _():
        tick(5 + i, 0)

    @pl.when(i == count - 1)
    def _():
        bias = btotal[0:1, :]
        bias = jnp.concatenate([bias[:, : box + cols], bias[:, box + 2 * cols :]], axis=1)
        wide = total.shape[0]
        for b in range(0, wide, 64):
            amain[b : b + 64, :] = total[b : b + 64, :].astype(BF)
        ending = jnp.where(lax.broadcasted_iota(jnp.int32, (amain.shape[0] - wide, d), 0) == 0, bias, 0.0)
        amain[wide:, :] = ending.astype(BF)
        for j in range(achunks):
            att.start(j)
        for slot in range(pages):
            d_copy(0, slot).wait_recv()
            here = spare(0, slot)
            here[...] = plus(here[...], drecv[0, slot])
            f_copy(slot).start()
        first = 5 + count
        when = [0, 4, 7, 9, 11, 13]
        ticks = 2 * (blocks - 1) + ffn.steps - first + 1
        when += list(range(14, 14 + ticks - len(when)))
        waves = max(achunks + 2 * (att.steps - 1), when[-1] + 1)

        outs = [pltpu.make_async_copy(ag.at[pl.ds(slot * HALF, HALF)], ig_any.at[pl.ds(slot * HALF, HALF)], o_sem.at[slot]) for slot in range(pages)]

        def wave(w, _):
            @pl.when(w == 8)
            def _():
                for slot in range(pages):
                    r = pl.ds(slot * HALF, HALF)
                    d_copy(1, slot).wait_recv()
                    f_copy(slot).wait_recv()
                    ag[r] = ag[r] + wd[1, r].astype(F32) + drecv[1, slot].astype(F32) + dxrecv[slot].astype(F32)
                    outs[slot].start()

            u = -100
            for n in range(ticks):
                u = jnp.where(w == when[n], first + n, u)
            tick(u, 0)
            for k in range(att.steps):

                @pl.when((w >= 2 * k) & (w - 2 * k < achunks))
                def _():
                    att.step(k, w - 2 * k)

            return 0

        lax.fori_loop(0, waves, wave, 0)
        for slot in range(pages):
            outs[slot].wait()
            f_copy(slot).wait_send()
            d_copy(0, slot).wait_send()
            d_copy(1, slot).wait_send()
            for g in (1, 2, 3):
                e_copy(g, slot).wait_send()
        lax.fori_loop(0, achunks, lambda j, _: (att.finish(j), 0)[1], 0)
        lax.fori_loop(0, chunks, lambda j, _: (ffn.finish(j), 0)[1], 0)
        lax.fori_loop(0, blocks, lambda b, _: (x_copy(b).wait_send(), 0)[1], 0)


def run_backward(hidden, wt, q, k, v, geo, p, inv, vg, g1, act, ug, fl, sl, scaled, second, ctx, weights):
    count, heads = p.shape[:2]
    pages = count // 2
    cols = q.shape[1]
    wide, d = wt.shape
    f = act.shape[2]
    rows = fl.shape[0]
    ways = lax.axis_size("dp")
    levels = ways.bit_length() - 1
    chunk = max(BLOCK, 16 * ways)
    per = chunk // BLOCK
    blocks = -(-((f + d) // BLOCK + 1) // per) * per
    chunks = blocks // per
    arows = 16 * ways
    achunks = -(-(wide + 1) // arows)
    turn = lambda i: lax.rem(i + pages, count)
    page = lambda n: pl.BlockSpec((PAGE, n), lambda i: (turn(i), 0))
    once = lambda a: pl.BlockSpec(a.shape, lambda i: (0,) * len(a.shape), pipeline_mode=pl.Buffered(1))
    return pl.pallas_call(
        partial(backward_kernel, pages=pages, ways=ways, blocks=blocks, per=per, arows=arows),
        out_shape=[S((blocks * BLOCK, d), BF), S((achunks * arows, d), BF), S((rows, d), F32)],
        grid=(count,),
        in_specs=[
            pl.BlockSpec((PAGE, d), lambda i: (page_of(turn(i), pages), 0)),
            once(wt), page(cols), page(cols), page(cols), page(POS),
            pl.BlockSpec((pl.Squeezed(), heads, PAGE, PAGE), lambda i: (turn(i), 0, 0, 0)),
            once(inv), once(vg), WHOLE,
        ]
        + [ANY] * 19,
        out_specs=[ANY] * 3,
        scratch_shapes=[
            V(act.shape, BF), V(ug.shape, BF), V((4, f, d), BF), V((4, cols, d), BF), V(fl.shape, BF), V(sl.shape, BF), V(fl.shape, BF), V(ctx.shape, BF),
            V((2, 2, BLOCK, d), BF), V((SLOTS, 2, BLOCK, d), BF), V((blocks, BLOCK, d), BF), V((blocks, BLOCK, d), BF),
            V((blocks * BLOCK, d), BF), V((blocks * BLOCK, d), BF), V((achunks * arows, d), BF), V((achunks * arows, d), BF),
            V((3, pages, HALF, cols), BF), V((4, pages, HALF, cols), BF), V((PAGE, cols), BF), V((wide, d), F32), V((8, wide), F32), V((PAGE, wide), BF),
            V((2, pages, HALF, d), BF), V((pages, HALF, d), BF), V((rows, d), F32), V((BLOCK, d), F32), V((8, d), F32), V((4, 8, f), F32),
            D((6,)), D((4, 4)), D((blocks,)), D((blocks,)), pltpu.SemaphoreType.REGULAR, D((blocks,)), D((blocks,)), D((4, chunks, levels + 1)), D((4, achunks, levels + 1)),
            D((3, pages)), D((3, pages)), D((2, pages)), D((2, pages)), D((pages,)), D((pages,)), D((pages,)),
        ],
        compiler_params=pltpu.CompilerParams(vmem_limit_bytes=67043328, collective_id=1, has_side_effects=True),
        name="backward",
    )(hidden, wt, q, k, v, geo, p, inv, vg, g1, act, ug, fl, sl, scaled, second, ctx, *weights)


def finish_kernel(fin_any, afin_any, grad_any, down_any, up_any, out_any, q_any, k_any, v_any, box_any, ig_any,
                  ub_ref, qb_ref, vb_ref, bb_ref, n0_ref, n1_ref, n2_ref, n3_ref, n4_ref, n5_ref,
                  low, alow, full, afull, boxt, grad, l_s, o_s):
    d = low.shape[1]
    cols = q_any.shape[0]
    box = box_any.shape[1]
    wide = box + 3 * cols
    f = down_any.shape[0]
    up = up_any.shape[0]
    rows = f + up + cols
    pieces = [(low, fin_any, full, a, BLOCK, (down_any if a < f else up_any), a % f) for a in range(0, f + up, BLOCK)]
    pieces += [(low, fin_any, full, f + up, cols + 16, out_any, 0)]
    pieces += [(alow, afin_any, afull, a, min(cols, wide + 16 - a), None, 0) for a in range(0, box, cols)]
    pieces += [(alow, afin_any, afull, box + n * cols, cols + (16 if n == 2 else 0), x, 0) for n, x in enumerate((q_any, k_any, v_any))]
    loads = [pltpu.make_async_copy(src.at[pl.ds(a, n)], buf.at[pl.ds(a, n)], l_s.at[j]) for j, (buf, src, _, a, n, _, _) in enumerate(pieces)]
    order = list(range(len(pieces) - 3 - box // cols, len(pieces))) + list(range(len(pieces) - 3 - box // cols))
    for j in order:
        loads[j].start()
    grad_in = pltpu.make_async_copy(grad_any, grad, l_s.at[len(pieces)])
    grad_out = pltpu.make_async_copy(grad, ig_any, o_s.at[len(pieces)])
    grad_in.start()
    stores = []
    for j in order:
        buf, _, wide_buf, a, n, dst, to = pieces[j]
        loads[j].wait()
        wide_buf[a : a + n, :] = buf[a : a + n, :].astype(F32)
        if dst is not None:
            n = min(n, dst.shape[0])
            c = pltpu.make_async_copy(wide_buf.at[pl.ds(a, n)], dst.at[pl.ds(to, n)], o_s.at[len(stores)])
            c.start()
            stores.append(c)
        elif a + n == box:
            boxt[...] = afull[:box, :].T
            c = pltpu.make_async_copy(boxt, box_any, o_s.at[len(stores)])
            c.start()
            stores.append(c)
    grad_in.wait()
    grad_out.start()
    stores.append(grad_out)
    tail = full[rows : rows + 8, :]
    ub_ref[...] = tail[0]
    width = d // 4
    for n, ref in enumerate((n0_ref, n1_ref, n2_ref, n3_ref, n4_ref, n5_ref)):
        ref[...] = tail[1 + n, :width]
    bias = afull[wide : wide + 8, :][0]
    bb_ref[...] = bias[:box]
    qb_ref[...] = bias[box : box + cols]
    vb_ref[...] = bias[box + cols : box + 2 * cols]
    for c in stores:
        c.wait()


def run_finish(fin, afin, grad, f, up, cols, box):
    d = fin.shape[1]
    rows = f + up + cols + 16
    wide = box + 3 * cols + 16
    width = d // 4
    vectors = [S((f,), F32), S((cols,), F32), S((cols,), F32), S((box,), F32)] + [S((width,), F32)] * 6
    n = (f + up) // BLOCK + 5 + box // cols
    return pl.pallas_call(
        finish_kernel,
        out_shape=[S((f, d), F32), S((up, d), F32), S((cols, d), F32)] + [S((cols, d), F32)] * 3 + [S((d, box), F32), S(grad.shape, F32)] + vectors,
        in_specs=[ANY] * 3,
        out_specs=[ANY] * 8 + [WHOLE] * 10,
        scratch_shapes=[V((rows, d), BF), V((wide, d), BF), V((rows, d), F32), V((wide, d), F32), V((d, box), F32), V(grad.shape, F32), D((n,)), D((n,))],
        compiler_params=pltpu.CompilerParams(vmem_limit_bytes=62 << 20),
        name="finish",
    )(fin, afin, grad)


def body(
    hidden_in, box_coords, page_lengths, query_weight, query_bias, key_weight, value_weight, value_bias, box_weight, box_bias, output_weight, output_bias,
    first_gain, first_shift, up_weight, up_bias, down_weight, down_bias, second_gain, second_shift, output_grad,
):
    rates = jnp.power(1000.0, -jnp.arange(FREQ, dtype=F32) / FREQ)
    rates = jnp.tile(rates, POS // FREQ).reshape(1, POS)
    q, k, v, geo, p, ctx, wt, ups, *gathered = run_forward(
        page_lengths, rates, hidden_in, box_coords, box_weight, query_bias, value_bias, box_bias, up_bias,
        query_weight.T, key_weight.T, value_weight.T, output_weight, up_weight, down_weight,
    )
    rows, d = output_grad.shape
    ctx = ctx.reshape(ctx.shape[0], rows, ctx.shape[3])
    weights = (output_weight, up_weight, down_weight, *gathered)
    layer_out, act, ug, fl, sl, scaled, second, inv, vg = run_middle(
        hidden_in, output_grad, ctx, weights, ups, (output_bias, first_gain, first_shift, down_bias, second_gain, second_shift), tile=384 if rows % 384 == 0 else BLOCK
    )
    fin, afin, grad = run_backward(hidden_in, wt, q, k, v, geo, p, inv, vg, first_gain, act, ug, fl, sl, scaled, second, ctx, weights)
    cols = query_weight.shape[1]
    down, up, out, q, k, v, box, input_grad, ub, qb, vb, bb, *norms = run_finish(fin, afin, grad, up_weight.shape[1], d, cols, box_weight.shape[1])
    return (
        layer_out, input_grad, q.T, qb, k.T, v.T, vb, box, bb, out, norms[0], norms[1], norms[2], up, ub, down, norms[3], norms[4], norms[5],
    )


def solution(mesh):
    shared = P()
    by_column = P(None, "tensor")
    by_row = P("tensor", None)
    vector = P("tensor")
    tokens = P(("dp", "tensor"), None)
    in_specs = (
        P("dp", None), P(None, "dp"), P("dp"), by_column, vector, by_column, by_column, vector, by_column, vector, by_row, shared,
        shared, shared, by_column, vector, by_row, shared, shared, shared, tokens,
    )
    out_specs = (
        tokens, tokens, by_column, vector, by_column, by_column, vector, by_column, vector, by_row, vector, vector, vector,
        by_column, vector, by_row, vector, vector, vector,
    )
    return jax.shard_map(body, mesh=mesh, in_specs=in_specs, out_specs=out_specs, check_vma=False)
```

```python
from functools import partial
import math
import jax
import jax.numpy as jnp
import numpy as np
from jax import lax
from jax.experimental import pallas as pl
from jax.experimental.pallas import tpu as pltpu
from jax.sharding import PartitionSpec as P

HEAD = 64
POS = 128
FREQ = 16
PAGE = 512
HALF = PAGE // 2
BLOCK = 256
PART = 192
EPS = 1e-05
LOG2E = 1.4426950408889634
F32 = jnp.float32
BF = jnp.bfloat16
MESH = pl.DeviceIdType.MESH
V = pltpu.VMEM
D = pltpu.SemaphoreType.DMA
S = jax.ShapeDtypeStruct
ANY = pl.BlockSpec(memory_space=pl.ANY)
WHOLE = pl.BlockSpec(memory_space=pltpu.VMEM)


def mm(a, b):
    return jnp.dot(a, b, preferred_element_type=F32)


def mm_nt(a, b):
    return lax.dot_general(a, b, (((1,), (1,)), ((), ())), preferred_element_type=F32)


def mm_tn(a, b):
    return lax.dot_general(a, b, (((0,), (0,)), ((), ())), preferred_element_type=F32)


def columns(x):
    return jnp.sum(x, axis=0, keepdims=True)


def row(ref):
    return ref[...].reshape(1, ref.shape[0])


def normal(z):
    mean = jnp.mean(z, axis=1, keepdims=True)
    centred = z - mean
    inverse = lax.rsqrt(jnp.mean(centred * centred, axis=1, keepdims=True) + EPS)
    return centred * inverse, inverse


def normal_back(inner, scaled, inverse):
    return inverse * (
        inner
        - jnp.mean(inner, axis=1, keepdims=True)
        - scaled * jnp.mean(inner * scaled, axis=1, keepdims=True)
    )


def geometry_of(coords, rates):
    n = coords.shape[1]
    split = jnp.concatenate([coords // 256, coords % 256], axis=0).astype(F32)
    split = jnp.concatenate([split, jnp.zeros_like(split)], axis=0).astype(BF)
    lane = lax.broadcasted_iota(jnp.int32, (16, POS), 1)
    which = lax.broadcasted_iota(jnp.int32, (16, POS), 0)
    spread = jnp.where((lane % (POS // 2)) // FREQ == which % 4, 1.0, 0.0)
    spread = jnp.where(which < 4, 256.0 * spread, spread).astype(BF)
    angle = mm_tn(split, spread) * rates
    turns = jnp.round(angle * 0.6366197723675814)
    r = ((angle - turns * 1.5703125) - turns * 4.837512969970703125e-4) - turns * 7.54978995489188216e-8
    z = r * r
    sine = r + r * z * (-1.6666654611e-1 + z * (8.3321608736e-3 - z * 1.9515295891e-4))
    cosine = 1.0 - 0.5 * z + z * z * (4.166664568298827e-2 + z * (-1.388731625493765e-3 + z * 2.443315711809948e-5))
    quarter = turns.astype(jnp.int32) + jnp.where(lax.broadcasted_iota(jnp.int32, (n, POS), 1) < POS // 2, 1, 0)
    value = jnp.where((quarter & 1) == 1, cosine, sine)
    return jnp.where((quarter & 2) == 2, -value, value).astype(BF)


def mixing(geo):
    half = POS // 2
    c = geo[:, :half]
    s = geo[:, half:]
    return jnp.concatenate([c, -c], axis=1), jnp.concatenate([s, s], axis=1)


def mix(coeff, cos_sign, sin_twice):
    return coeff * cos_sign + pltpu.roll(coeff, POS // 2, 1) * sin_twice


def remote(src, dst, sent, got, device):
    return pltpu.make_async_remote_copy(
        src_ref=src, dst_ref=dst, send_sem=sent, recv_sem=got, device_id=device, device_id_type=MESH
    )


def arrived(ref, sem):
    pltpu.make_async_copy(ref, ref, sem).wait()


def seats():
    group = lax.axis_index("dp")
    place = lax.axis_index("tensor")
    core = lax.rem(place, 2)
    chip = place // 2
    near = place + 1 - 2 * core
    far = place + 2 - 4 * chip
    cross = far + 1 - 2 * core
    return group, place, core, chip, near, far, cross


def page_of(i, pages):
    chip = lax.axis_index("tensor") // 2
    return jnp.where(i < pages, (1 - chip) * pages + i, chip * pages + i - pages)


def weight_chunks(arrays):
    chunks = []
    for a, w in enumerate(arrays):
        n = w.shape[0] // 4
        step = n // 2 if n > PART // 2 else n
        chunks += [(a, s, step) for s in range(0, n, step)]
    return chunks


def splits(chunk):
    return chunk[2] % 32 == 0


def forward_kernel(len_ref, rates_ref, h_ref, coords_ref, wb_ref, qb_ref, vb_ref, bb_ref, ub_ref, wq_any, wk_any, wv_any, wo_any, wu_any, wd_any,
                   q_ref, k_ref, v_ref, geo_ref, p_ref, ctx_any, wt_any, ua_any, no_any, nu_any, nd_any, fo_any, fu_any, fd_any, co_any, cu_any, cd_any,
                   wt, cat_q, cat_k, cpage, ubs, l_s, x_s, x_r, y_s, y_r, z_s, z_r, n_s, n_r, c_s, c_r, u_s, u_r, t_s, t_r, *, pages):
    i = pl.program_id(0)
    cols = q_ref.shape[1]
    heads = cols // HEAD
    box = heads * POS
    group, place, core, chip, near, far, cross = seats()
    y = lax.rem(group, 2)
    z = lax.rem(group // 2, 2)
    beside = group + 1 - 2 * y
    above = group + 2 - 4 * z
    q = y + 2 * z
    quarter = (q, q + 1 - 2 * y, q + 2 - 4 * z, q + 3 - 2 * y - 4 * z)
    own = (wo_any, wu_any, wd_any)
    nears = (no_any, nu_any, nd_any)
    fars = (fo_any, fu_any, fd_any)
    crosses = (co_any, cu_any, cd_any)
    chunks = weight_chunks(own)

    def rows(c, k, part=None):
        a, s, n = chunks[c]
        start = quarter[k] * (own[a].shape[0] // 4) + s
        if part is not None and splits(chunks[c]):
            n //= 2
            start += part * n
        return pl.ds(pl.multiple_of(start, 16), n)

    def hop(c, k, sems, to, part=None, source=fars):
        a = chunks[c][0]
        r = rows(c, k, part)
        return remote(source[a].at[r], fars[a].at[r], sems[0], sems[1], to)

    def x_copy(c):
        return hop(c, 0, (x_s.at[c], x_r.at[c]), (group, far), source=own)

    def y_copy(c, step, k):
        return hop(c, k, (y_s.at[step, c], y_r.at[step, c]), (beside, place), None if step == 0 else 0)

    def z_copy(c, step, k):
        return hop(c, k, (z_s.at[step, c], z_r.at[step, c]), (above, place), None if step == 0 else 1)

    def c_copy(c, k):
        a = chunks[c][0]
        r = rows(c, k)
        return remote(fars[a].at[r], crosses[a].at[r], c_s.at[k, c], c_r.at[k, c], (group, near))

    def stage(n, c):
        if n == 0:
            x_copy(c).wait_recv()
            y_copy(c, 0, 0).start()
            z_copy(c, 0, 0).start()
            c_copy(c, 0).start()
        elif n == 1:
            y_copy(c, 0, 1).wait_recv()
            if splits(chunks[c]):
                z_copy(c, 1, 1).start()
            z_copy(c, 0, 2).wait_recv()
            y_copy(c, 1, 2).start()
            c_copy(c, 1).start()
            c_copy(c, 2).start()
        else:
            y_copy(c, 1, 3).wait_recv()
            if splits(chunks[c]):
                z_copy(c, 1, 3).wait_recv()
            c_copy(c, 3).start()

    n_copies = [remote(own[a], nears[a], n_s.at[a], n_r.at[a], (group, near)) for a in range(3)]
    u_copies = [remote(ubs.at[0], ubs.at[g], u_s.at[g - 1], u_r.at[g - 1], (group, d)) for g, d in ((1, near), (2, far), (3, cross))]
    loads = [pltpu.make_async_copy(w, wt.at[pl.ds(box + n * cols, cols)], l_s.at[n]) for n, w in enumerate((wq_any, wk_any, wv_any))]
    keep_wt = pltpu.make_async_copy(wt, wt_any, l_s.at[3])

    @pl.when(i == 0)
    def _():
        for c in loads:
            c.start()
        ubs[0] = row(ub_ref)
        barrier = pltpu.get_barrier_semaphore()
        peers = [(group, near), (group, far), (group, cross), (beside, place), (above, place)]
        for device in peers:
            pl.semaphore_signal(barrier, inc=1, device_id=device, device_id_type=MESH)
        pl.semaphore_wait(barrier, len(peers))
        for c in range(len(chunks)):
            x_copy(c).start()
        for n in n_copies:
            n.start()
        for u in u_copies:
            u.start()
        wt[:box, :] = wb_ref[...].T
        for c in loads:
            c.wait()
        keep_wt.start()

    length = len_ref[page_of(i, pages)]
    geo = geometry_of(coords_ref[...], rates_ref[...])
    geo_ref[...] = geo
    proj = mm_nt(h_ref[...], wt[...])
    q_ref[...] = (proj[:, box : box + cols] + row(qb_ref)).astype(BF)
    k_ref[...] = proj[:, box + cols : box + 2 * cols].astype(BF)
    v_ref[...] = (proj[:, box + 2 * cols :] + row(vb_ref)).astype(BF)
    co, si = mixing(geo.astype(F32))
    bias = row(bb_ref)
    for head in range(heads):
        wide = slice(head * POS, (head + 1) * POS)
        lanes = slice(head * HEAD, (head + 1) * HEAD)
        cat_q[head, :, :POS] = mix(proj[:, wide] + bias[:, wide], co, si).astype(BF)
        cat_q[head, :, POS:] = q_ref[:, lanes]
        cat_k[head, :, :POS] = geo
        cat_k[head, :, POS:] = k_ref[:, lanes]
    count = 2 * pages
    plan = {1: [(0, 0)], 3: [(0, 1), (0, 2), (1, 0)], 5: [(0, 3), (0, 4), (1, 1)], 7: [(1, 2)], 9: [(1, 3), (1, 4), (2, 0), (2, 1)], 11: [(2, 2), (2, 3), (2, 4)]}

    def tick(odd):
        for at, todo in plan.items():
            if at % 2 == odd:

                @pl.when(i == at // 2)
                def _():
                    for n, c in todo:
                        stage(n, c)

    valid = lax.broadcasted_iota(jnp.int32, (PAGE, 1), 0) < length
    scale = LOG2E / math.sqrt(HEAD)
    s = mm_nt(cat_k[0], cat_q[0])
    for head in range(heads):
        lanes = slice(head * HEAD, (head + 1) * HEAD)
        now = s
        if head + 1 < heads:
            s = mm_nt(cat_k[head + 1], cat_q[head + 1])
        now = jnp.where(valid, now, -1e30)
        top = jnp.max(now, axis=0, keepdims=True)
        e = jnp.exp2((now - top) * scale)
        total = jnp.sum(e, axis=0, keepdims=True)
        p = (e * (1.0 / total)).astype(BF)
        p_ref[head] = p
        c = mm_tn(p, v_ref[:, lanes]).astype(BF)
        for k in range(2):
            cpage[2 * i + k, :, lanes] = c[k * HALF : (k + 1) * HALF]
        if head == heads // 2:
            tick(0)
    for k in range(2):
        piece = 2 * lax.rem(i, pages) + k
        oc = piece // pages
        slot = lax.rem(piece, pages)
        mine = oc == core

        @pl.when(i < pages)
        def _():
            g = jnp.where(mine, 2, 3)
            remote(cpage.at[2 * i + k], ctx_any.at[g, slot], t_s.at[2 * i + k], t_r.at[g, slot], (group, 2 * (1 - chip) + oc)).start()

        @pl.when((i >= pages) & jnp.logical_not(mine))
        def _():
            remote(cpage.at[2 * i + k], ctx_any.at[1, slot], t_s.at[2 * i + k], t_r.at[1, slot], (group, near)).start()

        @pl.when((i >= pages) & mine)
        def _():
            pltpu.make_async_copy(cpage.at[2 * i + k], ctx_any.at[0, slot], t_r.at[0, slot]).start()

    tick(1)

    @pl.when(i == count - 1)
    def _():
        keep_wt.wait()
        for u in u_copies:
            u.wait()
        keep_ub = pltpu.make_async_copy(ubs, ua_any, u_s.at[3])
        keep_ub.start()
        for n in n_copies:
            n.wait()
        keep_ub.wait()
        for slot in range(pages):
            for g in range(4):
                arrived(ctx_any.at[g, slot], t_r.at[g, slot])
        for j in range(2 * count):
            if j < count:
                arrived(cpage.at[j], t_s.at[j])
            else:

                @pl.when((j - count) // pages != core)
                def _():
                    arrived(cpage.at[j], t_s.at[j])

        for c in range(len(chunks)):
            x_copy(c).wait_send()
            for step in range(2):
                y_copy(c, step, 2 * step).wait_send()
                if step == 0 or splits(chunks[c]):
                    z_copy(c, step, step).wait_send()
            for k in range(4):
                c_copy(c, k).wait()


def run_forward(lengths, rates, hidden, coords, wb, qb, vb, bb, ub, wq, wk, wv, wo, wu, wd):
    cols, d = wq.shape
    heads = cols // HEAD
    pages = lengths.shape[0] // 2
    wide = wb.shape[1] + 3 * cols
    own = (wo, wu, wd)
    n = len(weight_chunks(own))
    page_out = lambda w: pl.BlockSpec((PAGE, w), lambda i: (i, 0))
    rows = 2 * pages * PAGE
    return pl.pallas_call(
        partial(forward_kernel, pages=pages),
        out_shape=[S((rows, cols), BF)] * 3
        + [S((rows, POS), BF), S((2 * pages, heads, PAGE, PAGE), BF), S((4, pages, HALF, cols), BF), S((wide, d), BF), S((4, 1, ub.shape[0]), F32)]
        + [S(x.shape, BF) for x in own] * 3,
        grid=(2 * pages,),
        in_specs=[
            pl.BlockSpec(memory_space=pltpu.SMEM),
            WHOLE,
            pl.BlockSpec((PAGE, d), lambda i: (page_of(i, pages), 0)),
            pl.BlockSpec((4, PAGE), lambda i: (0, page_of(i, pages))),
        ]
        + [WHOLE] * 5
        + [ANY] * 6,
        out_specs=[page_out(cols)] * 3
        + [page_out(POS), pl.BlockSpec((pl.Squeezed(), heads, PAGE, PAGE), lambda i: (i, 0, 0, 0))]
        + [ANY] * 12,
        scratch_shapes=[V((wide, d), BF), V((heads, PAGE, POS + HEAD), BF), V((heads, PAGE, POS + HEAD), BF), V((4 * pages, HALF, cols), BF), V((4, 1, ub.shape[0]), F32)]
        + [D((4,)), D((n,)), D((n,)), D((2, n)), D((2, n)), D((2, n)), D((2, n)), D((3,)), D((3,)), D((4, n)), D((4, n)), D((4,)), D((3,)), D((4 * pages,)), D((4, pages))],
        compiler_params=pltpu.CompilerParams(vmem_limit_bytes=56 << 20, collective_id=0, has_side_effects=True),
        name="forward",
    )(lengths, rates, hidden, coords, wb, qb, vb, bb, ub, wq, wk, wv, wo, wu, wd)


def middle_kernel(hid_any, og_any, ctx_any, w0, w1, w2, w3, w4, w5, w6, w7, w8, w9, w10, w11, ub_ref, ob_ref, g1_ref, s1_ref, db_ref, g2_ref, s2_ref,
                  out_any, act_any, ug_any, fl_any, sl_any, scaled_any, second_any, inv_ref, vg_ref,
                  hid, og, ctx, wo, wu, wd, act, ug, fl, sl, lo, first, scaled1, second2, ffn, sem_in, sem_w, sem_out, *, tile):
    rows, d = og.shape
    groups = wu.shape[0]
    weights = (w0, w1, w2, w3, w4, w5, w6, w7, w8, w9, w10, w11)
    place = lax.axis_index("tensor")
    head_loads = [
        pltpu.make_async_copy(ctx_any, ctx, sem_in.at[0]),
        pltpu.make_async_copy(hid_any.at[pl.ds(place * rows, rows)], hid, sem_in.at[1]),
        pltpu.make_async_copy(og_any, og, sem_in.at[2]),
    ]
    loads = [[pltpu.make_async_copy(weights[3 * g + k], (wo, wu, wd)[k].at[g], sem_w.at[k, g]) for g in range(groups)] for k in range(3)]
    head_loads[0].start()
    for c in loads[0]:
        c.start()
    head_loads[1].start()
    for g in range(groups):
        loads[1][g].start()
        loads[2][g].start()
    head_loads[2].start()
    head_loads[0].wait()
    for c in loads[0]:
        c.wait()
    head_loads[1].wait()
    vg_ref[...] = jnp.zeros_like(vg_ref)
    for g in range(groups):
        loads[1][g].wait()
        loads[2][g].wait()
    head_loads[2].wait()
    steps = rows // tile

    def stores(i):
        r = pl.ds(pl.multiple_of(i * tile, tile), tile)
        pairs = ((act.at[:, r], act_any.at[:, r]), (ug.at[:, r], ug_any.at[:, r]), (fl.at[r], fl_any.at[r]), (sl.at[r], sl_any.at[r]),
                 (lo.at[r], out_any.at[r]), (scaled1.at[r], scaled_any.at[r]), (second2.at[r], second_any.at[r]))
        return [pltpu.make_async_copy(a, b, sem_out.at[n, i]) for n, (a, b) in enumerate(pairs)]

    def step(i, _):
        r = pl.ds(pl.multiple_of(i * tile, tile), tile)
        attn = mm(ctx[0, r], wo[0])
        for g in range(1, groups):
            attn = attn + mm(ctx[g, r], wo[g])
        scaled, inverse = normal(attn + row(ob_ref) + hid[r].astype(F32))
        f = scaled * row(g1_ref) + row(s1_ref)
        first[...] = f
        scaled1[r] = scaled
        inv_ref[r] = inverse
        fl[r] = f.astype(BF)
        x = mm(fl[r], wu[0])
        for g in range(groups):
            now = x + ub_ref[g]
            if g + 1 < groups:
                x = mm(fl[r], wu[g + 1])
            half = 0.5 + 0.5 * lax.erf(now * 0.7071067811865476)
            a = (now * half).astype(BF)
            act[g, r] = a
            ug[g, r] = (half + now * jnp.exp(-0.5 * now * now) * 0.3989422804014327).astype(BF)
            part = mm(a, wd[g])
            if g == 0:
                ffn[...] = part
            else:
                ffn[...] += part

        scaled, inverse = normal(ffn[...] + row(db_ref) + first[...])
        lo[r] = (scaled * row(g2_ref) + row(s2_ref)).astype(BF)

        o = og[r].astype(F32)
        second = normal_back(o * row(g2_ref), scaled, inverse)
        vg_ref[3:4, :] += columns(second)
        vg_ref[4:5, :] += columns(o * scaled)
        vg_ref[5:6, :] += columns(o)
        sl[r] = second.astype(BF)
        second2[r] = second
        for c in stores(i):
            c.start()
        return 0

    lax.fori_loop(0, steps, step, 0)
    for i in range(steps):
        for c in stores(i):
            c.wait()


def run_middle(hidden, og, ctx, weights, ub, vectors, tile):
    rows, d = og.shape
    groups = 4
    q = weights[0].shape[0]
    f = weights[1].shape[1]
    return pl.pallas_call(
        partial(middle_kernel, tile=tile),
        out_shape=[S((rows, d), BF), S((groups, rows, f), BF), S((groups, rows, f), BF), S((rows, d), BF), S((rows, d), BF), S((rows, d), F32), S((rows, d), F32), S((rows, 1), F32), S((8, d), F32)],
        in_specs=[ANY] * 15 + [WHOLE] * 7,
        out_specs=[ANY] * 7 + [WHOLE] * 2,
        scratch_shapes=[
            V((rows, d), BF), V((rows, d), BF), V((groups, rows, q), BF), V((groups, q, d), BF), V((groups, d, f), BF), V((groups, f, d), BF),
            V((groups, rows, f), BF), V((groups, rows, f), BF), V((rows, d), BF), V((rows, d), BF), V((rows, d), BF),
            V((tile, d), F32), V((rows, d), F32), V((rows, d), F32), V((tile, d), F32),
            D((3,)), D((3, groups)), D((7, rows // tile)),
        ],
        compiler_params=pltpu.CompilerParams(vmem_limit_bytes=62 << 20),
        name="middle",
    )(hidden, og, ctx, *weights, ub, *vectors)


class Cube:
    def __init__(self, main, recv, out, sems, group, place, rows, levels):
        self.main, self.recv, self.out, self.sems = main, recv, out, sems
        self.group, self.place, self.rows, self.levels = group, place, rows, levels
        self.steps = 2 * levels - 1
        self.sides = [lax.rem(group // 2**n, 2) for n in range(levels)]
        self.mates = [group + 2**n * (1 - 2 * side) for n, side in enumerate(self.sides)]

    def pick(self, j, s, values):
        if s > 1:
            return values[s]
        return jnp.where((j & 3) == 3, values[1 - s], values[s])

    def side(self, j, s):
        return self.pick(j, s, self.sides)

    def partner(self, j, s):
        return (self.pick(j, s, self.mates), self.place)

    def got(self, n, sem, j, s):
        arrived(self.recv.at[pl.ds(0, n)], self.sems.at[sem, j, s])

    def low(self, j, s):
        at = j * self.rows
        for t in range(s):
            at = at + self.side(j, t) * (self.rows >> (t + 1))
        return at

    def span(self, start, n):
        return pl.ds(pl.multiple_of(start, 16), n)

    def r_copy(self, j, s):
        n = self.rows >> (s + 1)
        src = self.main.at[self.span(self.low(j, s) + (1 - self.side(j, s)) * n, n)]
        dst = self.recv.at[self.span(j * self.rows + self.rows - (self.rows >> s), n)]
        return remote(src, dst, self.sems.at[0, j, s], self.sems.at[1, j, s], self.partner(j, s))

    def g_copy(self, j, s):
        here = self.span(self.low(j, s + 1), self.rows >> (s + 1))
        src = self.main if s == self.levels - 1 else self.out
        return remote(src.at[here], self.out.at[here], self.sems.at[2, j, s], self.sems.at[3, j, s], self.partner(j, s))

    def keep(self, j):
        here = self.span(self.low(j, self.levels), self.rows >> self.levels)
        return pltpu.make_async_copy(self.main.at[here], self.out.at[here], self.sems.at[0, j, self.levels])

    def start(self, j):
        self.r_copy(j, 0).start()

    def step(self, k, j):
        last = self.levels - 1
        if k <= last:
            n = self.rows >> (k + 1)
            self.got(n, 1, j, k)
            mine = self.span(self.low(j, k + 1), n)
            got = self.span(j * self.rows + self.rows - (self.rows >> k), n)
            self.main[mine] = self.main[mine] + self.recv[got]
            if k < last:
                self.r_copy(j, k + 1).start()
            else:
                self.keep(j).start()
                self.g_copy(j, last).start()
        else:
            s = 2 * self.levels - 2 - k
            self.got(self.rows >> (s + 2), 3, j, s + 1)
            if s + 1 == last:
                self.got(self.rows >> self.levels, 0, j, self.levels)
            self.g_copy(j, s).start()

    def finish(self, j):
        self.got(self.rows >> 1, 3, j, 0)
        for s in range(self.levels):
            self.got(self.rows >> (s + 1), 0, j, s)
            self.got(self.rows >> (s + 1), 2, j, s)


SLOTS = 3


def backward_kernel(h_ref, wt_ref, q_ref, k_ref, v_ref, geo_ref, p_ref, inv_ref, vgin_ref, g1_ref,
                    act_any, ug_any, fl_any, sl_any, scaled_any, second_any, ctx_any,
                    o0, u0, n0, o1, u1, n1, o2, u2, n2, o3, u3, n3,
                    fin_any, afin_any, ig_any,
                    act, ug, wd, wo, fl, sl, al, ctx, cs, crecv, gx, xrecv, main, mrecv, amain, arecv, dsrc, dc, dcp, total, btotal, mixed, drecv, dxrecv, ag, acc, vg, ubg,
                    l_sem, w_sem, c_s, c_r, free, x_s, x_r, r_sem, a_sem, e_s, e_r, d_s, d_r, f_s, f_r, o_sem, *, pages, ways, blocks, per, arows):
    i = pl.program_id(0)
    count = 2 * pages
    group, place, core, chip, near, far, cross = seats()
    cols = q_ref.shape[1]
    heads = cols // HEAD
    box = heads * POS
    d = h_ref.shape[1]
    levels = ways.bit_length() - 1
    f = act.shape[2]
    qc = ctx.shape[2]
    downs = f // BLOCK
    ups = downs + d // BLOCK
    chunks = blocks // per
    achunks = amain.shape[0] // arows
    ffn = Cube(main, mrecv, fin_any, r_sem, group, place, per * BLOCK, levels)
    att = Cube(amain, arecv, afin_any, a_sem, group, place, arows, levels)
    second = total.at[pl.ds(0, pages * BLOCK), :]
    loads = [pltpu.make_async_copy(a, b, l_sem.at[n]) for n, (a, b) in enumerate(((sl_any, sl), (fl_any, fl), (ug_any, ug), (scaled_any, ag), (second_any, second), (ctx_any, ctx)))]
    act_loads = [pltpu.make_async_copy(act_any.at[g], act.at[g], w_sem.at[3, g]) for g in range(4)]
    wo_loads = [pltpu.make_async_copy(a, wo.at[g], w_sem.at[0, g]) for g, a in enumerate((o0, o1, o2, o3))]
    wu_loads = [pltpu.make_async_copy(a, act.at[g], w_sem.at[1, g]) for g, a in enumerate((u0, u1, u2, u3))]
    wd_loads = [pltpu.make_async_copy(a, wd.at[g], w_sem.at[2, g]) for g, a in enumerate((n0, n1, n2, n3))]
    spare = lambda which, slot: wd.at[which, pl.ds(slot * HALF, HALF)]

    def e_copy(g, slot):
        return remote(dsrc.at[g - 1, slot], dc.at[g, slot], e_s.at[g - 1, slot], e_r.at[g - 1, slot], (group, (near, far, cross)[g - 1]))

    def c_copy(b):
        return remote(cs.at[lax.rem(b, 2)], crecv.at[lax.rem(b, SLOTS)], c_s.at[b], c_r.at[b], (group, near))

    def x_copy(b):
        return remote(gx.at[b], xrecv.at[b], x_s.at[b], x_r.at[b], (group, far))

    def span(b):
        return pl.ds(pl.multiple_of(b * BLOCK, BLOCK), BLOCK)

    def plus(a, b):
        return a + b

    def put(b, g, value):
        value = value.astype(BF)
        if g == 0:
            main[span(b)] = value
        elif g == 2:
            gx[b] = value
        else:
            cs[lax.rem(b, 2), g // 2] = value

    def c_add(b):
        c_copy(b).wait_recv()
        slot = lax.rem(b, SLOTS)

        main[span(b)] = plus(main[span(b)], crecv[slot, 0])
        gx[b] = plus(gx[b], crecv[slot, 1])
        x_copy(b).start()

        @pl.when(b + SLOTS < blocks)
        def _():
            pl.semaphore_signal(free, inc=1, device_id=(group, near), device_id_type=MESH)

    def block(b, kind):
        @pl.when(b >= 2)
        def _():
            c_copy(b - 2).wait_send()

        if kind == "down":
            r = pl.ds(pl.multiple_of(b * BLOCK, BLOCK), BLOCK)
            for g in range(4):

                @pl.when(b == 0)
                def _():
                    act_loads[g].wait()

                put(b, g, mm_tn(act[g, :, r], sl[...]))
        elif kind == "up":
            r = pl.ds(pl.multiple_of((b - downs) * BLOCK, BLOCK), BLOCK)
            for g in range(4):
                put(b, g, mm_tn(fl[:, r], ug[g]))
        elif kind == "out":
            width = d // 4
            for g, place_g in enumerate((place, near, far, cross)):
                norms = vg[0:6, :width]
                for a in range(1, 4):
                    norms = jnp.where(place_g == a, vg[0:6, a * width : (a + 1) * width], norms)
                norms = jnp.concatenate([norms, jnp.zeros((6, d - width), F32)], axis=1)
                extra = jnp.concatenate([ubg[g, 0:1, :], norms, jnp.zeros((BLOCK - qc - 7, d), F32)], axis=0)
                put(b, g, jnp.concatenate([mm_tn(ctx[g], al[...]), extra], axis=0))
        else:
            for g in range(4):
                put(b, g, jnp.zeros((BLOCK, d), F32))

        @pl.when(b >= SLOTS)
        def _():
            pl.semaphore_wait(free, 1)

        c_copy(b).start()

    def x_add(b):
        x_copy(b).wait_recv()

        main[span(b)] = plus(main[span(b)], xrecv[b])

        @pl.when(lax.rem(b + 1, per) == 0)
        def _():
            ffn.start(b // per)

    def tick(u, low, high=blocks):
        half = u // 2
        odd = lax.rem(u, 2)
        if high == blocks:

            @pl.when((odd == 0) & (half >= low) & (half < high))
            def _():
                x_add(half)

        for k in range(ffn.steps):
            b = (u - k - 1) // 2

            @pl.when((lax.rem(u + k, 2) == 1) & (u > k) & (b >= low) & (b < high) & (lax.rem(b + 1, per) == 0))
            def _():
                ffn.step(k, b // per)

    @pl.when(i == 0)
    def _():
        loads[0].start()
        for c in act_loads:
            c.start()
        peers = [(group, near), (group, far), (group, cross)]
        peers += [(group + 2**n * (1 - 2 * lax.rem(group // 2**n, 2)), place) for n in range(levels)]
        barrier = pltpu.get_barrier_semaphore()
        for device in peers:
            pl.semaphore_signal(barrier, inc=1, device_id=device, device_id_type=MESH)

        for c in wd_loads:
            c.start()
        loads[2].start()
        loads[4].start()
        loads[3].start()
        for c in wo_loads:
            c.start()
        loads[1].start()
        loads[5].start()
        pl.semaphore_wait(barrier, len(peers))
        loads[0].wait()

        def down_block(b, _):
            block(b, "down")

            @pl.when(b >= 1)
            def _():
                c_add(b - 1)

            return 0

        lax.fori_loop(0, downs, down_block, 0)
        for c in wu_loads:
            c.start()
        for c in wd_loads:
            c.wait()
        for n in (2, 3, 4):
            loads[n].wait()
        c_add(downs - 1)
        for c in wo_loads:
            c.wait()
        vg[...] = vgin_ref[...]
        ubg[...] = jnp.zeros_like(ubg)

        def tile(t, _):
            r = pl.ds(pl.multiple_of(t * BLOCK, BLOCK), BLOCK)
            acc[...] = total[r, :]
            for g in range(4):
                u = (mm_nt(sl[r], wd[g]) * ug[g, r].astype(F32)).astype(BF)
                ug[g, r] = u
                ubg[g, 0:1, :] += columns(u.astype(F32))

                @pl.when(t == 0)
                def _():
                    wu_loads[g].wait()

                acc[...] += mm_nt(u, act[g])

            @pl.when(t == 1)
            def _():
                tick(0, 0)

            fg = acc[...]
            scaled = ag[r]
            a = normal_back(fg * row(g1_ref), scaled, inv_ref[r])
            vg[0:1, :] += columns(a)
            vg[1:2, :] += columns(fg * scaled)
            vg[2:3, :] += columns(fg)
            ag[r] = a
            low = a.astype(BF)
            al[r] = low
            for g in (2, 3, 1, 0):
                value = mm_nt(low, wo[g]).astype(BF)
                if g == 0:
                    dc[0, t] = value
                else:
                    dsrc[g - 1, t] = value
                    e_copy(g, t).start()

            @pl.when(t == 2)
            def _():
                tick(1, 0)

            return 0

        lax.fori_loop(0, pages, tile, 0)

        def up_block(b, _):
            block(b, "up")

            @pl.when(b > downs)
            def _():
                c_add(b - 1)

            @pl.when(b == downs + 1)
            def _():
                tick(2, 0)

            return 0

        for n in (1, 5):
            loads[n].wait()
        lax.fori_loop(downs, ups, up_block, 0)
        block(ups, "out")
        c_add(ups - 1)
        for b in range(ups + 1, blocks):
            block(b, "zero")
            c_add(b - 1)
        c_add(blocks - 1)
        for b in (blocks - 2, blocks - 1):
            c_copy(b).wait_send()
        total[...] = jnp.zeros_like(total)
        btotal[...] = jnp.zeros_like(btotal)
        tick(3, 0)
        for slot in range(pages):
            e_copy(1, slot).wait_recv()

    @pl.when(i == pages)
    def _():
        for g in (2, 3):
            for slot in range(pages):
                e_copy(g, slot).wait_recv()

    for k in range(2):
        piece = 2 * lax.rem(i, pages) + k
        g = jnp.where(piece // pages == core, 0, 1) + jnp.where(i < pages, 0, 2)
        dcp[k * HALF : (k + 1) * HALF, :] = dc[g, lax.rem(piece, pages)]
    geo = geo_ref[...]
    co, si = mixing(geo.astype(F32))
    factor = 1.0 / math.sqrt(HEAD)
    lanes = [slice(head * HEAD, (head + 1) * HEAD) for head in range(heads)]
    dp = mm_nt(v_ref[:, lanes[0]], dcp[:, lanes[0]])
    for head in range(heads):
        now = dp
        if head + 1 < heads:
            dp = mm_nt(v_ref[:, lanes[head + 1]], dcp[:, lanes[head + 1]])
        p = p_ref[head]
        mixed[:, box + 2 * cols + head * HEAD : box + 2 * cols + (head + 1) * HEAD] = mm(p, dcp[:, lanes[head]]).astype(BF)
        pf = p.astype(F32)
        delta = jnp.sum(pf * now, axis=0, keepdims=True)
        ds = (pf * (now - delta)).astype(BF)
        both = mm_tn(ds, jnp.concatenate([geo, k_ref[:, lanes[head]]], axis=1)) * factor
        mixed[:, box + head * HEAD : box + (head + 1) * HEAD] = both[:, POS:].astype(BF)
        mixed[:, head * POS : (head + 1) * POS] = mix(both[:, :POS], co, si).astype(BF)
        mixed[:, box + cols + head * HEAD : box + cols + (head + 1) * HEAD] = (mm(ds, q_ref[:, lanes[head]]) * factor).astype(BF)

    total[...] += mm_tn(mixed[...], h_ref[...])
    btotal[0:1, :] += columns(mixed[...].astype(F32))

    def d_copy(kind, slot):
        return remote(spare(2 + kind, slot), drecv.at[kind, slot], d_s.at[kind, slot], d_r.at[kind, slot], (group, near))

    def f_copy(slot):
        return remote(spare(0, slot), dxrecv.at[slot], f_s.at[slot], f_r.at[slot], (group, far))

    kind = jnp.where(i < pages, 1, 0)
    dx = mm(mixed[...], wt_ref[...]).astype(BF)
    for k in range(2):
        piece = 2 * lax.rem(i, pages) + k
        slot = lax.rem(piece, pages)
        value = dx[k * HALF : (k + 1) * HALF]
        mine = piece // pages == core
        r = pl.ds(pl.multiple_of(slot * HALF, HALF), HALF)

        @pl.when(mine)
        def _():
            wd[kind, r] = value

        @pl.when(jnp.logical_not(mine))
        def _():
            wd[2 + kind, r] = value
            remote(wd.at[2 + kind, r], drecv.at[kind, slot], d_s.at[kind, slot], d_r.at[kind, slot], (group, near)).start()

    @pl.when(i < 2)
    def _():
        tick(4 + i, 0)

    @pl.when(i >= 1)
    def _():
        tick(5 + i, 0)

    @pl.when(i == count - 1)
    def _():
        bias = btotal[0:1, :]
        bias = jnp.concatenate([bias[:, : box + cols], bias[:, box + 2 * cols :]], axis=1)
        wide = total.shape[0]
        for b in range(0, wide, 64):
            amain[b : b + 64, :] = total[b : b + 64, :].astype(BF)
        ending = jnp.where(lax.broadcasted_iota(jnp.int32, (amain.shape[0] - wide, d), 0) == 0, bias, 0.0)
        amain[wide:, :] = ending.astype(BF)
        for j in range(achunks):
            att.start(j)
        for slot in range(pages):
            d_copy(0, slot).wait_recv()
            here = spare(0, slot)
            here[...] = plus(here[...], drecv[0, slot])
            f_copy(slot).start()
        first = 5 + count
        when = [0, 4, 7, 9, 11, 13]
        ticks = 2 * (blocks - 1) + ffn.steps - first + 1
        when += list(range(14, 14 + ticks - len(when)))
        waves = max(achunks + 2 * (att.steps - 1), when[-1] + 1)

        def wave(w, _):
            u = -100
            for n in range(ticks):
                u = jnp.where(w == when[n], first + n, u)
            tick(u, 0)
            for k in range(att.steps):

                @pl.when((w >= 2 * k) & (w - 2 * k < achunks))
                def _():
                    att.step(k, w - 2 * k)

            return 0

        lax.fori_loop(0, waves, wave, 0)
        outs = [pltpu.make_async_copy(ag.at[pl.ds(slot * HALF, HALF)], ig_any.at[pl.ds(slot * HALF, HALF)], o_sem.at[slot]) for slot in range(pages)]
        for slot in range(pages):
            r = pl.ds(slot * HALF, HALF)
            d_copy(1, slot).wait_recv()
            f_copy(slot).wait_recv()
            ag[r] = ag[r] + wd[1, r].astype(F32) + drecv[1, slot].astype(F32) + dxrecv[slot].astype(F32)
            outs[slot].start()
        for slot in range(pages):
            outs[slot].wait()
            f_copy(slot).wait_send()
            d_copy(0, slot).wait_send()
            d_copy(1, slot).wait_send()
            for g in (1, 2, 3):
                e_copy(g, slot).wait_send()
        lax.fori_loop(0, achunks, lambda j, _: (att.finish(j), 0)[1], 0)
        lax.fori_loop(0, chunks, lambda j, _: (ffn.finish(j), 0)[1], 0)
        lax.fori_loop(0, blocks, lambda b, _: (x_copy(b).wait_send(), 0)[1], 0)


def run_backward(hidden, wt, q, k, v, geo, p, inv, vg, g1, act, ug, fl, sl, scaled, second, ctx, weights):
    count, heads = p.shape[:2]
    pages = count // 2
    cols = q.shape[1]
    wide, d = wt.shape
    f = act.shape[2]
    rows = fl.shape[0]
    ways = lax.axis_size("dp")
    levels = ways.bit_length() - 1
    chunk = max(BLOCK, 16 * ways)
    per = chunk // BLOCK
    blocks = -(-((f + d) // BLOCK + 1) // per) * per
    chunks = blocks // per
    arows = 16 * ways
    achunks = -(-(wide + 1) // arows)
    turn = lambda i: lax.rem(i + pages, count)
    page = lambda n: pl.BlockSpec((PAGE, n), lambda i: (turn(i), 0))
    once = lambda a: pl.BlockSpec(a.shape, lambda i: (0,) * len(a.shape), pipeline_mode=pl.Buffered(1))
    return pl.pallas_call(
        partial(backward_kernel, pages=pages, ways=ways, blocks=blocks, per=per, arows=arows),
        out_shape=[S((blocks * BLOCK, d), BF), S((achunks * arows, d), BF), S((rows, d), F32)],
        grid=(count,),
        in_specs=[
            pl.BlockSpec((PAGE, d), lambda i: (page_of(turn(i), pages), 0)),
            once(wt), page(cols), page(cols), page(cols), page(POS),
            pl.BlockSpec((pl.Squeezed(), heads, PAGE, PAGE), lambda i: (turn(i), 0, 0, 0)),
            once(inv), once(vg), WHOLE,
        ]
        + [ANY] * 19,
        out_specs=[ANY] * 3,
        scratch_shapes=[
            V(act.shape, BF), V(ug.shape, BF), V((4, f, d), BF), V((4, cols, d), BF), V(fl.shape, BF), V(sl.shape, BF), V(fl.shape, BF), V(ctx.shape, BF),
            V((2, 2, BLOCK, d), BF), V((SLOTS, 2, BLOCK, d), BF), V((blocks, BLOCK, d), BF), V((blocks, BLOCK, d), BF),
            V((blocks * BLOCK, d), BF), V((blocks * BLOCK, d), BF), V((achunks * arows, d), BF), V((achunks * arows, d), BF),
            V((3, pages, HALF, cols), BF), V((4, pages, HALF, cols), BF), V((PAGE, cols), BF), V((wide, d), F32), V((8, wide), F32), V((PAGE, wide), BF),
            V((2, pages, HALF, d), BF), V((pages, HALF, d), BF), V((rows, d), F32), V((BLOCK, d), F32), V((8, d), F32), V((4, 8, f), F32),
            D((6,)), D((4, 4)), D((blocks,)), D((blocks,)), pltpu.SemaphoreType.REGULAR, D((blocks,)), D((blocks,)), D((4, chunks, levels + 1)), D((4, achunks, levels + 1)),
            D((3, pages)), D((3, pages)), D((2, pages)), D((2, pages)), D((pages,)), D((pages,)), D((pages,)),
        ],
        compiler_params=pltpu.CompilerParams(vmem_limit_bytes=67043328, collective_id=1, has_side_effects=True),
        name="backward",
    )(hidden, wt, q, k, v, geo, p, inv, vg, g1, act, ug, fl, sl, scaled, second, ctx, *weights)


def finish_kernel(fin_any, afin_any, grad_any, down_any, up_any, out_any, q_any, k_any, v_any, box_any, ig_any,
                  ub_ref, qb_ref, vb_ref, bb_ref, n0_ref, n1_ref, n2_ref, n3_ref, n4_ref, n5_ref,
                  low, alow, full, afull, boxt, grad, l_s, o_s):
    d = low.shape[1]
    cols = q_any.shape[0]
    box = box_any.shape[1]
    wide = box + 3 * cols
    f = down_any.shape[0]
    up = up_any.shape[0]
    rows = f + up + cols
    pieces = [(low, fin_any, full, a, BLOCK, (down_any if a < f else up_any), a % f) for a in range(0, f + up, BLOCK)]
    pieces += [(low, fin_any, full, f + up, cols + 16, out_any, 0)]
    pieces += [(alow, afin_any, afull, a, min(cols, wide + 16 - a), None, 0) for a in range(0, box, cols)]
    pieces += [(alow, afin_any, afull, box + n * cols, cols + (16 if n == 2 else 0), x, 0) for n, x in enumerate((q_any, k_any, v_any))]
    loads = [pltpu.make_async_copy(src.at[pl.ds(a, n)], buf.at[pl.ds(a, n)], l_s.at[j]) for j, (buf, src, _, a, n, _, _) in enumerate(pieces)]
    order = list(range(len(pieces) - 3 - box // cols, len(pieces))) + list(range(len(pieces) - 3 - box // cols))
    for j in order:
        loads[j].start()
    grad_in = pltpu.make_async_copy(grad_any, grad, l_s.at[len(pieces)])
    grad_out = pltpu.make_async_copy(grad, ig_any, o_s.at[len(pieces)])
    grad_in.start()
    stores = []
    for j in order:
        buf, _, wide_buf, a, n, dst, to = pieces[j]
        loads[j].wait()
        wide_buf[a : a + n, :] = buf[a : a + n, :].astype(F32)
        if dst is not None:
            n = min(n, dst.shape[0])
            c = pltpu.make_async_copy(wide_buf.at[pl.ds(a, n)], dst.at[pl.ds(to, n)], o_s.at[len(stores)])
            c.start()
            stores.append(c)
        elif a + n == box:
            boxt[...] = afull[:box, :].T
            c = pltpu.make_async_copy(boxt, box_any, o_s.at[len(stores)])
            c.start()
            stores.append(c)
    grad_in.wait()
    grad_out.start()
    stores.append(grad_out)
    tail = full[rows : rows + 8, :]
    ub_ref[...] = tail[0]
    width = d // 4
    for n, ref in enumerate((n0_ref, n1_ref, n2_ref, n3_ref, n4_ref, n5_ref)):
        ref[...] = tail[1 + n, :width]
    bias = afull[wide : wide + 8, :][0]
    bb_ref[...] = bias[:box]
    qb_ref[...] = bias[box : box + cols]
    vb_ref[...] = bias[box + cols : box + 2 * cols]
    for c in stores:
        c.wait()


def run_finish(fin, afin, grad, f, up, cols, box):
    d = fin.shape[1]
    rows = f + up + cols + 16
    wide = box + 3 * cols + 16
    width = d // 4
    vectors = [S((f,), F32), S((cols,), F32), S((cols,), F32), S((box,), F32)] + [S((width,), F32)] * 6
    n = (f + up) // BLOCK + 5 + box // cols
    return pl.pallas_call(
        finish_kernel,
        out_shape=[S((f, d), F32), S((up, d), F32), S((cols, d), F32)] + [S((cols, d), F32)] * 3 + [S((d, box), F32), S(grad.shape, F32)] + vectors,
        in_specs=[ANY] * 3,
        out_specs=[ANY] * 8 + [WHOLE] * 10,
        scratch_shapes=[V((rows, d), BF), V((wide, d), BF), V((rows, d), F32), V((wide, d), F32), V((d, box), F32), V(grad.shape, F32), D((n,)), D((n,))],
        compiler_params=pltpu.CompilerParams(vmem_limit_bytes=62 << 20),
        name="finish",
    )(fin, afin, grad)


def body(
    hidden_in, box_coords, page_lengths, query_weight, query_bias, key_weight, value_weight, value_bias, box_weight, box_bias, output_weight, output_bias,
    first_gain, first_shift, up_weight, up_bias, down_weight, down_bias, second_gain, second_shift, output_grad,
):
    rates = np.power(1000.0, -np.arange(FREQ) / FREQ).astype(np.float32)
    rates = jnp.asarray(np.tile(rates, POS // FREQ).reshape(1, POS))
    q, k, v, geo, p, ctx, wt, ups, *gathered = run_forward(
        page_lengths, rates, hidden_in, box_coords, box_weight, query_bias, value_bias, box_bias, up_bias,
        query_weight.T, key_weight.T, value_weight.T, output_weight, up_weight, down_weight,
    )
    rows, d = output_grad.shape
    ctx = ctx.reshape(ctx.shape[0], rows, ctx.shape[3])
    weights = (output_weight, up_weight, down_weight, *gathered)
    layer_out, act, ug, fl, sl, scaled, second, inv, vg = run_middle(
        hidden_in, output_grad, ctx, weights, ups, (output_bias, first_gain, first_shift, down_bias, second_gain, second_shift), tile=384 if rows % 384 == 0 else BLOCK
    )
    fin, afin, grad = run_backward(hidden_in, wt, q, k, v, geo, p, inv, vg, first_gain, act, ug, fl, sl, scaled, second, ctx, weights)
    cols = query_weight.shape[1]
    down, up, out, q, k, v, box, input_grad, ub, qb, vb, bb, *norms = run_finish(fin, afin, grad, up_weight.shape[1], d, cols, box_weight.shape[1])
    return (
        layer_out, input_grad, q.T, qb, k.T, v.T, vb, box, bb, out, norms[0], norms[1], norms[2], up, ub, down, norms[3], norms[4], norms[5],
    )


def solution(mesh):
    shared = P()
    by_column = P(None, "tensor")
    by_row = P("tensor", None)
    vector = P("tensor")
    tokens = P(("dp", "tensor"), None)
    in_specs = (
        P("dp", None), P(None, "dp"), P("dp"), by_column, vector, by_column, by_column, vector, by_column, vector, by_row, shared,
        shared, shared, by_column, vector, by_row, shared, shared, shared, tokens,
    )
    out_specs = (
        tokens, tokens, by_column, vector, by_column, by_column, vector, by_column, vector, by_row, vector, vector, vector,
        by_column, vector, by_row, vector, vector, vector,
    )
    return jax.shard_map(body, mesh=mesh, in_specs=in_specs, out_specs=out_specs, check_vma=False)
```
